32 devices in a mesh: dp: 8 (over y, x, core), tensor: 4 (over z).
Axes of the slice: x: 2, y: 2, z: 4, core: 2. Of those that a mesh axis runs over, the one named last changes fastest.
Arguments:
- x_in: float32 [1024, 1024], P(('dp', 'tensor')), may hold values from -6 to 6
- seq_lengths: int32 [8, 8], P('dp'), may hold values from 1 to 64, 128 in all within a row
- ln1_gain: float32 [2, 1024], P(None, ('dp', 'tensor')), may hold values from 0.5 to 1.5
- ln1_bias: float32 [2, 1024], P(None, ('dp', 'tensor')), may hold values from -3 to 3
- ln2_gain: float32 [2, 1024], P(None, ('dp', 'tensor')), may hold values from 0.5 to 1.5
- ln2_bias: float32 [2, 1024], P(None, ('dp', 'tensor')), may hold values from -3 to 3
- res_bias: float32 [2, 1024], P(None, ('dp', 'tensor')), may hold values from -3 to 3
- w_qkv: bfloat16 [2, 1024, 3, 1024], P(None, 'dp', None, 'tensor'), may hold values from -1 to 1
- b_qkv: float32 [2, 3, 1024], P(None, None, ('tensor', 'dp')), may hold values from -3 to 3
- w_out: bfloat16 [2, 1024, 1024], P(None, 'tensor', 'dp'), may hold values from -0.75 to 0.75
- w_fc: bfloat16 [2, 1024, 4096], P(None, 'dp', 'tensor'), may hold values from -0.1875 to 0.1875
- b_fc: float32 [2, 4096], P(None, ('tensor', 'dp')), may hold values from -3 to 3
- w_proj: bfloat16 [2, 4096, 1024], P(None, 'tensor', 'dp'), may hold values from -0.09375 to 0.09375
- grad_out: float32 [1024, 1024], P(('dp', 'tensor')), may hold values from -6 to 6
Outputs:
- y_out: float32 [1024, 1024], P(('dp', 'tensor'))
- grad_x: float32 [1024, 1024], P(('dp', 'tensor'))
- grad_ln1_gain: float32 [2, 1024], P(None, ('dp', 'tensor'))
- grad_ln1_bias: float32 [2, 1024], P(None, ('dp', 'tensor'))
- grad_ln2_gain: float32 [2, 1024], P(None, ('dp', 'tensor'))
- grad_ln2_bias: float32 [2, 1024], P(None, ('dp', 'tensor'))
- grad_res_bias: float32 [2, 1024], P(None, ('dp', 'tensor'))
- grad_w_qkv: float32 [2, 1024, 3, 1024], P(None, 'dp', None, 'tensor')
- grad_b_qkv: float32 [2, 3, 1024], P(None, None, ('tensor', 'dp'))
- grad_w_out: float32 [2, 1024, 1024], P(None, 'tensor', 'dp')
- grad_w_fc: float32 [2, 1024, 4096], P(None, 'dp', 'tensor')
- grad_b_fc: float32 [2, 4096], P(None, ('tensor', 'dp'))
- grad_w_proj: float32 [2, 4096, 1024], P(None, 'tensor', 'dp')
The draws below stay inside these ranges and needn't reach their ends.
Inputs may be any that keep to these rules, and one draw needn't show every extreme that they name: `seq_lengths`: in every row the lengths sum to 128 and the largest is exactly 64.
All inputs are finite; a program needn't handle non-finite values.
Results may differ from the reference program's by a relative error of at most 0.035.
Values may be sent and summed in bfloat16 or wider, within the bound.
A program may use at most 128 MiB of HBM per device.

```python
import math
import jax
import jax.numpy as jnp
import numpy as np
from jax import lax

D = 1024
HEADS = 16
HD = 64
ROT = 16
FF = 4096
LAYERS = 2
NSEQ = 8
TOK_DEV = 32
GROUP = 128
GROUPS = 8
TOKENS = 1024
MAXLEN = 64
N_DP = 8
N_TENSOR = 4


def draw_w_qkv(key, part):
    fan_scale = D ** (-0.5)
    base_draw = jax.random.truncated_normal(key, -5.0, 5.0, (LAYERS, D, 3, D), jnp.float32) * fan_scale
    return base_draw.astype(jnp.bfloat16)


def spiked(array, rng, source, target, shards_of, factor):
    owner, partner = [(jnp.arange(array.shape[position]) // (array.shape[position] // shards_of)).reshape([-1 if axis == position else 1 for axis in range(array.ndim)]) for position in (source, target)]
    chosen = jax.random.permutation(rng, shards_of)[partner]
    strong = (owner == chosen) | (owner == (partner + shards_of // 2) % shards_of)
    return jnp.where(strong, factor * array, array)


def shard_levels(rng, extent, cuts, least, top_value):
    loudness = 1.0
    for position, parts in cuts:
        heights = jax.random.uniform(jax.random.fold_in(jax.random.fold_in(rng, 6), position), (parts,), jnp.float32, least / len(cuts), top_value / len(cuts))
        loudness = loudness * jnp.repeat(jnp.exp(heights), extent[position] // parts).reshape((-1,) + (1,) * (len(extent) - 1 - position))
    return loudness


def profile(count, total, bound, lean):
    weights = [(1 << 20) // math.isqrt(grade ** lean) + 1 for grade in range(2, count + 1)]
    rest, holding = total - bound - (count - 1), [1] * (count - 1)
    while rest > 0:
        movable = [i for i in range(count - 1) if holding[i] < bound]
        mass, budget = sum([weights[i] for i in movable]), rest
        for i in movable:
            more = min(bound - holding[i], max(1, budget * weights[i] // mass), rest)
            holding[i] = holding[i] + more
            rest = rest - more
    return np.array([bound] + holding)


def ragged(own_key, count, total, limit, lean):
    if count == 2:
        one = jax.random.randint(own_key, (), max(1, total - limit), min(limit, total - 1) + 1)
        return jnp.stack([one, total - one])
    lengths = jnp.asarray(profile(count, total, limit, lean), jnp.int32)
    couples = (count - 1) // 2
    source_of, sink = lengths[1:1 + 2 * couples:2], lengths[2:2 + 2 * couples:2]
    room = jnp.minimum(source_of - 1, limit - sink)
    passed = jax.random.randint(jax.random.fold_in(own_key, 1), (couples,), 0, 1 << 20) % (room + 1)
    lengths = lengths.at[1:1 + 2 * couples:2].set(source_of - passed).at[2:2 + 2 * couples:2].set(sink + passed)
    return lengths[jax.random.permutation(jax.random.fold_in(own_key, 2), count)]


def scatter_about(own_key, dims, scale, limit, pieces=(), kind=jnp.bfloat16):
    loudness = shard_levels(own_key, dims, pieces, -0.22, 0.18) if pieces else 1.0
    entries = jax.random.normal(own_key, dims, jnp.float32) * scale * loudness
    return jnp.minimum(jnp.maximum(entries, -limit), limit).astype(kind)


def bell_draw_with(stream_key, shape, spread, reach, cuts, heavy, kind=jnp.bfloat16):
    result = spread * jax.random.normal(stream_key, shape, jnp.float32)
    if cuts:
        result = result * shard_levels(stream_key, shape, cuts, -0.22, 0.18)
    return jnp.clip(spiked(result, jax.random.fold_in(stream_key, 3), *heavy), -reach, reach).astype(kind)


def setup_inputs(seed: int = 0) -> dict:
    key_of = jax.random.split(jax.random.key(seed), 15)
    return {
        "x_in": scatter_about(key_of[0], (TOKENS, D), 1.0, 6.0, ((0, 32),), jnp.float32),
        "seq_lengths": jax.vmap(lambda own: ragged(own, NSEQ, GROUP, MAXLEN, 2))(jax.random.split(key_of[1], GROUPS)).reshape((GROUPS, NSEQ)).astype(jnp.int32),
        "ln1_gain": jnp.clip(1.0 + 0.1 * jax.random.normal(key_of[2], (LAYERS, D), jnp.float32), 0.5, 1.5),
        "ln1_bias": scatter_about(key_of[3], (LAYERS, D), 0.5, 3.0, ((1, 32),), jnp.float32),
        "ln2_gain": jnp.clip(1.0 + 0.1 * jax.random.normal(key_of[4], (LAYERS, D), jnp.float32), 0.5, 1.5),
        "ln2_bias": scatter_about(key_of[5], (LAYERS, D), 0.5, 3.0, ((1, 32),), jnp.float32),
        "res_bias": scatter_about(key_of[6], (LAYERS, D), 0.5, 3.0, ((1, 32),), jnp.float32),
        "w_qkv": draw_w_qkv(jax.random.fold_in(key_of[14], 71), 0),
        "b_qkv": scatter_about(key_of[8], (LAYERS, 3, D), 0.5, 3.0, ((2, 32),), jnp.float32),
        "w_out": scatter_about(key_of[9], (LAYERS, D, D), (D // 16) ** -0.5, 0.75, ((1, 4), (2, 8))),
        "w_fc": scatter_about(key_of[10], (LAYERS, D, FF), D ** -0.5, 0.1875, ((1, 8), (2, 4))),
        "b_fc": scatter_about(key_of[11], (LAYERS, FF), 0.5, 3.0, ((1, 32),), jnp.float32),
        "w_proj": scatter_about(key_of[12], (LAYERS, FF, D), FF ** -0.5, 0.09375, ((1, 4), (2, 8))),
        "grad_out": bell_draw_with(key_of[13], (TOKENS, D), 1.0, 6.0, ((0, 32),), (0, 1, 32, 2.75), jnp.float32),
    }


EPS = 1e-05
HIGH = lax.Precision.HIGHEST
NEG_FILL = -1e+30

def layer_norm(values, gain_vec, bias_vec):
    average = lax.optimization_barrier(jnp.mean(values, axis=-1, keepdims=True))
    centred = values - average
    variance = lax.optimization_barrier(jnp.mean(centred * centred, axis=-1, keepdims=True))
    return centred * lax.rsqrt(variance + EPS) * gain_vec + bias_vec

def gelu_exact(values):
    return 0.5 * values * (1.0 + jax.scipy.special.erf(values * 0.7071067811865476))

def gelu_slope(values):
    normal_cdf = 0.5 * (1.0 + jax.scipy.special.erf(values * 0.7071067811865476))
    return normal_cdf + values * jnp.exp(-0.5 * values * values) * 0.3989422804014327

def group_layout(seq_len, total_rows):
    ends = jnp.cumsum(seq_len).astype(jnp.int32)
    starts = (ends - seq_len).astype(jnp.int32)
    row_ids = jnp.arange(total_rows, dtype=jnp.int32)
    member = (row_ids[:, None] >= starts[None, :]) & (row_ids[:, None] < ends[None, :])
    seq_index = jnp.arange(seq_len.shape[0], dtype=jnp.int32)
    seq_ids = lax.optimization_barrier(jnp.sum(jnp.where(member, seq_index[None, :], 0), axis=1)).astype(jnp.int32)
    row_start = lax.optimization_barrier(jnp.sum(jnp.where(member, starts[None, :], 0), axis=1)).astype(jnp.int32)
    return (seq_ids, (row_ids - row_start).astype(jnp.int32), row_ids)

def rotary_tables(positions):
    half_rot = ROT // 2
    freq_ids = jnp.arange(half_rot, dtype=jnp.float32)
    inverse = jnp.power(10000.0, -2.0 * freq_ids / ROT)
    angles = positions.astype(jnp.float32)[:, None] * inverse[None, :]
    return (jnp.cos(angles), jnp.sin(angles))

def rotate(vectors, cos_tab, sin_tab, direction_sign):
    half_rot = ROT // 2
    lower_half = vectors[..., :half_rot]
    upper_half = vectors[..., half_rot:ROT]
    cos_b = cos_tab[:, None, :]
    sin_b = sin_tab[:, None, :]
    new_lower = lower_half * cos_b - direction_sign * upper_half * sin_b
    new_upper = upper_half * cos_b + direction_sign * lower_half * sin_b
    return jnp.concatenate([new_lower, new_upper, vectors[..., ROT:]], axis=-1)

def masked_scores(queries, keys, seq_ids, row_ids):
    scores = jnp.einsum('qhd,khd->hqk', queries.astype(jnp.float32), keys.astype(jnp.float32), precision=HIGH) * HD ** (-0.5)
    allowed = (seq_ids[:, None] == seq_ids[None, :]) & (row_ids[None, :] <= row_ids[:, None])
    return jnp.where(allowed[None], scores, NEG_FILL)

def shard_sum(partials):
    rounded = lax.optimization_barrier(partials.astype(jnp.bfloat16))
    return lax.optimization_barrier(jnp.sum(rounded.astype(jnp.float32), axis=0))

def forward_layer(resid, weights, layout):
    gain_one, bias_one, gain_two, bias_two, out_bias, qkv_mat, qkv_vec, out_mat, fc_mat, fc_vec, proj_mat = weights
    seq_ids, row_ids, cos_tab, sin_tab = layout
    row_count = resid.shape[0]
    normed_a = layer_norm(resid, gain_one, bias_one).astype(jnp.bfloat16)
    normed_m = layer_norm(resid, gain_two, bias_two).astype(jnp.bfloat16)
    projected = jnp.dot(normed_a, qkv_mat.reshape(D, 3 * D), preferred_element_type=jnp.float32).reshape(row_count, 3, D) + qkv_vec[None]
    split_heads = projected.reshape(row_count, 3, HEADS, HD)
    queries = rotate(split_heads[:, 0], cos_tab, sin_tab, 1.0).astype(jnp.bfloat16)
    keys = rotate(split_heads[:, 1], cos_tab, sin_tab, 1.0).astype(jnp.bfloat16)
    values = split_heads[:, 2].astype(jnp.bfloat16)
    scores = masked_scores(queries, keys, seq_ids, row_ids)
    top_val = lax.optimization_barrier(jnp.max(scores, axis=-1, keepdims=True))
    exponent_terms = jnp.exp(scores - top_val)
    totals = lax.optimization_barrier(jnp.sum(exponent_terms, axis=-1, keepdims=True))
    attn_probs = (exponent_terms / totals).astype(jnp.bfloat16)
    contexts = jnp.einsum('hqk,khd->qhd', attn_probs.astype(jnp.float32), values.astype(jnp.float32), precision=HIGH).astype(jnp.bfloat16)
    log_totals = (top_val + jnp.log(totals))[..., 0]
    hidden_pre = jnp.dot(normed_m, fc_mat, preferred_element_type=jnp.float32) + fc_vec
    activated = gelu_exact(hidden_pre).astype(jnp.bfloat16)
    partials = jnp.einsum('gtk,tkn->tgn', contexts.reshape(row_count, N_TENSOR, -1).astype(jnp.float32), out_mat.reshape(N_TENSOR, -1, D).astype(jnp.float32), precision=HIGH)
    partials = partials + jnp.einsum('gtk,tkn->tgn', activated.reshape(row_count, N_TENSOR, -1).astype(jnp.float32), proj_mat.reshape(N_TENSOR, -1, D).astype(jnp.float32), precision=HIGH)
    branch = shard_sum(partials)
    new_resid = resid + branch + out_bias
    return (new_resid, (resid, normed_a, normed_m, queries, keys, values, contexts, log_totals, hidden_pre, activated))

def backward_layer(d_resid, saved, weights, layout):
    gain_one, bias_one, gain_two, bias_two, out_bias, qkv_mat, qkv_vec, out_mat, fc_mat, fc_vec, proj_mat = weights
    seq_ids, row_ids, cos_tab, sin_tab = layout
    resid, normed_a, normed_m, queries, keys, values, contexts, log_totals, hidden_pre, activated = saved
    row_count = d_resid.shape[0]
    out_bias_grad = lax.optimization_barrier(jnp.sum(d_resid, axis=0))
    d_rows = d_resid.astype(jnp.bfloat16)
    flat_context = contexts.reshape(row_count, D)
    d_context = jnp.dot(d_rows, out_mat.T, preferred_element_type=jnp.float32).astype(jnp.bfloat16).reshape(row_count, HEADS, HD)
    grad_out_mat = jnp.dot(flat_context.T, d_rows, preferred_element_type=jnp.float32)
    d_act = jnp.dot(d_rows, proj_mat.T, preferred_element_type=jnp.float32)
    grad_proj_mat = jnp.dot(activated.T, d_rows, preferred_element_type=jnp.float32)
    d_pre = d_act * gelu_slope(hidden_pre)
    grad_fc_vec = lax.optimization_barrier(jnp.sum(d_pre, axis=0))
    d_pre_b = d_pre.astype(jnp.bfloat16)
    grad_fc_mat = jnp.dot(normed_m.T, d_pre_b, preferred_element_type=jnp.float32)
    scores = masked_scores(queries, keys, seq_ids, row_ids)
    probs_full = jnp.exp(scores - log_totals[..., None])
    d_probs = jnp.einsum('qhd,khd->hqk', d_context.astype(jnp.float32), values.astype(jnp.float32), precision=HIGH)
    delta = lax.optimization_barrier(jnp.sum(d_context.astype(jnp.float32) * contexts.astype(jnp.float32), axis=-1))
    d_scores = probs_full * (d_probs - jnp.transpose(delta)[:, :, None])
    d_scaled = (d_scores * HD ** (-0.5)).astype(jnp.bfloat16)
    d_queries = jnp.einsum('hqk,khd->qhd', d_scaled.astype(jnp.float32), keys.astype(jnp.float32), precision=HIGH)
    d_keys = jnp.einsum('hqk,qhd->khd', d_scaled.astype(jnp.float32), queries.astype(jnp.float32), precision=HIGH)
    d_values = jnp.einsum('hqk,qhd->khd', probs_full.astype(jnp.bfloat16).astype(jnp.float32), d_context.astype(jnp.float32), precision=HIGH)
    d_queries = rotate(d_queries, cos_tab, sin_tab, -1.0)
    d_keys = rotate(d_keys, cos_tab, sin_tab, -1.0)
    d_projected = jnp.stack([d_queries, d_keys, d_values], axis=1).reshape(row_count, 3, D)
    grad_qkv_vec = lax.optimization_barrier(jnp.sum(d_projected, axis=0))
    d_projected_b = d_projected.astype(jnp.bfloat16)
    grad_qkv_mat = jnp.dot(normed_a.T, d_projected_b.reshape(row_count, 3 * D), preferred_element_type=jnp.float32).reshape(D, 3, D)
    d_norm_a = shard_sum(jnp.einsum('gctk,dctk->tgd', d_projected_b.reshape(row_count, 3, N_TENSOR, -1).astype(jnp.float32), qkv_mat.reshape(D, 3, N_TENSOR, -1).astype(jnp.float32), precision=HIGH))
    d_norm_m = shard_sum(jnp.einsum('gtk,dtk->tgd', d_pre_b.reshape(row_count, N_TENSOR, -1).astype(jnp.float32), fc_mat.reshape(D, N_TENSOR, -1).astype(jnp.float32), precision=HIGH))
    unused_one, back_one = jax.vjp(layer_norm, resid, gain_one, bias_one)
    d_res_one, grad_gain_one, grad_bias_one = back_one(d_norm_a)
    unused_two, back_two = jax.vjp(layer_norm, resid, gain_two, bias_two)
    d_res_two, grad_gain_two, grad_bias_two = back_two(d_norm_m)
    d_input = d_resid + d_res_one + d_res_two
    return (d_input, (grad_gain_one, grad_bias_one, grad_gain_two, grad_bias_two, out_bias_grad, grad_qkv_mat, grad_qkv_vec, grad_out_mat, grad_fc_mat, grad_fc_vec, grad_proj_mat))

def reference(x_in, seq_lengths, ln1_gain, ln1_bias, ln2_gain, ln2_bias, res_bias, w_qkv, b_qkv, w_out, w_fc, b_fc, w_proj, grad_out):
    group_rows = TOK_DEV * N_TENSOR
    params = (ln1_gain, ln1_bias, ln2_gain, ln2_bias, res_bias, w_qkv, b_qkv, w_out, w_fc, b_fc, w_proj)
    x_groups = x_in.reshape(N_DP, group_rows, D)
    d_groups = grad_out.reshape(N_DP, group_rows, D)

    def per_group(carry, inputs):
        x_grp, len_grp, d_grp = inputs
        seq_ids, positions, row_ids = group_layout(len_grp, group_rows)
        cos_tab, sin_tab = rotary_tables(positions)
        layout = (seq_ids, row_ids, cos_tab, sin_tab)
        resid = x_grp
        saved_all = []
        for layer_idx in range(LAYERS):
            weights = tuple((param_arr[layer_idx] for param_arr in params))
            resid, saved = forward_layer(resid, weights, layout)
            saved_all.append(saved)
        d_resid = d_grp
        layer_grads = [None] * LAYERS
        for layer_idx in reversed(range(LAYERS)):
            weights = tuple((param_arr[layer_idx] for param_arr in params))
            d_resid, layer_grads[layer_idx] = backward_layer(d_resid, saved_all[layer_idx], weights, layout)
        new_carry = tuple((carry[member_idx] + jnp.stack([layer_grads[layer_idx][member_idx] for layer_idx in range(LAYERS)]) for member_idx in range(len(params))))
        return (new_carry, (resid, d_resid))
    init = tuple((jnp.zeros(param_arr.shape, jnp.float32) for param_arr in params))
    totals, outputs = lax.scan(per_group, init, (x_groups, seq_lengths, d_groups))
    y_groups, dx_groups = outputs
    g_ln1_gain, g_ln1_bias, g_ln2_gain, g_ln2_bias, g_res_bias, g_w_qkv, g_b_qkv, g_w_out, g_w_fc, g_b_fc, g_w_proj = totals
    return (y_groups.reshape(-1, D), dx_groups.reshape(-1, D), g_ln1_gain, g_ln1_bias, g_ln2_gain, g_ln2_bias, g_res_bias, g_w_qkv, g_b_qkv, g_w_out, g_w_fc, g_b_fc, g_w_proj)
```

```python
import functools
import types

import jax
import jax.numpy as jnp
from jax import lax
from jax.experimental import pallas as pl
from jax.experimental.pallas import tpu as pltpu
from jax.sharding import PartitionSpec as P

HD = 64
ROT = 16


EPS = 1e-05
NEG_FILL = -1e30


def gelu_exact(values):
    return 0.5 * values * (1.0 + jax.scipy.special.erf(values * 0.7071067811865476))


def gelu_slope(values):
    normal_cdf = 0.5 * (1.0 + jax.scipy.special.erf(values * 0.7071067811865476))
    return normal_cdf + values * jnp.exp(-0.5 * values * values) * 0.3989422804014327


MESH = pl.DeviceIdType.MESH
ANY = pl.BlockSpec(memory_space=pl.ANY)
VMEM = pl.BlockSpec(memory_space=pltpu.VMEM)
N_SEMS = 448
N_LOCAL = 96


class Links:
    def __init__(self, n_dp, n_tensor, send_sems, recv_sems, local_sems):
        self.n_dp, self.n_tensor = n_dp, n_tensor
        self.dp, self.tensor = lax.axis_index("dp"), lax.axis_index("tensor")
        self.send_sems, self.recv_sems, self.local_sems = send_sems, recv_sems, local_sems
        self.used, self.used_local = 0, 0
        self.sent = []

    def send(self, src, dst, **where):
        copy = pltpu.make_async_remote_copy(
            src_ref=src,
            dst_ref=dst,
            send_sem=self.send_sems.at[self.used],
            recv_sem=self.recv_sems.at[self.used],
            device_id=where,
            device_id_type=MESH,
        )
        self.used += 1
        copy.start()
        self.sent.append(copy)
        return copy

    def local(self, src, dst):
        copy = pltpu.make_async_copy(src, dst, self.local_sems.at[self.used_local])
        self.used_local += 1
        copy.start()
        return copy

    def dp_peer(self, step):
        return lax.rem(self.dp + step, self.n_dp)

    def tensor_peer(self, step):
        return lax.rem(self.tensor + step, self.n_tensor)

    def barrier(self):
        sem = pltpu.get_barrier_semaphore()
        for step in range(1, self.n_tensor):
            pl.semaphore_signal(
                sem, inc=1, device_id={"tensor": self.tensor_peer(step)}, device_id_type=MESH
            )
        for step in range(1, self.n_dp):
            pl.semaphore_signal(
                sem, inc=1, device_id={"dp": self.dp_peer(step)}, device_id_type=MESH
            )
        pl.semaphore_wait(sem, self.n_tensor + self.n_dp - 2)

    def finish(self):
        for copy in self.sent:
            copy.wait_send()


class DpGather:
    def __init__(self, links, own, slot):
        self.links, self.own, self.slot = links, own, slot
        self.chips = links.n_dp // 2
        self.core, self.chip = lax.rem(links.dp, 2), links.dp // 2
        self.partner = links.dp + 1 - 2 * self.core
        self.relays = self.chips == 4
        rows = own.shape[0] // 2
        self.halves = [pl.ds(half * rows, rows) for half in range(2)]
        self.passed = []
        if self.relays:
            near = self.chip + 1 - 2 * lax.rem(self.chip, 2)
            far = lax.rem(self.chip + 2, 4)
            self.across = lax.rem(near + 2, 4)
            self.order = ((near, far), (far, near))

    def device(self, chip):
        return chip * 2 + self.core

    def out(self, rows, chip):
        return self.links.send(
            self.own.at[rows], self.slot(self.links.dp).at[rows], dp=self.device(chip)
        )

    def pass_on(self, rows, chip, target):
        block = self.slot(self.device(chip)).at[rows]
        return self.links.send(block, block, dp=target)

    def start(self):
        if self.relays:
            self.first = [self.out(rows, order[0]) for rows, order in zip(self.halves, self.order)]
            self.second = [self.out(rows, order[1]) for rows, order in zip(self.halves, self.order)]
        else:
            self.direct = [
                [self.out(rows, lax.rem(self.chip + step, self.chips)) for rows in self.halves]
                for step in range(1, self.chips)
            ]
        own_slot = self.slot(self.links.dp)
        self.passed.append(self.links.send(self.own, own_slot, dp=self.partner))
        self.kept = self.links.local(self.own, own_slot)

    def relay(self):
        if not self.relays:
            return
        self.relayed = []
        for copy, rows, order in zip(self.first, self.halves, self.order):
            copy.wait_recv()
            self.relayed.append(self.pass_on(rows, order[0], self.device(order[1])))
            self.passed.append(self.pass_on(rows, order[0], self.partner))

    def rest(self):
        if not self.relays:
            for step, copies in enumerate(self.direct):
                origin = lax.rem(self.chip + self.chips - step - 1, self.chips)
                for copy, rows in zip(copies, self.halves):
                    copy.wait_recv()
                    self.passed.append(self.pass_on(rows, origin, self.partner))
            return
        for copy, rows, order in zip(self.second, self.halves, self.order):
            copy.wait_recv()
            self.passed.append(self.pass_on(rows, order[1], self.partner))
        for copy, rows in zip(self.relayed, self.halves):
            copy.wait_recv()
            self.passed.append(self.pass_on(rows, self.across, self.partner))

    def finish(self):
        for copy in self.passed:
            copy.wait_recv()
        self.kept.wait()


class Group:
    def __init__(self, *gathers):
        self.gathers = gathers

    def start(self):
        for gather in self.gathers:
            gather.start()

    def relay(self):
        for gather in self.gathers:
            gather.relay()

    def rest(self):
        for gather in self.gathers:
            gather.rest()

    def finish(self):
        for gather in self.gathers:
            gather.finish()


class Pump:
    def __init__(self):
        self.todo, self.started, self.relayed, self.every = [], [], [], []

    def add(self, group):
        self.todo.append(group)
        self.every.append(group)
        if not self.started:
            self.start()

    def start(self):
        if self.todo:
            group = self.todo.pop(0)
            group.start()
            self.started.append(group)

    def relay(self):
        group = self.started.pop(0)
        group.relay()
        self.relayed.append(group)
        if not self.started:
            self.start()

    def rest(self):
        self.relayed.pop(0).rest()


def row_slot(ref, rows):
    return lambda d: ref.at[pl.ds(pl.multiple_of(d * rows, rows), rows)]


def column_slot(ref, size):
    return lambda d: ref.at[:, pl.ds(pl.multiple_of(d * size, size), size)]


def lead_slot(ref):
    return lambda d: ref.at[d]


class Scatter:
    def __init__(self, links, part, landing):
        self.links, self.part, self.landing = links, part, landing
        self.rows = landing.shape[1]
        slot = row_slot(part, self.rows)
        self.copies = [
            links.send(
                slot(links.tensor_peer(step)),
                landing.at[step - 1],
                tensor=links.tensor_peer(step),
            )
            for step in range(1, links.n_tensor)
        ]

    def total(self):
        own = pl.ds(pl.multiple_of(self.links.tensor * self.rows, self.rows), self.rows)
        total = self.part[own, :].astype(jnp.float32)
        for step, copy in enumerate(self.copies):
            copy.wait_recv()
            total = total + self.landing[step].astype(jnp.float32)
        return total


class Spread:
    def __init__(self, links, ref, value):
        rows = value.shape[0]
        slot = row_slot(ref, rows)
        ref[pl.ds(pl.multiple_of(links.tensor * rows, rows), rows), :] = value
        self.copies = [
            links.send(slot(links.tensor), slot(links.tensor), tensor=links.tensor_peer(step))
            for step in range(1, links.n_tensor)
        ]

    def finish(self):
        for copy in self.copies:
            copy.wait_recv()


class Cross:
    def __init__(self, links, stage, out, value):
        self.links, self.out = links, out
        n_dp, _, width = stage.shape
        for d in range(n_dp):
            stage[d] = value[:, d * width : (d + 1) * width]
        here = out.at[links.dp, links.tensor]
        self.copies = [
            links.send(stage.at[links.dp_peer(step)], here, dp=links.dp_peer(step))
            for step in range(1, n_dp)
        ]
        self.kept = links.local(stage.at[links.dp], here)

    def forward(self):
        links = self.links
        for copy in self.copies:
            copy.wait_recv()
        self.kept.wait()
        mine = self.out.at[:, links.tensor]
        self.wide = [
            links.send(mine, mine, tensor=links.tensor_peer(step))
            for step in range(1, links.n_tensor)
        ]

    def finish(self):
        for copy in self.wide:
            copy.wait_recv()


def unit_rows(values):
    average = jnp.mean(values, axis=-1, keepdims=True)
    centred = values - average
    variance = jnp.mean(centred * centred, axis=-1, keepdims=True)
    scale = lax.rsqrt(variance + EPS)
    return centred * scale, scale


def back_unit(values, grad):
    unit, scale = unit_rows(values)
    return scale * (
        grad
        - jnp.mean(grad, axis=-1, keepdims=True)
        - unit * jnp.mean(grad * unit, axis=-1, keepdims=True)
    )


def dot_nn(left, right):
    return jnp.dot(left, right, preferred_element_type=jnp.float32)


def dot_nt(left, right):
    return lax.dot_general(left, right, (((1,), (1,)), ((), ())), preferred_element_type=jnp.float32)


def dot_tn(left, right):
    return lax.dot_general(left, right, (((0,), (0,)), ((), ())), preferred_element_type=jnp.float32)


def turn(vectors, same, up, down, sign):
    width = vectors.shape[1]
    above = pltpu.roll(vectors, width - ROT // 2, 1)
    below = pltpu.roll(vectors, ROT // 2, 1)
    return vectors * same + sign * (above * up + below * down)


def head_scores(query, key, mask):
    scores = dot_nt(query, key) * HD ** (-0.5)
    scores = jnp.where(mask, scores, NEG_FILL)
    terms = jnp.exp(scores - jnp.max(scores, axis=-1, keepdims=True))
    return terms / jnp.sum(terms, axis=-1, keepdims=True)


def layout_tables(r):
    f32 = jnp.float32
    rows, width = r.same.shape
    lengths = r.lens_v[...]
    row_of = lax.broadcasted_iota(jnp.int32, (rows, rows), 0)
    col_of = lax.broadcasted_iota(jnp.int32, (rows, rows), 1)
    row_lane = lax.broadcasted_iota(jnp.int32, (rows, 128), 0)
    start = jnp.zeros((rows, rows), jnp.int32)
    start_lane = jnp.zeros((rows, 128), jnp.int32)
    end = jnp.zeros((1, 1), jnp.int32)
    for k in range(lengths.shape[1]):
        end = end + lengths[:, k : k + 1]
        start = jnp.where(row_of >= end, end, start)
        start_lane = jnp.where(row_lane >= end, end, start_lane)
    r.mask[...] = jnp.where((col_of >= start) & (col_of <= row_of), 1.0, 0.0)
    positions = (row_lane - start_lane).astype(f32)
    lane = lax.rem(lax.broadcasted_iota(jnp.int32, (1, 128), 1), HD)
    half = ROT // 2
    inverse = jnp.power(10000.0, -2.0 * lax.rem(lane, half).astype(f32) / ROT)
    angles = positions * inverse
    cos_tab, sin_tab = jnp.cos(angles), jnp.sin(angles)
    same = jnp.where(lane < ROT, cos_tab, 1.0)
    up = jnp.where(lane < half, -sin_tab, 0.0)
    down = jnp.where((lane >= half) & (lane < ROT), sin_tab, 0.0)
    for ref, table in ((r.same, same), (r.up, up), (r.down, down)):
        for place in range(width // 128):
            ref[:, place * 128 : (place + 1) * 128] = table


def gain_rows(r, layer):
    layers = r.resid.shape[0]
    return tuple(r.vecs[k * layers + layer : k * layers + layer + 1, :] for k in range(5))


def forward_attention(r, layer):
    bf16 = jnp.bfloat16
    g1, b1, _, _, _ = gain_rows(r, layer)
    part = r.ctx.shape[2]
    normed_a = (r.unit[layer].astype(jnp.float32) * g1 + b1).astype(bf16)
    projected = dot_nn(normed_a, r.wq[layer])
    tables = (r.same[...], r.up[...], r.down[...])
    for which in range(3):
        block = projected[:, which * part : (which + 1) * part]
        block = block + r.bq[3 * layer + which : 3 * layer + which + 1, :]
        if which < 2:
            block = turn(block, *tables, 1.0)
        r.qkv[layer, :, which * part : (which + 1) * part] = block.astype(bf16)
    allowed = r.mask[...] > 0.0
    for head in range(part // HD):
        q, k, v = (
            r.qkv[layer, :, which * part + head * HD : which * part + (head + 1) * HD]
            for which in range(3)
        )
        probs = head_scores(q, k, allowed).astype(bf16)
        r.ctx[layer, :, head * HD : (head + 1) * HD] = dot_nn(probs, v).astype(bf16)


def forward_hidden(r, layer):
    bf16 = jnp.bfloat16
    _, _, g2, b2, _ = gain_rows(r, layer)
    normed_m = (r.unit[layer].astype(jnp.float32) * g2 + b2).astype(bf16)
    hidden = dot_nn(normed_m, r.wf[layer]) + r.bf[layer : layer + 1, :]
    r.pre[layer] = hidden
    r.act[layer] = gelu_exact(hidden).astype(bf16)


def forward_part(r, layer):
    r.part_f[layer] = (
        dot_nn(r.ctx[layer], r.wo[layer]) + dot_nn(r.act[layer], r.wp[layer])
    ).astype(jnp.bfloat16)


def backward_hidden(r, layer):
    bf16 = jnp.bfloat16
    r.dctx[...] = dot_nt(r.drows[layer], r.wo[layer]).astype(bf16)
    r.du[layer] = (dot_nt(r.drows[layer], r.wp[layer]) * gelu_slope(r.pre[layer])).astype(bf16)


def backward_attention(r, layer):
    bf16, f32 = jnp.bfloat16, jnp.float32
    part = r.ctx.shape[2]
    allowed = r.mask[...] > 0.0
    pieces = [[], [], []]
    for head in range(part // HD):
        here = slice(head * HD, (head + 1) * HD)
        q, k, v = (
            r.qkv[layer, :, which * part + head * HD : which * part + (head + 1) * HD]
            for which in range(3)
        )
        dc = r.dctx[:, here]
        probs = head_scores(q, k, allowed)
        delta = jnp.sum(
            dc.astype(f32) * r.ctx[layer, :, here].astype(f32), axis=-1, keepdims=True
        )
        d_scaled = (probs * (dot_nt(dc, v) - delta) * HD ** (-0.5)).astype(bf16)
        pieces[0].append(dot_nn(d_scaled, k))
        pieces[1].append(dot_tn(d_scaled, q))
        pieces[2].append(dot_tn(probs.astype(bf16), dc))
    tables = (r.same[...], r.up[...], r.down[...])
    for which in range(3):
        block = jnp.concatenate(pieces[which], axis=1)
        if which < 2:
            block = turn(block, *tables, -1.0)
        r.dqkv[layer, :, which * part : (which + 1) * part] = block.astype(bf16)


def backward_part(r, layer):
    g1, _, g2, _, _ = gain_rows(r, layer)
    d_a = dot_nt(r.dqkv[layer], r.wq[layer])
    d_m = dot_nt(r.du[layer], r.wf[layer])
    r.part_e[layer] = (d_a * g1 + d_m * g2).astype(jnp.bfloat16)
    wide = r.unit[layer].astype(jnp.float32)
    for row, term in enumerate((d_a * wide, d_a, d_m * wide, d_m)):
        r.sums[5 * layer + row : 5 * layer + row + 1, :] = jnp.sum(term, axis=0, keepdims=True)


def pack_small(r, links):
    count, layers, vec = r.sv.shape
    width = vec * links.n_tensor
    r.pack[...] = jnp.zeros_like(r.pack)
    owner = lax.broadcasted_iota(jnp.int32, (layers, width), 1) // vec
    for k in range(count):
        value = jnp.concatenate([r.sv[k]] * links.n_tensor, axis=1)
        r.pack[k * layers : (k + 1) * layers, 0:width] = jnp.where(
            owner == links.tensor, value, 0.0
        )
    at = count * layers
    for layer in range(layers):
        r.pack[at + 3 * layer : at + 3 * layer + 3, 0 : r.sq.shape[2]] = r.sq[layer]
    at = at + 3 * layers
    r.pack[at : at + layers, 0 : r.sf.shape[1]] = r.sf[...]


def unpack_small(r, links):
    count, layers, vec = r.sv.shape
    width = vec * links.n_tensor
    rows = count * layers
    for d in range(links.n_dp):
        total = r.small[0, d, 0:rows, 0:width]
        for t in range(1, links.n_tensor):
            total = total + r.small[t, d, 0:rows, 0:width]
        r.vecs[0:rows, d * width : (d + 1) * width] = total
    for ref, height, lanes in ((r.bq, 3 * layers, r.sq.shape[2]), (r.bf, layers, r.sf.shape[1])):
        ref[0:height, :] = jnp.concatenate(
            [r.small[links.tensor, d, rows : rows + height, 0:lanes] for d in range(links.n_dp)],
            axis=1,
        )
        rows = rows + height


def in_columns(r, links, layer):
    for blocks, whole in ((r.wo_blocks, r.wo), (r.wp_blocks, r.wp)):
        width = blocks.shape[3]
        for d in range(links.n_dp):
            whole[layer, :, d * width : (d + 1) * width] = blocks[layer, d]


def layers_kernel(n_dp, n_tensor, names, *refs):
    r = types.SimpleNamespace(**dict(zip(names, refs)))
    links = Links(n_dp, n_tensor, r.send_sems, r.recv_sems, r.local_sems)
    bf16 = jnp.bfloat16
    layers = r.w_out.shape[0]
    last = layers - 1
    columns_ok = not hasattr(r, "wo_blocks")
    x_load = links.local(r.x_in, r.resid.at[0])
    d_load = links.local(r.grad_out, r.dres.at[last])
    loads = [links.local(r.lens, r.lens_v)]
    for k, ref in enumerate((r.ln1_gain, r.ln1_bias, r.ln2_gain, r.ln2_bias, r.res_bias)):
        loads.append(links.local(ref, r.sv.at[k]))
    loads.append(links.local(r.b_qkv, r.sq))
    loads.append(links.local(r.b_fc, r.sf))

    qkv_g, fc_g, proj_g, fwd_g, du_g, dqkv_g = [], [], [], [], [], []
    for layer in range(layers):
        dp_width = r.w_qkv.shape[1]
        qkv_g.append(
            Group(DpGather(links, r.w_qkv.at[layer], row_slot(r.wq.at[layer], dp_width)))
        )
        fc_g.append(Group(DpGather(links, r.w_fc.at[layer], row_slot(r.wf.at[layer], dp_width))))
        if columns_ok:
            slots = [column_slot(ref.at[layer], dp_width) for ref in (r.wo, r.wp)]
        else:
            slots = [lead_slot(ref.at[layer]) for ref in (r.wo_blocks, r.wp_blocks)]
        proj_g.append(
            Group(
                DpGather(links, r.w_out.at[layer], slots[0]),
                DpGather(links, r.w_proj.at[layer], slots[1]),
            )
        )
        rows = r.ctx.shape[1]
        ctx_j, act_j, dqkv_j, du_j = (
            DpGather(links, own.at[layer], row_slot(whole.at[layer], rows))
            for own, whole in (
                (r.ctx, r.ctx_all),
                (r.act, r.act_all),
                (r.dqkv, r.dqkv_all),
                (r.du, r.du_all),
            )
        )
        fwd_g.append(Group(ctx_j, act_j))
        du_g.append(Group(du_j))
        dqkv_g.append(Group(dqkv_j))

    links.barrier()
    pump = Pump()
    for layer in range(layers):
        for group in (qkv_g[layer], fc_g[layer], proj_g[layer]):
            pump.add(group)
    x_load.wait()
    unit = unit_rows(r.resid[0])[0].astype(bf16)
    unit_s = Spread(links, r.unit.at[0], unit)
    for load in loads:
        load.wait()
    pack_small(r, links)
    here = r.small.at[links.tensor, links.dp]
    small_sent = [links.send(r.pack, here, dp=links.dp_peer(step)) for step in range(1, n_dp)]
    small_kept = links.local(r.pack, here)
    d_load.wait()
    d_bf = r.dres[last].astype(bf16)
    rows_s = Spread(links, r.drows.at[last], d_bf)
    crosses = [
        Cross(links, r.stage.at[0, 0], r.cross.at[0, 0], unit),
        Cross(links, r.stage.at[last, 1], r.cross.at[last, 1], d_bf),
    ]
    r.sums[...] = jnp.zeros_like(r.sums)
    layout_tables(r)
    pump.relay()
    small_kept.wait()
    for copy in small_sent:
        copy.wait_recv()
    mine = r.small.at[links.tensor]
    small_wide = [
        links.send(mine, mine, tensor=links.tensor_peer(step)) for step in range(1, n_tensor)
    ]
    for copy in small_wide:
        copy.wait_recv()
    unpack_small(r, links)

    for layer in range(layers):
        pump.rest()
        qkv_g[layer].finish()
        if layer > 0:
            pump.relay()
        unit_s.finish()
        forward_attention(r, layer)
        if layer == 0:
            pump.relay()
        pump.rest()
        fc_g[layer].finish()
        forward_hidden(r, layer)
        pump.add(fwd_g[layer])
        pump.relay()
        pump.rest()
        proj_g[layer].finish()
        if not columns_ok:
            in_columns(r, links, layer)
        forward_part(r, layer)
        scatter = Scatter(links, r.part_f.at[layer], r.land_f.at[layer])
        if layer == 0:
            for cross in crosses:
                cross.forward()
        if layer < last:
            pump.relay()
            values = r.resid[layer] + scatter.total() + gain_rows(r, layer)[4]
            r.resid[layer + 1] = values
            unit = unit_rows(values)[0].astype(bf16)
            unit_s = Spread(links, r.unit.at[layer + 1], unit)
            crosses.append(
                Cross(links, r.stage.at[layer + 1, 0], r.cross.at[layer + 1, 0], unit)
            )

    sent_y = scatter
    width = r.half.shape[1]
    for layer in reversed(range(layers)):
        rows_s.finish()
        backward_hidden(r, layer)
        pump.add(du_g[layer])
        if layer < last:
            pump.rest()
        pump.relay()
        backward_attention(r, layer)
        pump.add(dqkv_g[layer])
        pump.rest()
        backward_part(r, layer)
        scatter = Scatter(links, r.part_e.at[layer], r.land_e.at[layer])
        r.sums[5 * layer + 4 : 5 * layer + 5, :] = jnp.sum(r.dres[layer], axis=0, keepdims=True)
        if layer == 0:
            for d in range(n_dp):
                r.sums_stage[d] = r.sums[:, d * width : (d + 1) * width]
            sums_sent = [
                links.send(
                    r.sums_stage.at[links.dp_peer(step)],
                    r.land_s.at[step - 1],
                    dp=links.dp_peer(step),
                )
                for step in range(1, n_dp)
            ]
        pump.relay()
        if layer > 0:
            for cross in crosses[2:]:
                cross.forward()
            new_d = r.dres[layer] + back_unit(r.resid[layer], scatter.total())
            r.dres[layer - 1] = new_d
            d_bf = new_d.astype(bf16)
            rows_s = Spread(links, r.drows.at[layer - 1], d_bf)
            crosses.append(
                Cross(links, r.stage.at[layer - 1, 1], r.cross.at[layer - 1, 1], d_bf)
            )
            pump.rest()
            pump.relay()

    r.y_v[...] = r.resid[last] + sent_y.total() + gain_rows(r, last)[4]
    stores = [links.local(r.y_v, r.y_out), links.local(r.vecs, r.vecs_out)]
    r.gx_v[...] = r.dres[0] + back_unit(r.resid[0], scatter.total())
    stores.append(links.local(r.gx_v, r.grad_x))
    for cross in crosses[layers + 1 :]:
        cross.forward()
    total = r.sums_stage[links.dp]
    for step, copy in enumerate(sums_sent):
        copy.wait_recv()
        total = total + r.land_s[step]
    r.half[...] = total
    wide = [
        links.send(r.half, r.land_t.at[step - 1], tensor=links.tensor_peer(step))
        for step in range(1, n_tensor)
    ]
    while pump.relayed or pump.started:
        if pump.relayed:
            pump.rest()
        if pump.started:
            pump.relay()
    for step, copy in enumerate(wide):
        copy.wait_recv()
        total = total + r.land_t[step]
    r.total_v[...] = total
    stores.append(links.local(r.total_v, r.total_out))
    for group in fwd_g + du_g + dqkv_g:
        group.finish()
    for cross in crosses:
        cross.finish()
    for store in stores:
        store.wait()
    links.finish()


def grads_kernel(n_tensor, names, *refs):
    r = types.SimpleNamespace(**dict(zip(names, refs)))
    r.g_out = [getattr(r, f"g{k}") for k in range(5)]
    bf16, f32 = jnp.bfloat16, jnp.float32
    layers = r.w_out_g.shape[0]
    dp, tensor = lax.axis_index("dp"), lax.axis_index("tensor")
    count = [0]

    def local(src, dst):
        copy = pltpu.make_async_copy(src, dst, r.sems.at[count[0]])
        count[0] += 1
        copy.start()
        return copy

    stores = [local(r.y_in, r.y_out), local(r.gx_in, r.grad_x)]
    first = [local(r.vecs, r.vecs_v), local(r.total, r.total_v), local(r.cross, r.cross_v)]
    loads = []
    for layer in range(layers):
        for source, place in (
            (r.ctx_all, r.ctx_v),
            (r.act_all, r.act_v),
            (r.du_all, r.du_v),
            (r.dqkv_all, r.dqkv_v),
        ):
            loads.append(local(source.at[layer], place.at[layer]))
    for load in first:
        load.wait()
    width = r.cross.shape[-1]
    vec = r.g_out[0].shape[1]
    rolled = pltpu.roll(r.total_v[...], lax.rem(width - tensor * vec, width), 1)
    for k in range(5):
        for layer in range(layers):
            r.g_v[k, layer : layer + 1, :] = rolled[5 * layer + k : 5 * layer + k + 1, 0:vec]
        stores.append(local(r.g_v.at[k], r.g_out[k]))
    mine = pl.ds(pl.multiple_of(dp * width, width), width)
    for layer in range(layers):
        unit = r.cross_v[layer, 0].reshape(-1, width).astype(f32)
        d_t = r.cross_v[layer, 1].reshape(-1, width)
        g1, b1, g2, b2 = (
            r.vecs_v[k * layers + layer : k * layers + layer + 1, mine] for k in range(4)
        )
        a_t = (unit * g1 + b1).astype(bf16)
        m_t = (unit * g2 + b2).astype(bf16)
        ctx_l, act_l, du_l, dqkv_l = loads[4 * layer : 4 * layer + 4]
        ctx_l.wait()
        r.out_v[layer] = jnp.transpose(dot_tn(d_t, r.ctx_v[layer]))
        stores.append(local(r.out_v.at[layer], r.w_out_g.at[layer]))
        act_l.wait()
        r.proj_v[layer] = jnp.transpose(dot_tn(d_t, r.act_v[layer]))
        stores.append(local(r.proj_v.at[layer], r.w_proj_g.at[layer]))
        du_l.wait()
        r.fc_v[layer] = dot_tn(m_t, r.du_v[layer])
        stores.append(local(r.fc_v.at[layer], r.w_fc_g.at[layer]))
        dqkv_l.wait()
        r.qkv_v[layer] = dot_tn(a_t, r.dqkv_v[layer])
        stores.append(local(r.qkv_v.at[layer], r.w_qkv_g.at[layer]))
        own = r.bq_v.shape[2]
        part = r.ctx_v.shape[2]
        block = (dp * own) // 128 * 128
        back = lax.rem(128 - lax.rem(dp * own, 128), 128)
        for which in range(3):
            columns = pl.ds(pl.multiple_of(which * part + block, 128), 128)
            sums = jnp.sum(r.dqkv_v[layer, :, columns].astype(f32), axis=0, keepdims=True)
            r.bq_v[layer, which : which + 1, :] = pltpu.roll(sums, back, 1)[:, 0:own]
        own = r.bf_v.shape[1]
        columns = pl.ds(pl.multiple_of(dp * own, own), own)
        r.bf_v[layer : layer + 1, :] = jnp.sum(
            r.du_v[layer, :, columns].astype(f32), axis=0, keepdims=True
        )
    stores.append(local(r.bq_v, r.b_qkv_g))
    stores.append(local(r.bf_v, r.b_fc_g))
    for store in stores:
        store.wait()


def shaped(shape, dtype):
    return jax.ShapeDtypeStruct(tuple(shape), dtype)


def kernel_call(kernel, name, ins, outs, scratch, params):
    names = list(ins) + list(outs) + list(scratch)
    results = pl.pallas_call(
        functools.partial(kernel, names),
        out_shape=tuple(outs.values()),
        in_specs=[ANY] * len(ins),
        out_specs=(ANY,) * len(outs),
        scratch_shapes=list(scratch.values()),
        name=name,
        compiler_params=pltpu.CompilerParams(**params),
    )(*ins.values())
    return dict(zip(outs, results))


def per_device(
    x_in,
    seq_lengths,
    ln1_gain,
    ln1_bias,
    ln2_gain,
    ln2_bias,
    res_bias,
    w_qkv,
    b_qkv,
    w_out,
    w_fc,
    b_fc,
    w_proj,
    grad_out,
):
    n_tensor, n_dp = lax.axis_size("tensor"), lax.axis_size("dp")
    my_tensor, my_dp = lax.axis_index("tensor"), lax.axis_index("dp")
    bf16, f32 = jnp.bfloat16, jnp.float32
    my_rows, width = x_in.shape
    group_rows = my_rows * n_tensor
    total_rows = group_rows * n_dp
    layers = w_qkv.shape[0]
    part = w_qkv.shape[3]
    hidden = w_fc.shape[2]
    dp_width = width // n_dp
    vec = ln1_gain.shape[1]
    columns_ok = dp_width % 128 == 0
    vm = pltpu.VMEM
    pad8 = lambda n: -(-n // 8) * 8
    small_rows = pad8(9 * layers)
    vec_rows = pad8(5 * layers)

    ins = {
        "x_in": x_in,
        "lens": seq_lengths,
        "ln1_gain": ln1_gain,
        "ln1_bias": ln1_bias,
        "ln2_gain": ln2_gain,
        "ln2_bias": ln2_bias,
        "res_bias": res_bias,
        "w_qkv": w_qkv.reshape(layers, dp_width, -1),
        "b_qkv": b_qkv,
        "w_out": w_out,
        "w_fc": w_fc,
        "b_fc": b_fc,
        "w_proj": w_proj,
        "grad_out": grad_out,
    }
    outs = {
        "y_out": shaped(x_in.shape, f32),
        "grad_x": shaped(x_in.shape, f32),
        "vecs_out": shaped((vec_rows, width), f32),
        "total_out": shaped((vec_rows, dp_width), f32),
        "cross": shaped((layers, 2, n_dp, n_tensor, my_rows, dp_width), bf16),
        "ctx_all": shaped((layers, total_rows, part), bf16),
        "act_all": shaped((layers, total_rows, hidden), bf16),
        "dqkv_all": shaped((layers, total_rows, 3 * part), bf16),
        "du_all": shaped((layers, total_rows, hidden), bf16),
    }
    rows_block = (layers, my_rows, width)
    group_block = (layers, group_rows, width)
    land = (layers, n_tensor - 1, my_rows, width)
    scratch = {
        "resid": vm(rows_block, f32),
        "dres": vm(rows_block, f32),
        "lens_v": vm(seq_lengths.shape, jnp.int32),
        "sv": vm((5,) + ln1_gain.shape, f32),
        "sq": vm(b_qkv.shape, f32),
        "sf": vm(b_fc.shape, f32),
        "pack": vm((small_rows, 128), f32),
        "small": vm((n_tensor, n_dp, small_rows, 128), f32),
        "vecs": vm((vec_rows, width), f32),
        "bq": vm((pad8(3 * layers), part), f32),
        "bf": vm((pad8(layers), hidden), f32),
        "same": vm((group_rows, part), f32),
        "up": vm((group_rows, part), f32),
        "down": vm((group_rows, part), f32),
        "mask": vm((group_rows, group_rows), f32),
        "wq": vm((layers, width, 3 * part), bf16),
        "wf": vm((layers, width, hidden), bf16),
        "wo": vm((layers, part, width), bf16),
        "wp": vm((layers, hidden, width), bf16),
        "unit": vm(group_block, bf16),
        "drows": vm(group_block, bf16),
        "qkv": vm((layers, group_rows, 3 * part), bf16),
        "ctx": vm((layers, group_rows, part), bf16),
        "pre": vm((layers, group_rows, hidden), f32),
        "act": vm((layers, group_rows, hidden), bf16),
        "dctx": vm((group_rows, part), bf16),
        "du": vm((layers, group_rows, hidden), bf16),
        "dqkv": vm((layers, group_rows, 3 * part), bf16),
        "part_f": vm(group_block, bf16),
        "part_e": vm(group_block, bf16),
        "land_f": vm(land, bf16),
        "land_e": vm(land, bf16),
        "stage": vm((layers, 2, n_dp, my_rows, dp_width), bf16),
        "sums": vm((vec_rows, width), f32),
        "sums_stage": vm((n_dp, vec_rows, dp_width), f32),
        "land_s": vm((n_dp - 1, vec_rows, dp_width), f32),
        "half": vm((vec_rows, dp_width), f32),
        "land_t": vm((n_tensor - 1, vec_rows, dp_width), f32),
        "total_v": vm((vec_rows, dp_width), f32),
        "y_v": vm((my_rows, width), f32),
        "gx_v": vm((my_rows, width), f32),
        "send_sems": pltpu.SemaphoreType.DMA((N_SEMS,)),
        "recv_sems": pltpu.SemaphoreType.DMA((N_SEMS,)),
        "local_sems": pltpu.SemaphoreType.DMA((N_LOCAL,)),
    }
    if not columns_ok:
        scratch["wo_blocks"] = vm((layers, n_dp, part, dp_width), bf16)
        scratch["wp_blocks"] = vm((layers, n_dp, hidden, dp_width), bf16)
    step = kernel_call(
        functools.partial(layers_kernel, n_dp, n_tensor),
        "layers",
        ins,
        outs,
        scratch,
        {"collective_id": 0, "has_side_effects": True, "vmem_limit_bytes": 58 << 20},
    )

    act_bytes = layers * total_rows * (4 * part + 2 * hidden) * 2
    if act_bytes <= 16 << 20 and columns_ok:
        grad_ins = {
            "y_in": step["y_out"],
            "gx_in": step["grad_x"],
            "vecs": step["vecs_out"],
            "total": step["total_out"],
        }
        scratch = {
            "vecs_v": vm((vec_rows, width), f32),
            "total_v": vm((vec_rows, dp_width), f32),
            "g_v": vm((5, layers, vec), f32),
            "bq_v": vm(b_qkv.shape, f32),
            "bf_v": vm(b_fc.shape, f32),
            "qkv_v": vm((layers, dp_width, 3 * part), f32),
            "out_v": vm(w_out.shape, f32),
            "fc_v": vm(w_fc.shape, f32),
            "proj_v": vm(w_proj.shape, f32),
            "sems": pltpu.SemaphoreType.DMA((64,)),
        }
        for name in ("cross", "ctx_all", "act_all", "dqkv_all", "du_all"):
            grad_ins[name] = step[name]
            scratch[name.removesuffix("_all") + "_v"] = vm(step[name].shape, bf16)
        grad_outs = {"y_out": shaped(x_in.shape, f32), "grad_x": shaped(x_in.shape, f32)}
        for k in range(5):
            grad_outs[f"g{k}"] = shaped(ln1_gain.shape, f32)
        grad_outs |= {
            "w_qkv_g": shaped((layers, dp_width, 3 * part), f32),
            "b_qkv_g": shaped(b_qkv.shape, f32),
            "w_out_g": shaped(w_out.shape, f32),
            "w_fc_g": shaped(w_fc.shape, f32),
            "b_fc_g": shaped(b_fc.shape, f32),
            "w_proj_g": shaped(w_proj.shape, f32),
        }
        done = kernel_call(
            functools.partial(grads_kernel, n_tensor),
            "grads",
            grad_ins,
            grad_outs,
            scratch,
            {"vmem_limit_bytes": 58 << 20},
        )
        return (
            tuple(done[name] for name in ("y_out", "grad_x", "g0", "g1", "g2", "g3", "g4"))
            + (done["w_qkv_g"].reshape(w_qkv.shape),)
            + tuple(done[name] for name in ("b_qkv_g", "w_out_g", "w_fc_g", "b_fc_g", "w_proj_g"))
        )

    over_tokens = (((0,), (0,)), ((), ()))
    grads = [[] for _ in range(6)]
    vectors = step["vecs_out"][: 5 * layers].reshape(5, layers, width)
    vectors = lax.dynamic_slice_in_dim(vectors, my_dp * dp_width, dp_width, axis=2)
    for layer in range(layers):
        context_t, act_t, dqkv_t, d_pre_t = (
            step[name][layer] for name in ("ctx_all", "act_all", "dqkv_all", "du_all")
        )
        unit_t = step["cross"][layer, 0].reshape(total_rows, dp_width).astype(f32)
        d_t = step["cross"][layer, 1].reshape(total_rows, dp_width)
        a_t = (unit_t * vectors[0, layer] + vectors[1, layer]).astype(bf16)
        m_t = (unit_t * vectors[2, layer] + vectors[3, layer]).astype(bf16)

        def contract(left, right):
            return lax.dot_general(left, right, over_tokens, preferred_element_type=f32)

        qkv_sums = jnp.sum(dqkv_t.astype(f32), axis=0).reshape(3, -1)
        fc_sums = jnp.sum(d_pre_t.astype(f32), axis=0)
        grads[0].append(contract(a_t, dqkv_t).reshape(w_qkv.shape[1:]))
        grads[1].append(
            lax.dynamic_slice_in_dim(qkv_sums, my_dp * b_qkv.shape[2], b_qkv.shape[2], axis=1)
        )
        grads[2].append(contract(context_t, d_t))
        grads[3].append(contract(m_t, d_pre_t))
        grads[4].append(lax.dynamic_slice_in_dim(fc_sums, my_dp * b_fc.shape[1], b_fc.shape[1]))
        grads[5].append(contract(act_t, d_t))
    vector_grads = lax.dynamic_slice_in_dim(
        step["total_out"][: 5 * layers].reshape(layers, 5, dp_width), my_tensor * vec, vec, axis=2
    )
    return (
        (step["y_out"], step["grad_x"])
        + tuple(vector_grads[:, k] for k in range(5))
        + tuple(jnp.stack(group) for group in grads)
    )


def solution(mesh):
    in_specs = (
        P(("dp", "tensor"), None),
        P("dp", None),
        P(None, ("dp", "tensor")),
        P(None, ("dp", "tensor")),
        P(None, ("dp", "tensor")),
        P(None, ("dp", "tensor")),
        P(None, ("dp", "tensor")),
        P(None, "dp", None, "tensor"),
        P(None, None, ("tensor", "dp")),
        P(None, "tensor", "dp"),
        P(None, "dp", "tensor"),
        P(None, ("tensor", "dp")),
        P(None, "tensor", "dp"),
        P(("dp", "tensor"), None),
    )
    out_specs = (
        P(("dp", "tensor"), None),
        P(("dp", "tensor"), None),
        P(None, ("dp", "tensor")),
        P(None, ("dp", "tensor")),
        P(None, ("dp", "tensor")),
        P(None, ("dp", "tensor")),
        P(None, ("dp", "tensor")),
        P(None, "dp", None, "tensor"),
        P(None, None, ("tensor", "dp")),
        P(None, "tensor", "dp"),
        P(None, "dp", "tensor"),
        P(None, ("tensor", "dp")),
        P(None, "tensor", "dp"),
    )
    return jax.shard_map(
        per_device, mesh=mesh, in_specs=in_specs, out_specs=out_specs, check_vma=False
    )
```

```python
import functools
import types

import jax
import jax.numpy as jnp
from jax import lax
from jax.experimental import pallas as pl
from jax.experimental.pallas import tpu as pltpu
from jax.sharding import PartitionSpec as P

HD = 64
ROT = 16


EPS = 1e-05
NEG_FILL = -1e30


def gelu_exact(values):
    return 0.5 * values * (1.0 + jax.scipy.special.erf(values * 0.7071067811865476))


def gelu_slope(values):
    normal_cdf = 0.5 * (1.0 + jax.scipy.special.erf(values * 0.7071067811865476))
    return normal_cdf + values * jnp.exp(-0.5 * values * values) * 0.3989422804014327


MESH = pl.DeviceIdType.MESH
ANY = pl.BlockSpec(memory_space=pl.ANY)
VMEM = pl.BlockSpec(memory_space=pltpu.VMEM)


def copy_counts(n_dp, n_tensor, layers):
    chips = n_dp // 2
    remote = (n_tensor - 1) * (6 * layers + 2) + (n_dp - 1) * 3
    if chips == 4:
        return remote + layers * (4 * 13 + 4 * 3 + 2 * 3 + 4), 14 * layers + 14
    return remote + layers * (8 * (4 * chips - 3) + 2 * (n_dp - 1)), 10 * layers + 15


class Links:
    def __init__(self, n_dp, n_tensor, send_sems, recv_sems, local_sems):
        self.n_dp, self.n_tensor = n_dp, n_tensor
        self.dp, self.tensor = lax.axis_index("dp"), lax.axis_index("tensor")
        self.core, self.chip = lax.rem(self.dp, 2), self.dp // 2
        self.partner = self.dp + 1 - 2 * self.core
        self.paired = n_dp == 8
        if self.paired:
            self.x = lax.rem(self.chip, 2)
            self.over_x = self.dp + 2 - 4 * self.x
            self.over_y = lax.rem(self.dp + 4, 8)
            self.place = self.chip // 2 * 2 + self.core
            self.far_place = lax.rem(self.place + 2, 4)
        self.send_sems, self.recv_sems, self.local_sems = send_sems, recv_sems, local_sems
        self.used, self.used_local = 0, 0
        self.sent = []

    def send(self, src, dst, **where):
        copy = pltpu.make_async_remote_copy(
            src_ref=src,
            dst_ref=dst,
            send_sem=self.send_sems.at[self.used],
            recv_sem=self.recv_sems.at[self.used],
            device_id=where,
            device_id_type=MESH,
        )
        self.used += 1
        copy.start()
        self.sent.append(copy)
        return copy

    def local(self, src, dst):
        copy = pltpu.make_async_copy(src, dst, self.local_sems.at[self.used_local])
        self.used_local += 1
        copy.start()
        return copy

    def dp_peer(self, step):
        return lax.rem(self.dp + step, self.n_dp)

    def tensor_peer(self, step):
        return lax.rem(self.tensor + step, self.n_tensor)

    def enter(self):
        sem = pltpu.get_barrier_semaphore()
        for step in range(1, self.n_tensor):
            pl.semaphore_signal(
                sem, inc=1, device_id={"tensor": self.tensor_peer(step)}, device_id_type=MESH
            )
        for step in range(1, self.n_dp):
            pl.semaphore_signal(
                sem, inc=1, device_id={"dp": self.dp_peer(step)}, device_id_type=MESH
            )

    def barrier(self):
        pl.semaphore_wait(pltpu.get_barrier_semaphore(), self.n_tensor + self.n_dp - 2)

    def finish(self):
        for copy in self.sent:
            copy.wait_send()


class DpGather:
    def __init__(self, links, own, slot, axis=0):
        self.links, self.own, self.slot = links, own, slot
        self.chips = links.n_dp // 2
        self.core, self.chip, self.partner = links.core, links.chip, links.partner
        self.relays = self.chips == 4
        rows = own.shape[axis] // 2
        self.halves = [
            (slice(None),) * axis + (pl.ds(half * rows, rows),) for half in range(2)
        ]
        self.passed = []
        if self.relays:
            near = self.chip + 1 - 2 * lax.rem(self.chip, 2)
            far = lax.rem(self.chip + 2, 4)
            self.across = lax.rem(near + 2, 4)
            self.order = ((near, far), (far, near))

    def device(self, chip):
        return chip * 2 + self.core

    def out(self, rows, chip):
        return self.links.send(
            self.own.at[rows], self.slot(self.links.dp).at[rows], dp=self.device(chip)
        )

    def pass_on(self, rows, chip, target):
        block = self.slot(self.device(chip)).at[rows]
        return self.links.send(block, block, dp=target)

    def start(self):
        if self.relays:
            self.first = [self.out(rows, order[0]) for rows, order in zip(self.halves, self.order)]
            self.second = [self.out(rows, order[1]) for rows, order in zip(self.halves, self.order)]
        else:
            self.direct = [
                [self.out(rows, lax.rem(self.chip + step, self.chips)) for rows in self.halves]
                for step in range(1, self.chips)
            ]
        own_slot = self.slot(self.links.dp)
        self.passed.append(self.links.send(self.own, own_slot, dp=self.partner))
        self.kept = self.links.local(self.own, own_slot)

    def relay(self):
        if not self.relays:
            return
        self.relayed = []
        for copy, rows, order in zip(self.first, self.halves, self.order):
            copy.wait_recv()
            self.relayed.append(self.pass_on(rows, order[0], self.device(order[1])))
            self.passed.append(self.pass_on(rows, order[0], self.partner))

    def rest(self):
        if not self.relays:
            for step, copies in enumerate(self.direct):
                origin = lax.rem(self.chip + self.chips - step - 1, self.chips)
                for copy, rows in zip(copies, self.halves):
                    copy.wait_recv()
                    self.passed.append(self.pass_on(rows, origin, self.partner))
            return
        for copy, rows, order in zip(self.second, self.halves, self.order):
            copy.wait_recv()
            self.passed.append(self.pass_on(rows, order[1], self.partner))
        for copy, rows in zip(self.relayed, self.halves):
            copy.wait_recv()
            self.passed.append(self.pass_on(rows, self.across, self.partner))

    def finish(self):
        for copy in self.passed:
            copy.wait_recv()
        self.kept.wait()


class PairGather:
    def __init__(self, links, own, slot):
        self.links, self.own, self.slot = links, own, slot

    def start(self):
        links, here = self.links, self.slot(self.links.place)
        self.out = links.send(self.own, here, dp=links.over_y)
        self.passed = [links.send(self.own, here, dp=links.partner)]
        self.kept = links.local(self.own, here)

    def rest(self):
        self.out.wait_recv()
        block = self.slot(self.links.far_place)
        self.passed.append(self.links.send(block, block, dp=self.links.partner))

    def finish(self):
        for copy in self.passed:
            copy.wait_recv()
        self.kept.wait()


class Group:
    def __init__(self, *gathers):
        self.gathers = gathers

    def start(self):
        for gather in self.gathers:
            gather.start()

    def relay(self):
        for gather in self.gathers:
            gather.relay()

    def rest(self):
        for gather in self.gathers:
            gather.rest()

    def finish(self):
        for gather in self.gathers:
            gather.finish()


class Pump:
    def __init__(self):
        self.todo, self.started, self.relayed, self.every = [], [], [], []

    def add(self, group):
        self.todo.append(group)
        self.every.append(group)
        if not self.started:
            self.start()

    def start(self):
        if self.todo:
            group = self.todo.pop(0)
            group.start()
            self.started.append(group)

    def relay(self):
        group = self.started.pop(0)
        group.relay()
        self.relayed.append(group)
        if not self.started:
            self.start()

    def rest(self):
        self.relayed.pop(0).rest()


def row_slot(ref, rows):
    return lambda d: ref.at[pl.ds(pl.multiple_of(d * rows, rows), rows)]


def middle_slot(ref, rows):
    return lambda d: ref.at[:, pl.ds(pl.multiple_of(d * rows, rows), rows)]


def column_slot(ref, size):
    return lambda d: ref.at[:, pl.ds(pl.multiple_of(d * size, size), size)]


def lead_slot(ref):
    return lambda d: ref.at[d]


class Scatter:
    def __init__(self, links, part, landing):
        self.links, self.part, self.landing = links, part, landing
        self.rows = landing.shape[1]
        slot = row_slot(part, self.rows)
        self.copies = [
            links.send(
                slot(links.tensor_peer(step)),
                landing.at[step - 1],
                tensor=links.tensor_peer(step),
            )
            for step in range(1, links.n_tensor)
        ]

    def total(self):
        own = pl.ds(pl.multiple_of(self.links.tensor * self.rows, self.rows), self.rows)
        total = self.part[own, :].astype(jnp.float32)
        for step, copy in enumerate(self.copies):
            copy.wait_recv()
            total = total + self.landing[step].astype(jnp.float32)
        return total


class Spread:
    def __init__(self, links, ref, value):
        rows = value.shape[0]
        self.links, self.here = links, row_slot(ref, rows)(links.tensor)
        ref[pl.ds(pl.multiple_of(links.tensor * rows, rows), rows), :] = value

    def send(self):
        links = self.links
        self.copies = [
            links.send(self.here, self.here, tensor=links.tensor_peer(step))
            for step in range(1, links.n_tensor)
        ]

    def finish(self):
        for copy in self.copies:
            copy.wait_recv()


class Cross:
    def __init__(self, links, stage, out, value):
        self.links, self.stage, self.out = links, stage, out
        self.count, _, width = stage.shape
        self.me = links.place if links.paired else links.dp
        if not links.paired:
            for d in range(self.count):
                stage[d] = value[:, d * width : (d + 1) * width]
            return
        half = width // 2
        wide = value.astype(jnp.float32)
        for s in range(self.count):
            at = [(s // 2 * 4 + 2 * x + s % 2) * half for x in range(2)]
            one, two = (wide[:, place : place + half] for place in at)
            stage[s, :, 0:half] = jnp.where(links.x == 0, one, two).astype(value.dtype)
            stage[s, :, half:width] = jnp.where(links.x == 0, two, one).astype(value.dtype)

    def send(self):
        links, stage = self.links, self.stage
        here = self.out.at[self.me, links.tensor]
        self.copies = []
        for step in range(1, self.count):
            peer = lax.rem(self.me + step, self.count)
            device = peer // 2 * 4 + 2 * links.x + lax.rem(peer, 2) if links.paired else peer
            self.copies.append(links.send(stage.at[peer], here, dp=device))
        self.kept = links.local(stage.at[self.me], here)

    def forward(self):
        links = self.links
        for copy in self.copies:
            copy.wait_recv()
        self.kept.wait()
        mine = self.out.at[:, links.tensor]
        self.wide = [
            links.send(mine, mine, tensor=links.tensor_peer(step))
            for step in range(1, links.n_tensor)
        ]

    def finish(self):
        for copy in self.wide:
            copy.wait_recv()


class Product:
    def __init__(self, links, own, away, landing, rows, columns):
        self.own, self.landing = own, landing
        parts = own.shape[0] if len(own.shape) == 3 else 1
        half, width = own.shape[-2:]
        for k in range(parts):
            total = dot_tn(rows, columns[:, k * width : (k + 1) * width])
            if len(own.shape) == 3:
                own[k] = total[:half]
                away[k] = total[half:].astype(away.dtype)
            else:
                own[...] = total[:half]
                away[...] = total[half:].astype(away.dtype)
        self.copy = links.send(away, landing, dp=links.over_x)

    def total(self):
        self.copy.wait_recv()
        return self.own[...] + self.landing[...].astype(jnp.float32)


def unit_rows(values):
    average = jnp.mean(values, axis=-1, keepdims=True)
    centred = values - average
    variance = jnp.mean(centred * centred, axis=-1, keepdims=True)
    scale = lax.rsqrt(variance + EPS)
    return centred * scale, scale


def back_unit(values, grad):
    unit, scale = unit_rows(values)
    return scale * (
        grad
        - jnp.mean(grad, axis=-1, keepdims=True)
        - unit * jnp.mean(grad * unit, axis=-1, keepdims=True)
    )


def dot_nn(left, right):
    return jnp.dot(left, right, preferred_element_type=jnp.float32)


def dot_nt(left, right):
    return lax.dot_general(left, right, (((1,), (1,)), ((), ())), preferred_element_type=jnp.float32)


def dot_tn(left, right):
    return lax.dot_general(left, right, (((0,), (0,)), ((), ())), preferred_element_type=jnp.float32)


def turn(vectors, same, up, down, sign):
    width = vectors.shape[1]
    above = pltpu.roll(vectors, width - ROT // 2, 1)
    below = pltpu.roll(vectors, ROT // 2, 1)
    return vectors * same + sign * (above * up + below * down)


def head_scores(query, key, mask):
    scores = dot_nt(query, key) * HD ** (-0.5)
    scores = jnp.where(mask, scores, NEG_FILL)
    terms = jnp.exp(scores - jnp.max(scores, axis=-1, keepdims=True))
    return terms / jnp.sum(terms, axis=-1, keepdims=True)


def layout_tables(r):
    f32 = jnp.float32
    rows, width = r.same.shape
    lengths = r.lens_v[...]
    row_of = lax.broadcasted_iota(jnp.int32, (rows, rows), 0)
    col_of = lax.broadcasted_iota(jnp.int32, (rows, rows), 1)
    row_lane = lax.broadcasted_iota(jnp.int32, (rows, 128), 0)
    start = jnp.zeros((rows, rows), jnp.int32)
    start_lane = jnp.zeros((rows, 128), jnp.int32)
    end = jnp.zeros((1, 1), jnp.int32)
    for k in range(lengths.shape[1]):
        end = end + lengths[:, k : k + 1]
        start = jnp.where(row_of >= end, end, start)
        start_lane = jnp.where(row_lane >= end, end, start_lane)
    r.mask[...] = jnp.where((col_of >= start) & (col_of <= row_of), 1.0, 0.0)
    positions = (row_lane - start_lane).astype(f32)
    lane = lax.rem(lax.broadcasted_iota(jnp.int32, (1, 128), 1), HD)
    half = ROT // 2
    inverse = jnp.power(10000.0, -2.0 * lax.rem(lane, half).astype(f32) / ROT)
    angles = positions * inverse
    cos_tab, sin_tab = jnp.cos(angles), jnp.sin(angles)
    same = jnp.where(lane < ROT, cos_tab, 1.0)
    up = jnp.where(lane < half, -sin_tab, 0.0)
    down = jnp.where((lane >= half) & (lane < ROT), sin_tab, 0.0)
    for ref, table in ((r.same, same), (r.up, up), (r.down, down)):
        for place in range(width // 128):
            ref[:, place * 128 : (place + 1) * 128] = table


def gain_rows(r, layer):
    layers = r.resid.shape[0]
    return tuple(r.vecs[k * layers + layer : k * layers + layer + 1, :] for k in range(5))


def forward_attention(r, layer):
    bf16 = jnp.bfloat16
    g1, b1, _, _, _ = gain_rows(r, layer)
    layers, _, part = r.ctx.shape
    normed_a = (r.unit[layer].astype(jnp.float32) * g1 + b1).astype(bf16)
    tables = (r.same[...], r.up[...], r.down[...])
    for which in range(3):
        row = which * layers + layer
        block = dot_nn(normed_a, r.wq[layer, which]) + r.bq[row : row + 1, :]
        if which < 2:
            block = turn(block, *tables, 1.0)
        r.qkv[layer, :, which * part : (which + 1) * part] = block.astype(bf16)
    allowed = r.mask[...] > 0.0
    for head in range(part // HD):
        q, k, v = (
            r.qkv[layer, :, which * part + head * HD : which * part + (head + 1) * HD]
            for which in range(3)
        )
        probs = head_scores(q, k, allowed).astype(bf16)
        r.ctx[layer, :, head * HD : (head + 1) * HD] = dot_nn(probs, v).astype(bf16)


def forward_hidden(r, layer):
    bf16 = jnp.bfloat16
    _, _, g2, b2, _ = gain_rows(r, layer)
    normed_m = (r.unit[layer].astype(jnp.float32) * g2 + b2).astype(bf16)
    hidden = dot_nn(normed_m, r.wf[layer]) + r.bf[layer : layer + 1, :]
    r.pre[layer] = hidden
    r.act[layer] = gelu_exact(hidden).astype(bf16)


def forward_part(r, layer):
    r.part_f[layer] = (
        dot_nn(r.ctx[layer], r.wo[layer]) + dot_nn(r.act[layer], r.wp[layer])
    ).astype(jnp.bfloat16)


def backward_hidden(r, layer):
    bf16 = jnp.bfloat16
    r.dctx[...] = dot_nt(r.drows[layer], r.wo[layer]).astype(bf16)
    d_pre = dot_nt(r.drows[layer], r.wp[layer]) * gelu_slope(r.pre[layer])
    r.sums_f[layer : layer + 1, :] = jnp.sum(d_pre, axis=0, keepdims=True)
    r.du[layer] = d_pre.astype(bf16)


def backward_attention(r, layer):
    bf16, f32 = jnp.bfloat16, jnp.float32
    part = r.ctx.shape[2]
    allowed = r.mask[...] > 0.0
    pieces = [[], [], []]
    for head in range(part // HD):
        here = slice(head * HD, (head + 1) * HD)
        q, k, v = (
            r.qkv[layer, :, which * part + head * HD : which * part + (head + 1) * HD]
            for which in range(3)
        )
        dc = r.dctx[:, here]
        probs = head_scores(q, k, allowed)
        delta = jnp.sum(
            dc.astype(f32) * r.ctx[layer, :, here].astype(f32), axis=-1, keepdims=True
        )
        d_scaled = (probs * (dot_nt(dc, v) - delta) * HD ** (-0.5)).astype(bf16)
        pieces[0].append(dot_nn(d_scaled, k))
        pieces[1].append(dot_tn(d_scaled, q))
        pieces[2].append(dot_tn(probs.astype(bf16), dc))
    tables = (r.same[...], r.up[...], r.down[...])
    for which in range(3):
        block = jnp.concatenate(pieces[which], axis=1)
        if which < 2:
            block = turn(block, *tables, -1.0)
        row = which * r.ctx.shape[0] + layer
        r.sums_q[row : row + 1, :] = jnp.sum(block, axis=0, keepdims=True)
        r.dqkv[layer, :, which * part : (which + 1) * part] = block.astype(bf16)


def backward_part(r, layer):
    g1, _, g2, _, _ = gain_rows(r, layer)
    part = r.ctx.shape[2]
    d_a = sum(
        dot_nt(r.dqkv[layer, :, which * part : (which + 1) * part], r.wq[layer, which])
        for which in range(3)
    )
    d_m = dot_nt(r.du[layer], r.wf[layer])
    r.part_e[layer] = (d_a * g1 + d_m * g2).astype(jnp.bfloat16)
    wide = r.unit[layer].astype(jnp.float32)
    for row, term in enumerate((d_a * wide, d_a, d_m * wide, d_m)):
        r.sums[5 * layer + row : 5 * layer + row + 1, :] = jnp.sum(term, axis=0, keepdims=True)


def pack_small(r, links):
    count, layers, vec = r.sv.shape
    r.pack_v[...] = jnp.zeros_like(r.pack_v)
    owner = lax.broadcasted_iota(jnp.int32, (layers, vec * links.n_tensor), 1) // vec
    for k in range(count):
        value = jnp.concatenate([r.sv[k]] * links.n_tensor, axis=1)
        r.pack_v[k * layers : (k + 1) * layers, :] = jnp.where(owner == links.tensor, value, 0.0)
    r.pack_b[...] = jnp.zeros_like(r.pack_b)
    for which in range(3):
        r.pack_b[which * layers : (which + 1) * layers, 0 : r.sq.shape[2]] = r.sq[which]
    r.pack_b[3 * layers : 4 * layers, 0 : r.sf.shape[1]] = r.sf[...]


def unpack_small(r, links):
    layers = r.sf.shape[0]
    width = r.vec_all.shape[2]
    rows = 0
    for d in range(links.n_dp):
        r.vecs[:, d * width : (d + 1) * width] = r.vec_all[d]
    for ref, height, lanes in ((r.bq, 3 * layers, r.sq.shape[2]), (r.bf, layers, r.sf.shape[1])):
        ref[0:height, :] = jnp.concatenate(
            [r.small_b[d, rows : rows + height, 0:lanes] for d in range(links.n_dp)], axis=1
        )
        rows = rows + height


def in_columns(r, links, layer):
    for blocks, whole in ((r.wo_blocks, r.wo), (r.wp_blocks, r.wp)):
        width = blocks.shape[3]
        for d in range(links.n_dp):
            whole[layer, :, d * width : (d + 1) * width] = blocks[layer, d]


def start_sums(r, links):
    layers = r.resid.shape[0]
    width = r.sums_stage.shape[2]
    rows = r.sums.shape[0]
    lanes_q, lanes_f = r.sq.shape[2], r.sf.shape[1]
    r.sums_stage[...] = jnp.zeros_like(r.sums_stage)
    for d in range(links.n_dp):
        r.sums_stage[d, 0:rows, :] = r.sums[:, d * width : (d + 1) * width]
        r.sums_stage[d, rows : rows + 3 * layers, 0:lanes_q] = r.sums_q[
            0 : 3 * layers, d * lanes_q : (d + 1) * lanes_q
        ]
        r.sums_stage[d, rows + 3 * layers : rows + 4 * layers, 0:lanes_f] = r.sums_f[
            0:layers, d * lanes_f : (d + 1) * lanes_f
        ]
    return [
        links.send(
            r.sums_stage.at[links.dp_peer(step)], r.land_s.at[step - 1], dp=links.dp_peer(step)
        )
        for step in range(1, links.n_dp)
    ]


def middle_sums(r, links, sent):
    rows = r.sums.shape[0]
    total = r.sums_stage[links.dp]
    for step, copy in enumerate(sent):
        copy.wait_recv()
        total = total + r.land_s[step]
    r.total_v[...] = total
    r.half[...] = total[0:rows]
    return [
        links.send(r.half, r.land_t.at[step - 1], tensor=links.tensor_peer(step))
        for step in range(1, links.n_tensor)
    ]


def end_sums(r, links, sent):
    rows = r.sums.shape[0]
    total = r.half[...]
    for step, copy in enumerate(sent):
        copy.wait_recv()
        total = total + r.land_t[step]
    r.total_v[0:rows, :] = total
    return links.local(r.total_v, r.total_out)


def token_rows(r, layer, which):
    block = r.cross[layer, which]
    return block.reshape(-1, block.shape[-1])


def normed_rows(r, links, layer, norm):
    layers = r.resid.shape[0]
    half = r.cross.shape[-1] // 2
    gain, bias = (
        jnp.concatenate(
            [
                r.vecs[row : row + 1, pl.ds(pl.multiple_of(d * half, half), half)]
                for d in (links.dp, links.over_x)
            ],
            axis=1,
        )
        for row in (2 * norm * layers + layer, (2 * norm + 1) * layers + layer)
    )
    unit = token_rows(r, layer, 0).astype(jnp.float32)
    return (unit * gain + bias).astype(jnp.bfloat16)


class Products:
    def __init__(self, r, links):
        self.r, self.links, self.stores = r, links, []

    def columns(self, ref, layer):
        block = ref[layer]
        return block.reshape(-1, block.shape[-1])

    def outputs(self, layer):
        r = self.r
        d_t = token_rows(r, layer, 1)
        return [
            Product(
                self.links, own.at[layer], away.at[layer], land.at[layer], d_t,
                self.columns(columns, layer),
            )
            for own, away, land, columns in (
                (r.go_own, r.go_away, r.go_land, r.ctx_all),
                (r.gp_own, r.gp_away, r.gp_land, r.act_all),
            )
        ]

    def hidden(self, layer):
        r = self.r
        return Product(
            self.links, r.gf_own.at[layer], r.gf_away.at[layer], r.gf_land.at[layer],
            normed_rows(r, self.links, layer, 1), self.columns(r.du_all, layer),
        )

    def heads(self, layer):
        r = self.r
        return Product(
            self.links, r.gq_own.at[layer], r.gq_away.at[layer], r.gq_land.at[layer],
            normed_rows(r, self.links, layer, 0), self.columns(r.dqkv_all, layer),
        )

    def store_outputs(self, layer, products):
        r = self.r
        for product, turned, out in zip(products, (r.go_v, r.gp_v), (r.w_out_g, r.w_proj_g)):
            turned[layer] = jnp.transpose(product.total())
            self.stores.append(self.links.local(turned.at[layer], out.at[layer]))

    def store(self, layer, product, out):
        product.own[...] = product.total()
        self.stores.append(self.links.local(product.own, out.at[layer]))


def layers_kernel(n_dp, n_tensor, names, *refs):
    r = types.SimpleNamespace(**dict(zip(names, refs)))
    links = Links(n_dp, n_tensor, r.send_sems, r.recv_sems, r.local_sems)
    bf16 = jnp.bfloat16
    layers = r.w_out.shape[0]
    last = layers - 1
    columns_ok = not hasattr(r, "wo_blocks")
    links.enter()
    x_load = links.local(r.x_in, r.resid.at[0])
    d_load = links.local(r.grad_out, r.dres.at[last])
    loads = [links.local(r.lens, r.lens_v)]
    for k, ref in enumerate((r.ln1_gain, r.ln1_bias, r.ln2_gain, r.ln2_bias, r.res_bias)):
        loads.append(links.local(ref, r.sv.at[k]))
    loads.append(links.local(r.b_qkv, r.sq))
    loads.append(links.local(r.b_fc, r.sf))

    qkv_g, fc_g, proj_g, fwd_g, du_g, dqkv_g = [], [], [], [], [], []
    for layer in range(layers):
        dp_width = r.w_qkv.shape[2]
        qkv_g.append(
            Group(DpGather(links, r.w_qkv.at[layer], middle_slot(r.wq.at[layer], dp_width), 1))
        )
        fc_g.append(Group(DpGather(links, r.w_fc.at[layer], row_slot(r.wf.at[layer], dp_width))))
        if columns_ok:
            slots = [column_slot(ref.at[layer], dp_width) for ref in (r.wo, r.wp)]
        else:
            slots = [lead_slot(ref.at[layer]) for ref in (r.wo_blocks, r.wp_blocks)]
        proj_g.append(
            Group(
                DpGather(links, r.w_out.at[layer], slots[0]),
                DpGather(links, r.w_proj.at[layer], slots[1]),
            )
        )
        rows = r.ctx.shape[1]
        ctx_j, act_j, dqkv_j, du_j = (
            PairGather(links, own.at[layer], lead_slot(whole.at[layer]))
            if links.paired
            else DpGather(links, own.at[layer], row_slot(whole.at[layer], rows))
            for own, whole in (
                (r.ctx, r.ctx_all),
                (r.act, r.act_all),
                (r.dqkv, r.dqkv_all),
                (r.du, r.du_all),
            )
        )
        fwd_g.append(Group(ctx_j, act_j))
        du_g.append(Group(du_j))
        dqkv_g.append(Group(dqkv_j))

    x_load.wait()
    unit = unit_rows(r.resid[0])[0].astype(bf16)
    unit_s = Spread(links, r.unit.at[0], unit)
    for load in loads:
        load.wait()
    pack_small(r, links)
    d_load.wait()
    d_bf = r.dres[last].astype(bf16)
    rows_s = Spread(links, r.drows.at[last], d_bf)
    crosses = [
        Cross(links, r.stage.at[0, 0], r.cross.at[0, 0], unit),
        Cross(links, r.stage.at[last, 1], r.cross.at[last, 1], d_bf),
    ]
    r.sums[...] = jnp.zeros_like(r.sums)
    layout_tables(r)
    links.barrier()

    vec_sent = [
        links.send(r.pack_v, r.land_v.at[step - 1], tensor=links.tensor_peer(step))
        for step in range(1, n_tensor)
    ]
    b_here = r.small_b.at[links.dp]
    small_sent = [
        links.send(r.pack_b, b_here, dp=links.dp_peer(step)) for step in range(1, n_dp)
    ]
    small_kept = links.local(r.pack_b, b_here)
    pump = Pump()
    for layer in range(layers):
        for group in (qkv_g[layer], fc_g[layer], proj_g[layer]):
            pump.add(group)
    unit_s.send()
    crosses[0].send()
    total = r.pack_v[...]
    for step, copy in enumerate(vec_sent):
        copy.wait_recv()
        total = total + r.land_v[step]
    r.vec_all[links.dp] = total
    vec_here = r.vec_all.at[links.dp]
    vec_wide = [
        links.send(vec_here, vec_here, dp=links.dp_peer(step)) for step in range(1, n_dp)
    ]
    rows_s.send()
    pump.relay()
    crosses[1].send()
    small_kept.wait()
    for copy in small_sent + vec_wide:
        copy.wait_recv()
    unpack_small(r, links)

    for layer in range(layers):
        pump.rest()
        qkv_g[layer].finish()
        if layer == 0:
            crosses[0].forward()
        else:
            pump.relay()
        unit_s.finish()
        forward_attention(r, layer)
        if layer == 0:
            pump.relay()
            crosses[1].forward()
        pump.rest()
        fc_g[layer].finish()
        forward_hidden(r, layer)
        if layer > 0:
            crosses[-1].forward()
        if not links.paired:
            pump.add(fwd_g[layer])
        pump.relay()
        if links.paired and layer == last:
            fwd_g[last].start()
        pump.rest()
        proj_g[layer].finish()
        if not columns_ok:
            in_columns(r, links, layer)
        forward_part(r, layer)
        scatter = Scatter(links, r.part_f.at[layer], r.land_f.at[layer])
        if layer < last:
            pump.relay()
            values = r.resid[layer] + scatter.total() + gain_rows(r, layer)[4]
            r.resid[layer + 1] = values
            unit = unit_rows(values)[0].astype(bf16)
            unit_s = Spread(links, r.unit.at[layer + 1], unit)
            unit_s.send()
            crosses.append(
                Cross(links, r.stage.at[layer + 1, 0], r.cross.at[layer + 1, 0], unit)
            )
            crosses[-1].send()

    sent_y = scatter
    if links.paired:
        finish = backward_paired
    else:
        finish = backward_gathered
    stores = finish(r, links, pump, fwd_g, du_g, dqkv_g, crosses, rows_s, sent_y)
    for store in stores:
        store.wait()
    links.finish()
    assert (links.used, links.used_local) == copy_counts(n_dp, n_tensor, layers)


def start_back(r, links, layer):
    backward_part(r, layer)
    scatter = Scatter(links, r.part_e.at[layer], r.land_e.at[layer])
    r.sums[5 * layer + 4 : 5 * layer + 5, :] = jnp.sum(r.dres[layer], axis=0, keepdims=True)
    return scatter


def step_back(r, links, layer, scatter, crosses):
    new_d = r.dres[layer] + back_unit(r.resid[layer], scatter.total())
    r.dres[layer - 1] = new_d
    d_bf = new_d.astype(jnp.bfloat16)
    rows_s = Spread(links, r.drows.at[layer - 1], d_bf)
    rows_s.send()
    crosses.append(Cross(links, r.stage.at[layer - 1, 1], r.cross.at[layer - 1, 1], d_bf))
    crosses[-1].send()
    return rows_s


def store_rows(r, links, sent_y, scatter):
    last = r.resid.shape[0] - 1
    r.y_v[...] = r.resid[last] + sent_y.total() + gain_rows(r, last)[4]
    stores = [links.local(r.y_v, r.y_out)]
    r.gx_v[...] = r.dres[0] + back_unit(r.resid[0], scatter.total())
    return stores + [links.local(r.gx_v, r.grad_x)]


def backward_paired(r, links, pump, fwd_g, du_g, dqkv_g, crosses, rows_s, sent_y):
    layers = r.resid.shape[0]
    last = layers - 1
    products = Products(r, links)
    done = []
    for layer in reversed(range(1, layers)):
        rows_s.finish()
        backward_hidden(r, layer)
        backward_attention(r, layer)
        du_g[layer].start()
        scatter = start_back(r, links, layer)
        fwd_g[layer].rest()
        dqkv_g[layer].start()
        if layer == last:
            for cross in crosses:
                cross.finish()
        fwd_g[layer].finish()
        outputs = products.outputs(layer)
        rows_s = step_back(r, links, layer, scatter, crosses)
        du_g[layer].rest()
        fwd_g[layer - 1].start()
        du_g[layer].finish()
        hidden = products.hidden(layer)
        dqkv_g[layer].rest()
        dqkv_g[layer].finish()
        done.append((layer, outputs, hidden, products.heads(layer)))
        crosses[-1].forward()
    rows_s.finish()
    backward_hidden(r, 0)
    du_g[0].start()
    backward_attention(r, 0)
    dqkv_g[0].start()
    scatter = start_back(r, links, 0)
    sums_sent = start_sums(r, links)
    fwd_g[0].rest()
    for layer, outputs, _, _ in done:
        products.store_outputs(layer, outputs)
    for cross in crosses[layers + 1 :]:
        cross.finish()
    fwd_g[0].finish()
    outputs = products.outputs(0)
    du_g[0].rest()
    du_g[0].finish()
    hidden = products.hidden(0)
    sums_wide = middle_sums(r, links, sums_sent)
    dqkv_g[0].rest()
    for layer, _, product, _ in done:
        products.store(layer, product, r.w_fc_g)
    dqkv_g[0].finish()
    heads = products.heads(0)
    stores = store_rows(r, links, sent_y, scatter)
    for layer, _, _, product in done:
        products.store(layer, product, r.w_qkv_g)
    stores.append(end_sums(r, links, sums_wide))
    products.store_outputs(0, outputs)
    products.store(0, hidden, r.w_fc_g)
    products.store(0, heads, r.w_qkv_g)
    return stores + products.stores


def backward_gathered(r, links, pump, fwd_g, du_g, dqkv_g, crosses, rows_s, sent_y):
    layers = r.resid.shape[0]
    last = layers - 1
    for layer in reversed(range(layers)):
        rows_s.finish()
        backward_hidden(r, layer)
        pump.add(du_g[layer])
        if layer == last:
            pump.relay()
        else:
            crosses[-1].forward()
        backward_attention(r, layer)
        pump.add(dqkv_g[layer])
        scatter = start_back(r, links, layer)
        if layer == 0:
            sums_sent = start_sums(r, links)
        pump.rest()
        pump.relay()
        if layer > 0:
            rows_s = step_back(r, links, layer, scatter, crosses)
            pump.rest()
            pump.relay()

    stores = store_rows(r, links, sent_y, scatter)
    stores.append(links.local(r.vecs, r.vecs_out))
    sums_wide = middle_sums(r, links, sums_sent)
    while pump.relayed or pump.started:
        if pump.relayed:
            pump.rest()
        if pump.started:
            pump.relay()
    stores.append(end_sums(r, links, sums_wide))
    for group in fwd_g + du_g + dqkv_g:
        group.finish()
    for cross in crosses:
        cross.finish()
    return stores


def places_kernel(names, *refs):
    r = types.SimpleNamespace(**dict(zip(names, refs)))
    tensor = lax.axis_index("tensor")
    count = [0]

    def local(src, dst):
        copy = pltpu.make_async_copy(src, dst, r.sems.at[count[0]])
        count[0] += 1
        copy.start()
        return copy

    load = local(r.total, r.total_v)
    moves = [
        (local(source, held), held, out)
        for source, held, out in (
            (r.qkv_in, r.qkv_v, r.w_qkv_g),
            (r.fc_in, r.fc_v, r.w_fc_g),
            (r.proj_in, r.proj_v, r.w_proj_g),
            (r.out_in, r.out_v, r.w_out_g),
            (r.y_in, r.y_v, r.y_out),
            (r.gx_in, r.gx_v, r.grad_x),
        )
    ]
    stores = []
    load.wait()
    layers, vec = r.g0.shape
    width = r.total.shape[1]
    rolled = pltpu.roll(r.total_v[...], lax.rem(width - tensor * vec, width), 1)
    for k, out in enumerate((r.g0, r.g1, r.g2, r.g3, r.g4)):
        for layer in range(layers):
            r.g_v[k, layer : layer + 1, :] = rolled[5 * layer + k : 5 * layer + k + 1, 0:vec]
        stores.append(local(r.g_v.at[k], out))
    rows = -(-5 * layers // 8) * 8
    for which in range(3):
        at = rows + which * layers
        r.bq_v[which] = r.total_v[at : at + layers, 0 : r.bq_v.shape[2]]
    at = rows + 3 * layers
    r.bf_v[...] = r.total_v[at : at + layers, 0 : r.bf_v.shape[1]]
    stores.append(local(r.bq_v, r.b_qkv_g))
    stores.append(local(r.bf_v, r.b_fc_g))
    for move, held, out in moves:
        move.wait()
        stores.append(local(held, out))
    for store in stores:
        store.wait()


def shaped(shape, dtype):
    return jax.ShapeDtypeStruct(tuple(shape), dtype)


def kernel_call(kernel, name, ins, outs, scratch, params):
    names = list(ins) + list(outs) + list(scratch)
    results = pl.pallas_call(
        functools.partial(kernel, names),
        out_shape=tuple(outs.values()),
        in_specs=[ANY] * len(ins),
        out_specs=(ANY,) * len(outs),
        scratch_shapes=list(scratch.values()),
        name=name,
        compiler_params=pltpu.CompilerParams(**params),
    )(*ins.values())
    return dict(zip(outs, results))


def per_device(
    x_in,
    seq_lengths,
    ln1_gain,
    ln1_bias,
    ln2_gain,
    ln2_bias,
    res_bias,
    w_qkv,
    b_qkv,
    w_out,
    w_fc,
    b_fc,
    w_proj,
    grad_out,
):
    n_tensor, n_dp = lax.axis_size("tensor"), lax.axis_size("dp")
    my_tensor, my_dp = lax.axis_index("tensor"), lax.axis_index("dp")
    bf16, f32 = jnp.bfloat16, jnp.float32
    my_rows, width = x_in.shape
    group_rows = my_rows * n_tensor
    total_rows = group_rows * n_dp
    layers = w_qkv.shape[0]
    part = w_qkv.shape[3]
    hidden = w_fc.shape[2]
    dp_width = width // n_dp
    vec = ln1_gain.shape[1]
    columns_ok = dp_width % 128 == 0
    vm = pltpu.VMEM
    pad8 = lambda n: -(-n // 8) * 8
    small_rows = pad8(4 * layers)
    vec_rows = pad8(5 * layers)
    n_remote, n_local = copy_counts(n_dp, n_tensor, layers)
    paired = n_dp == 8

    ins = dict(
        x_in=x_in,
        lens=seq_lengths,
        ln1_gain=ln1_gain,
        ln1_bias=ln1_bias,
        ln2_gain=ln2_gain,
        ln2_bias=ln2_bias,
        res_bias=res_bias,
        w_qkv=jnp.transpose(w_qkv, (0, 2, 1, 3)),
        b_qkv=jnp.transpose(b_qkv, (1, 0, 2)),
        w_out=w_out,
        w_fc=w_fc,
        b_fc=b_fc,
        w_proj=w_proj,
        grad_out=grad_out,
    )
    outs = dict(
        y_out=shaped(x_in.shape, f32),
        grad_x=shaped(x_in.shape, f32),
        total_out=shaped((vec_rows + small_rows, dp_width), f32),
    )
    gathered = dict(ctx_all=part, act_all=hidden, dqkv_all=3 * part, du_all=hidden)
    if paired:
        cross = (layers, 2, 4, n_tensor, my_rows, 2 * dp_width)
        outs |= dict(
            w_qkv_g=shaped(ins["w_qkv"].shape, f32),
            w_out_g=shaped(w_out.shape, f32),
            w_fc_g=shaped(w_fc.shape, f32),
            w_proj_g=shaped(w_proj.shape, f32),
        )
    else:
        cross = (layers, 2, n_dp, n_tensor, my_rows, dp_width)
        outs |= dict(vecs_out=shaped((vec_rows, width), f32), cross=shaped(cross, bf16))
        for name, size in gathered.items():
            outs[name] = shaped((layers, total_rows, size), bf16)
    rows_block = (layers, my_rows, width)
    group_block = (layers, group_rows, width)
    land = (layers, n_tensor - 1, my_rows, width)
    scratch = dict(
        resid=vm(rows_block, f32),
        dres=vm(rows_block, f32),
        lens_v=vm(seq_lengths.shape, jnp.int32),
        sv=vm((5,) + ln1_gain.shape, f32),
        sq=vm(ins["b_qkv"].shape, f32),
        sf=vm(b_fc.shape, f32),
        pack_v=vm((vec_rows, dp_width), f32),
        pack_b=vm((small_rows, 128), f32),
        land_v=vm((n_tensor - 1, vec_rows, dp_width), f32),
        vec_all=vm((n_dp, vec_rows, dp_width), f32),
        small_b=vm((n_dp, small_rows, 128), f32),
        vecs=vm((vec_rows, width), f32),
        bq=vm((pad8(3 * layers), part), f32),
        bf=vm((pad8(layers), hidden), f32),
        same=vm((group_rows, part), f32),
        up=vm((group_rows, part), f32),
        down=vm((group_rows, part), f32),
        mask=vm((group_rows, group_rows), f32),
        wq=vm((layers, 3, width, part), bf16),
        wf=vm((layers, width, hidden), bf16),
        wo=vm((layers, part, width), bf16),
        wp=vm((layers, hidden, width), bf16),
        unit=vm(group_block, bf16),
        drows=vm(group_block, bf16),
        qkv=vm((layers, group_rows, 3 * part), bf16),
        ctx=vm((layers, group_rows, part), bf16),
        pre=vm((layers, group_rows, hidden), f32),
        act=vm((layers, group_rows, hidden), bf16),
        dctx=vm((group_rows, part), bf16),
        du=vm((layers, group_rows, hidden), bf16),
        dqkv=vm((layers, group_rows, 3 * part), bf16),
        part_f=vm(group_block, bf16),
        part_e=vm(group_block, bf16),
        land_f=vm(land, bf16),
        land_e=vm(land, bf16),
        stage=vm(cross[:3] + cross[4:], bf16),
        sums=vm((vec_rows, width), f32),
        sums_q=vm((pad8(3 * layers), part), f32),
        sums_f=vm((pad8(layers), hidden), f32),
        sums_stage=vm((n_dp, vec_rows + small_rows, dp_width), f32),
        land_s=vm((n_dp - 1, vec_rows + small_rows, dp_width), f32),
        half=vm((vec_rows, dp_width), f32),
        land_t=vm((n_tensor - 1, vec_rows, dp_width), f32),
        total_v=vm((vec_rows + small_rows, dp_width), f32),
        y_v=vm((my_rows, width), f32),
        gx_v=vm((my_rows, width), f32),
        send_sems=pltpu.SemaphoreType.DMA((n_remote,)),
        recv_sems=pltpu.SemaphoreType.DMA((n_remote,)),
        local_sems=pltpu.SemaphoreType.DMA((n_local,)),
    )
    if not columns_ok:
        scratch["wo_blocks"] = vm((layers, n_dp, part, dp_width), bf16)
        scratch["wp_blocks"] = vm((layers, n_dp, hidden, dp_width), bf16)
    if paired:
        scratch["cross"] = vm(cross, bf16)
        for name, size in gathered.items():
            scratch[name] = vm((layers, 4, group_rows, size), bf16)
        halves = dict(
            gq=ins["w_qkv"].shape,
            go=(layers, dp_width, part),
            gf=(layers, dp_width, hidden),
            gp=(layers, dp_width, hidden),
        )
        for name, shape in halves.items():
            scratch[name + "_own"] = vm(shape, f32)
            scratch[name + "_away"] = vm(shape, bf16)
            scratch[name + "_land"] = vm(shape, bf16)
        scratch |= dict(go_v=vm(w_out.shape, f32), gp_v=vm(w_proj.shape, f32))
    step = kernel_call(
        functools.partial(layers_kernel, n_dp, n_tensor),
        "layers",
        ins,
        outs,
        scratch,
        {"collective_id": 0, "has_side_effects": True, "vmem_limit_bytes": 58 << 20},
    )

    if paired:
        vectors = {f"g{k}": shaped(ln1_gain.shape, f32) for k in range(5)}
        done = kernel_call(
            places_kernel,
            "places",
            dict(
                y_in=step["y_out"],
                gx_in=step["grad_x"],
                total=step["total_out"],
                qkv_in=step["w_qkv_g"],
                out_in=step["w_out_g"],
                fc_in=step["w_fc_g"],
                proj_in=step["w_proj_g"],
            ),
            dict(
                y_out=shaped(x_in.shape, f32),
                grad_x=shaped(x_in.shape, f32),
                w_qkv_g=shaped(ins["w_qkv"].shape, f32),
                b_qkv_g=shaped(ins["b_qkv"].shape, f32),
                w_out_g=shaped(w_out.shape, f32),
                w_fc_g=shaped(w_fc.shape, f32),
                b_fc_g=shaped(b_fc.shape, f32),
                w_proj_g=shaped(w_proj.shape, f32),
                **vectors,
            ),
            dict(
                total_v=vm(step["total_out"].shape, f32),
                g_v=vm((5, layers, vec), f32),
                bq_v=vm(ins["b_qkv"].shape, f32),
                bf_v=vm(b_fc.shape, f32),
                qkv_v=vm(ins["w_qkv"].shape, f32),
                fc_v=vm(w_fc.shape, f32),
                proj_v=vm(w_proj.shape, f32),
                out_v=vm(w_out.shape, f32),
                y_v=vm(x_in.shape, f32),
                gx_v=vm(x_in.shape, f32),
                sems=pltpu.SemaphoreType.DMA((20,)),
            ),
            {"vmem_limit_bytes": 58 << 20},
        )
        return (
            (done["y_out"], done["grad_x"])
            + tuple(done[name] for name in vectors)
            + (
                jnp.transpose(done["w_qkv_g"], (0, 2, 1, 3)),
                jnp.transpose(done["b_qkv_g"], (1, 0, 2)),
            )
            + tuple(done[name] for name in ("w_out_g", "w_fc_g", "b_fc_g", "w_proj_g"))
        )

    over_tokens = (((0,), (0,)), ((), ()))
    grads = [[] for _ in range(6)]
    small = step["total_out"][vec_rows:]
    vectors = step["vecs_out"][: 5 * layers].reshape(5, layers, width)
    vectors = lax.dynamic_slice_in_dim(vectors, my_dp * dp_width, dp_width, axis=2)
    for layer in range(layers):
        context_t, act_t, dqkv_t, d_pre_t = (
            step[name][layer] for name in ("ctx_all", "act_all", "dqkv_all", "du_all")
        )
        unit_t = step["cross"][layer, 0].reshape(total_rows, dp_width).astype(f32)
        d_t = step["cross"][layer, 1].reshape(total_rows, dp_width)
        a_t = (unit_t * vectors[0, layer] + vectors[1, layer]).astype(bf16)
        m_t = (unit_t * vectors[2, layer] + vectors[3, layer]).astype(bf16)

        def contract(left, right):
            return lax.dot_general(left, right, over_tokens, preferred_element_type=f32)

        grads[0].append(contract(a_t, dqkv_t).reshape(w_qkv.shape[1:]))
        grads[1].append(small[layer : 3 * layers : layers, : b_qkv.shape[2]])
        grads[2].append(contract(context_t, d_t))
        grads[3].append(contract(m_t, d_pre_t))
        grads[4].append(small[3 * layers + layer, : b_fc.shape[1]])
        grads[5].append(contract(act_t, d_t))
    vector_grads = lax.dynamic_slice_in_dim(
        step["total_out"][: 5 * layers].reshape(layers, 5, dp_width), my_tensor * vec, vec, axis=2
    )
    return (
        (step["y_out"], step["grad_x"])
        + tuple(vector_grads[:, k] for k in range(5))
        + tuple(jnp.stack(group) for group in grads)
    )


def solution(mesh):
    in_specs = (
        P(("dp", "tensor"), None),
        P("dp", None),
        P(None, ("dp", "tensor")),
        P(None, ("dp", "tensor")),
        P(None, ("dp", "tensor")),
        P(None, ("dp", "tensor")),
        P(None, ("dp", "tensor")),
        P(None, "dp", None, "tensor"),
        P(None, None, ("tensor", "dp")),
        P(None, "tensor", "dp"),
        P(None, "dp", "tensor"),
        P(None, ("tensor", "dp")),
        P(None, "tensor", "dp"),
        P(("dp", "tensor"), None),
    )
    out_specs = (
        P(("dp", "tensor"), None),
        P(("dp", "tensor"), None),
        P(None, ("dp", "tensor")),
        P(None, ("dp", "tensor")),
        P(None, ("dp", "tensor")),
        P(None, ("dp", "tensor")),
        P(None, ("dp", "tensor")),
        P(None, "dp", None, "tensor"),
        P(None, None, ("tensor", "dp")),
        P(None, "tensor", "dp"),
        P(None, "dp", "tensor"),
        P(None, ("tensor", "dp")),
        P(None, "tensor", "dp"),
    )
    return jax.shard_map(
        per_device, mesh=mesh, in_specs=in_specs, out_specs=out_specs, check_vma=False
    )
```

```python
import functools
import types

import jax
import jax.numpy as jnp
from jax import lax
from jax.experimental import pallas as pl
from jax.experimental.pallas import tpu as pltpu
from jax.sharding import PartitionSpec as P

HD = 64
ROT = 16


EPS = 1e-05
NEG_FILL = -1e30


def gelu_exact(values):
    return 0.5 * values * (1.0 + jax.scipy.special.erf(values * 0.7071067811865476))


def gelu_slope(values):
    normal_cdf = 0.5 * (1.0 + jax.scipy.special.erf(values * 0.7071067811865476))
    return normal_cdf + values * jnp.exp(-0.5 * values * values) * 0.3989422804014327


MESH = pl.DeviceIdType.MESH
ANY = pl.BlockSpec(memory_space=pl.ANY)
VMEM = pl.BlockSpec(memory_space=pltpu.VMEM)


def copy_counts(n_dp, n_tensor, layers):
    chips = n_dp // 2
    remote = (n_tensor - 1) * (6 * layers + 2) + (n_dp - 1) * 3
    if chips == 4:
        return remote + layers * (4 * 13 + 4 * 3 + 2 * 3 + 4), 14 * layers + 14
    return remote + layers * (8 * (4 * chips - 3) + 2 * (n_dp - 1)), 10 * layers + 15


class Links:
    def __init__(self, n_dp, n_tensor, send_sems, recv_sems, local_sems):
        self.n_dp, self.n_tensor = n_dp, n_tensor
        self.dp, self.tensor = lax.axis_index("dp"), lax.axis_index("tensor")
        self.core, self.chip = lax.rem(self.dp, 2), self.dp // 2
        self.partner = self.dp + 1 - 2 * self.core
        self.paired = n_dp == 8
        if self.paired:
            self.gather_y, self.gather_x = Turn(self, False), Turn(self, True)
        self.send_sems, self.recv_sems, self.local_sems = send_sems, recv_sems, local_sems
        self.used, self.used_local = 0, 0
        self.sent = []

    def send(self, src, dst, **where):
        copy = pltpu.make_async_remote_copy(
            src_ref=src,
            dst_ref=dst,
            send_sem=self.send_sems.at[self.used],
            recv_sem=self.recv_sems.at[self.used],
            device_id=where,
            device_id_type=MESH,
        )
        self.used += 1
        copy.start()
        self.sent.append(copy)
        return copy

    def local(self, src, dst):
        copy = pltpu.make_async_copy(src, dst, self.local_sems.at[self.used_local])
        self.used_local += 1
        copy.start()
        return copy

    def dp_peer(self, step):
        return lax.rem(self.dp + step, self.n_dp)

    def tensor_peer(self, step):
        return lax.rem(self.tensor + step, self.n_tensor)

    def enter(self):
        sem = pltpu.get_barrier_semaphore()
        for step in range(1, self.n_tensor):
            pl.semaphore_signal(
                sem, inc=1, device_id={"tensor": self.tensor_peer(step)}, device_id_type=MESH
            )
        for step in range(1, self.n_dp):
            pl.semaphore_signal(
                sem, inc=1, device_id={"dp": self.dp_peer(step)}, device_id_type=MESH
            )

    def barrier(self):
        pl.semaphore_wait(pltpu.get_barrier_semaphore(), self.n_tensor + self.n_dp - 2)

    def finish(self):
        for copy in self.sent:
            copy.wait_send()


class Turn:
    def __init__(self, links, gather_x):
        x, y = lax.rem(links.chip, 2), links.chip // 2
        over = (links.dp + 2 - 4 * x, lax.rem(links.dp + 4, 8))
        self.gather_x = gather_x
        self.gather_dp, self.sum_dp = over if gather_x else over[::-1]
        self.along, self.apart = (x, y) if gather_x else (y, x)
        self.place = self.along * 2 + links.core
        self.far_place = lax.rem(self.place + 2, 4)

    def block(self, place, apart):
        if self.gather_x:
            return apart * 4 + place
        return place // 2 * 4 + 2 * apart + lax.rem(place, 2)


class DpGather:
    def __init__(self, links, own, slot, axis=0):
        self.links, self.own, self.slot = links, own, slot
        self.chips = links.n_dp // 2
        self.core, self.chip, self.partner = links.core, links.chip, links.partner
        self.relays = self.chips == 4
        rows = own.shape[axis] // 2
        self.halves = [
            (slice(None),) * axis + (pl.ds(half * rows, rows),) for half in range(2)
        ]
        self.passed = []
        if self.relays:
            near = self.chip + 1 - 2 * lax.rem(self.chip, 2)
            far = lax.rem(self.chip + 2, 4)
            self.across = lax.rem(near + 2, 4)
            self.order = ((near, far), (far, near))

    def device(self, chip):
        return chip * 2 + self.core

    def out(self, rows, chip):
        return self.links.send(
            self.own.at[rows], self.slot(self.links.dp).at[rows], dp=self.device(chip)
        )

    def pass_on(self, rows, chip, target):
        block = self.slot(self.device(chip)).at[rows]
        return self.links.send(block, block, dp=target)

    def start(self):
        if self.relays:
            self.first = [self.out(rows, order[0]) for rows, order in zip(self.halves, self.order)]
            self.second = [self.out(rows, order[1]) for rows, order in zip(self.halves, self.order)]
        else:
            self.direct = [
                [self.out(rows, lax.rem(self.chip + step, self.chips)) for rows in self.halves]
                for step in range(1, self.chips)
            ]
        own_slot = self.slot(self.links.dp)
        self.passed.append(self.links.send(self.own, own_slot, dp=self.partner))
        self.kept = self.links.local(self.own, own_slot)

    def relay(self):
        if not self.relays:
            return
        self.relayed = []
        for copy, rows, order in zip(self.first, self.halves, self.order):
            copy.wait_recv()
            self.relayed.append(self.pass_on(rows, order[0], self.device(order[1])))
            self.passed.append(self.pass_on(rows, order[0], self.partner))

    def rest(self):
        if not self.relays:
            for step, copies in enumerate(self.direct):
                origin = lax.rem(self.chip + self.chips - step - 1, self.chips)
                for copy, rows in zip(copies, self.halves):
                    copy.wait_recv()
                    self.passed.append(self.pass_on(rows, origin, self.partner))
            return
        for copy, rows, order in zip(self.second, self.halves, self.order):
            copy.wait_recv()
            self.passed.append(self.pass_on(rows, order[1], self.partner))
        for copy, rows in zip(self.relayed, self.halves):
            copy.wait_recv()
            self.passed.append(self.pass_on(rows, self.across, self.partner))

    def finish(self):
        for copy in self.passed:
            copy.wait_recv()
        self.kept.wait()


class PairGather:
    def __init__(self, links, turn, own, slot):
        self.links, self.turn, self.own, self.slot = links, turn, own, slot

    def start(self):
        links, here = self.links, self.slot(self.turn.place)
        self.out = links.send(self.own, here, dp=self.turn.gather_dp)
        self.passed = [links.send(self.own, here, dp=links.partner)]
        self.kept = links.local(self.own, here)

    def rest(self):
        self.out.wait_recv()
        block = self.slot(self.turn.far_place)
        self.passed.append(self.links.send(block, block, dp=self.links.partner))

    def finish(self):
        for copy in self.passed:
            copy.wait_recv()
        self.kept.wait()


class Group:
    def __init__(self, *gathers):
        self.gathers = gathers

    def start(self):
        for gather in self.gathers:
            gather.start()

    def relay(self):
        for gather in self.gathers:
            gather.relay()

    def rest(self):
        for gather in self.gathers:
            gather.rest()

    def finish(self):
        for gather in self.gathers:
            gather.finish()


class Pump:
    def __init__(self):
        self.todo, self.started, self.relayed, self.every = [], [], [], []

    def add(self, group):
        self.todo.append(group)
        self.every.append(group)
        if not self.started:
            self.start()

    def start(self):
        if self.todo:
            group = self.todo.pop(0)
            group.start()
            self.started.append(group)

    def relay(self):
        group = self.started.pop(0)
        group.relay()
        self.relayed.append(group)
        if not self.started:
            self.start()

    def rest(self):
        self.relayed.pop(0).rest()


def row_slot(ref, rows):
    return lambda d: ref.at[pl.ds(pl.multiple_of(d * rows, rows), rows)]


def middle_slot(ref, rows):
    return lambda d: ref.at[:, pl.ds(pl.multiple_of(d * rows, rows), rows)]


def column_slot(ref, size):
    return lambda d: ref.at[:, pl.ds(pl.multiple_of(d * size, size), size)]


def lead_slot(ref):
    return lambda d: ref.at[d]


class Scatter:
    def __init__(self, links, part, landing):
        self.links, self.part, self.landing = links, part, landing
        self.rows = landing.shape[1]
        slot = row_slot(part, self.rows)
        self.copies = [
            links.send(
                slot(links.tensor_peer(step)),
                landing.at[step - 1],
                tensor=links.tensor_peer(step),
            )
            for step in range(1, links.n_tensor)
        ]

    def total(self):
        own = pl.ds(pl.multiple_of(self.links.tensor * self.rows, self.rows), self.rows)
        total = self.part[own, :].astype(jnp.float32)
        for step, copy in enumerate(self.copies):
            copy.wait_recv()
            total = total + self.landing[step].astype(jnp.float32)
        return total


class Spread:
    def __init__(self, links, ref, value):
        rows = value.shape[0]
        self.links, self.here = links, row_slot(ref, rows)(links.tensor)
        ref[pl.ds(pl.multiple_of(links.tensor * rows, rows), rows), :] = value

    def send(self):
        links = self.links
        self.copies = [
            links.send(self.here, self.here, tensor=links.tensor_peer(step))
            for step in range(1, links.n_tensor)
        ]

    def finish(self):
        for copy in self.copies:
            copy.wait_recv()


class Cross:
    def __init__(self, links, turn, stage, out, value):
        self.links, self.turn, self.stage, self.out = links, turn, stage, out
        self.count, _, width = stage.shape
        self.me = turn.place if links.paired else links.dp
        if not links.paired:
            for d in range(self.count):
                stage[d] = value[:, d * width : (d + 1) * width]
            return
        half = width // 2
        wide = value.astype(jnp.float32)
        for s in range(self.count):
            at = [
                (apart * 4 + s if turn.gather_x else s // 2 * 4 + 2 * apart + s % 2) * half
                for apart in range(2)
            ]
            one, two = (wide[:, place : place + half] for place in at)
            stage[s, :, 0:half] = jnp.where(turn.apart == 0, one, two).astype(value.dtype)
            stage[s, :, half:width] = jnp.where(turn.apart == 0, two, one).astype(value.dtype)

    def send(self):
        links, stage = self.links, self.stage
        here = self.out.at[self.me, links.tensor]
        self.copies = []
        for step in range(1, self.count):
            peer = lax.rem(self.me + step, self.count)
            device = self.turn.block(peer, self.turn.apart) if links.paired else peer
            self.copies.append(links.send(stage.at[peer], here, dp=device))
        self.kept = links.local(stage.at[self.me], here)

    def forward(self):
        links = self.links
        for copy in self.copies:
            copy.wait_recv()
        self.kept.wait()
        mine = self.out.at[:, links.tensor]
        self.wide = [
            links.send(mine, mine, tensor=links.tensor_peer(step))
            for step in range(1, links.n_tensor)
        ]

    def finish(self):
        for copy in self.wide:
            copy.wait_recv()


class Product:
    def __init__(self, links, turn, own, away, landing, rows, columns):
        self.own, self.landing = own, landing
        parts = own.shape[0] if len(own.shape) == 3 else 1
        half, width = own.shape[-2:]
        for k in range(parts):
            total = dot_tn(rows, columns[:, k * width : (k + 1) * width])
            if len(own.shape) == 3:
                own[k] = total[:half]
                away[k] = total[half:].astype(away.dtype)
            else:
                own[...] = total[:half]
                away[...] = total[half:].astype(away.dtype)
        self.copy = links.send(away, landing, dp=turn.sum_dp)

    def total(self):
        self.copy.wait_recv()
        return self.own[...] + self.landing[...].astype(jnp.float32)


def unit_rows(values):
    average = jnp.mean(values, axis=-1, keepdims=True)
    centred = values - average
    variance = jnp.mean(centred * centred, axis=-1, keepdims=True)
    scale = lax.rsqrt(variance + EPS)
    return centred * scale, scale


def back_unit(values, grad):
    unit, scale = unit_rows(values)
    return scale * (
        grad
        - jnp.mean(grad, axis=-1, keepdims=True)
        - unit * jnp.mean(grad * unit, axis=-1, keepdims=True)
    )


def dot_nn(left, right):
    return jnp.dot(left, right, preferred_element_type=jnp.float32)


def dot_nt(left, right):
    return lax.dot_general(left, right, (((1,), (1,)), ((), ())), preferred_element_type=jnp.float32)


def dot_tn(left, right):
    return lax.dot_general(left, right, (((0,), (0,)), ((), ())), preferred_element_type=jnp.float32)


def turn(vectors, same, up, down, sign):
    width = vectors.shape[1]
    above = pltpu.roll(vectors, width - ROT // 2, 1)
    below = pltpu.roll(vectors, ROT // 2, 1)
    return vectors * same + sign * (above * up + below * down)


def head_scores(query, key, mask):
    scores = dot_nt(query, key) * HD ** (-0.5)
    scores = jnp.where(mask, scores, NEG_FILL)
    terms = jnp.exp(scores - jnp.max(scores, axis=-1, keepdims=True))
    return terms / jnp.sum(terms, axis=-1, keepdims=True)


def layout_tables(r):
    f32 = jnp.float32
    rows, width = r.same.shape
    lengths = r.lens_v[...]
    row_of = lax.broadcasted_iota(jnp.int32, (rows, rows), 0)
    col_of = lax.broadcasted_iota(jnp.int32, (rows, rows), 1)
    row_lane = lax.broadcasted_iota(jnp.int32, (rows, 128), 0)
    start = jnp.zeros((rows, rows), jnp.int32)
    start_lane = jnp.zeros((rows, 128), jnp.int32)
    end = jnp.zeros((1, 1), jnp.int32)
    for k in range(lengths.shape[1]):
        end = end + lengths[:, k : k + 1]
        start = jnp.where(row_of >= end, end, start)
        start_lane = jnp.where(row_lane >= end, end, start_lane)
    r.mask[...] = jnp.where((col_of >= start) & (col_of <= row_of), 1.0, 0.0)
    positions = (row_lane - start_lane).astype(f32)
    lane = lax.rem(lax.broadcasted_iota(jnp.int32, (1, 128), 1), HD)
    half = ROT // 2
    inverse = jnp.power(10000.0, -2.0 * lax.rem(lane, half).astype(f32) / ROT)
    angles = positions * inverse
    cos_tab, sin_tab = jnp.cos(angles), jnp.sin(angles)
    same = jnp.where(lane < ROT, cos_tab, 1.0)
    up = jnp.where(lane < half, -sin_tab, 0.0)
    down = jnp.where((lane >= half) & (lane < ROT), sin_tab, 0.0)
    for ref, table in ((r.same, same), (r.up, up), (r.down, down)):
        for place in range(width // 128):
            ref[:, place * 128 : (place + 1) * 128] = table


def gain_rows(r, layer):
    layers = r.resid.shape[0]
    return tuple(r.vecs[k * layers + layer : k * layers + layer + 1, :] for k in range(5))


def forward_attention(r, layer):
    bf16 = jnp.bfloat16
    g1, b1, _, _, _ = gain_rows(r, layer)
    layers, _, part = r.ctx.shape
    normed_a = (r.unit[layer].astype(jnp.float32) * g1 + b1).astype(bf16)
    tables = (r.same[...], r.up[...], r.down[...])
    for which in range(3):
        row = which * layers + layer
        block = dot_nn(normed_a, r.wq[layer, which]) + r.bq[row : row + 1, :]
        if which < 2:
            block = turn(block, *tables, 1.0)
        r.qkv[layer, :, which * part : (which + 1) * part] = block.astype(bf16)
    allowed = r.mask[...] > 0.0
    for head in range(part // HD):
        q, k, v = (
            r.qkv[layer, :, which * part + head * HD : which * part + (head + 1) * HD]
            for which in range(3)
        )
        probs = head_scores(q, k, allowed).astype(bf16)
        r.ctx[layer, :, head * HD : (head + 1) * HD] = dot_nn(probs, v).astype(bf16)


def forward_hidden(r, layer):
    bf16 = jnp.bfloat16
    _, _, g2, b2, _ = gain_rows(r, layer)
    normed_m = (r.unit[layer].astype(jnp.float32) * g2 + b2).astype(bf16)
    hidden = dot_nn(normed_m, r.wf[layer]) + r.bf[layer : layer + 1, :]
    r.pre[layer] = hidden
    r.act[layer] = gelu_exact(hidden).astype(bf16)


def forward_part(r, layer):
    r.part_f[layer] = (
        dot_nn(r.ctx[layer], r.wo[layer]) + dot_nn(r.act[layer], r.wp[layer])
    ).astype(jnp.bfloat16)


def backward_hidden(r, layer):
    bf16 = jnp.bfloat16
    r.dctx[...] = dot_nt(r.drows[layer], r.wo[layer]).astype(bf16)
    d_pre = dot_nt(r.drows[layer], r.wp[layer]) * gelu_slope(r.pre[layer])
    r.sums_f[layer : layer + 1, :] = jnp.sum(d_pre, axis=0, keepdims=True)
    r.du[layer] = d_pre.astype(bf16)


def backward_attention(r, layer):
    bf16, f32 = jnp.bfloat16, jnp.float32
    part = r.ctx.shape[2]
    allowed = r.mask[...] > 0.0
    pieces = [[], [], []]
    for head in range(part // HD):
        here = slice(head * HD, (head + 1) * HD)
        q, k, v = (
            r.qkv[layer, :, which * part + head * HD : which * part + (head + 1) * HD]
            for which in range(3)
        )
        dc = r.dctx[:, here]
        probs = head_scores(q, k, allowed)
        delta = jnp.sum(
            dc.astype(f32) * r.ctx[layer, :, here].astype(f32), axis=-1, keepdims=True
        )
        d_scaled = (probs * (dot_nt(dc, v) - delta) * HD ** (-0.5)).astype(bf16)
        pieces[0].append(dot_nn(d_scaled, k))
        pieces[1].append(dot_tn(d_scaled, q))
        pieces[2].append(dot_tn(probs.astype(bf16), dc))
    tables = (r.same[...], r.up[...], r.down[...])
    for which in range(3):
        block = jnp.concatenate(pieces[which], axis=1)
        if which < 2:
            block = turn(block, *tables, -1.0)
        row = which * r.ctx.shape[0] + layer
        r.sums_q[row : row + 1, :] = jnp.sum(block, axis=0, keepdims=True)
        r.dqkv[layer, :, which * part : (which + 1) * part] = block.astype(bf16)


def backward_part(r, layer):
    g1, _, g2, _, _ = gain_rows(r, layer)
    part = r.ctx.shape[2]
    d_a = sum(
        dot_nt(r.dqkv[layer, :, which * part : (which + 1) * part], r.wq[layer, which])
        for which in range(3)
    )
    d_m = dot_nt(r.du[layer], r.wf[layer])
    r.part_e[layer] = (d_a * g1 + d_m * g2).astype(jnp.bfloat16)
    wide = r.unit[layer].astype(jnp.float32)
    for row, term in enumerate((d_a * wide, d_a, d_m * wide, d_m)):
        r.sums[5 * layer + row : 5 * layer + row + 1, :] = jnp.sum(term, axis=0, keepdims=True)


def pack_small(r, links):
    count, layers, vec = r.sv.shape
    r.pack_v[...] = jnp.zeros_like(r.pack_v)
    owner = lax.broadcasted_iota(jnp.int32, (layers, vec * links.n_tensor), 1) // vec
    for k in range(count):
        value = jnp.concatenate([r.sv[k]] * links.n_tensor, axis=1)
        r.pack_v[k * layers : (k + 1) * layers, :] = jnp.where(owner == links.tensor, value, 0.0)
    r.pack_b[...] = jnp.zeros_like(r.pack_b)
    for which in range(3):
        r.pack_b[which * layers : (which + 1) * layers, 0 : r.sq.shape[2]] = r.sq[which]
    r.pack_b[3 * layers : 4 * layers, 0 : r.sf.shape[1]] = r.sf[...]


def unpack_small(r, links):
    layers = r.sf.shape[0]
    width = r.vec_all.shape[2]
    rows = 0
    for d in range(links.n_dp):
        r.vecs[:, d * width : (d + 1) * width] = r.vec_all[d]
    for ref, height, lanes in ((r.bq, 3 * layers, r.sq.shape[2]), (r.bf, layers, r.sf.shape[1])):
        ref[0:height, :] = jnp.concatenate(
            [r.small_b[d, rows : rows + height, 0:lanes] for d in range(links.n_dp)], axis=1
        )
        rows = rows + height


def in_columns(r, links, layer):
    for blocks, whole in ((r.wo_blocks, r.wo), (r.wp_blocks, r.wp)):
        width = blocks.shape[3]
        for d in range(links.n_dp):
            whole[layer, :, d * width : (d + 1) * width] = blocks[layer, d]


def start_sums(r, links):
    layers = r.resid.shape[0]
    width = r.sums_stage.shape[2]
    rows = r.sums.shape[0]
    lanes_q, lanes_f = r.sq.shape[2], r.sf.shape[1]
    r.sums_stage[...] = jnp.zeros_like(r.sums_stage)
    for d in range(links.n_dp):
        r.sums_stage[d, 0:rows, :] = r.sums[:, d * width : (d + 1) * width]
        r.sums_stage[d, rows : rows + 3 * layers, 0:lanes_q] = r.sums_q[
            0 : 3 * layers, d * lanes_q : (d + 1) * lanes_q
        ]
        r.sums_stage[d, rows + 3 * layers : rows + 4 * layers, 0:lanes_f] = r.sums_f[
            0:layers, d * lanes_f : (d + 1) * lanes_f
        ]
    return [
        links.send(
            r.sums_stage.at[links.dp_peer(step)], r.land_s.at[step - 1], dp=links.dp_peer(step)
        )
        for step in range(1, links.n_dp)
    ]


def middle_sums(r, links, sent):
    rows = r.sums.shape[0]
    total = r.sums_stage[links.dp]
    for step, copy in enumerate(sent):
        copy.wait_recv()
        total = total + r.land_s[step]
    r.total_v[...] = total
    r.half[...] = total[0:rows]
    return [
        links.send(r.half, r.land_t.at[step - 1], tensor=links.tensor_peer(step))
        for step in range(1, links.n_tensor)
    ]


def end_sums(r, links, sent):
    rows = r.sums.shape[0]
    total = r.half[...]
    for step, copy in enumerate(sent):
        copy.wait_recv()
        total = total + r.land_t[step]
    r.total_v[0:rows, :] = total
    return links.local(r.total_v, r.total_out)


def token_rows(r, layer, which):
    block = r.cross[layer, which]
    return block.reshape(-1, block.shape[-1])


def product_turn(links, layer, which):
    if not links.paired:
        return None
    return links.gather_y if (layer, which) == (0, 1) else links.gather_x


def normed_rows(r, links, layer, norm):
    layers = r.resid.shape[0]
    half = r.cross.shape[-1] // 2
    gain, bias = (
        jnp.concatenate(
            [
                r.vecs[row : row + 1, pl.ds(pl.multiple_of(d * half, half), half)]
                for d in (links.dp, product_turn(links, layer, 0).sum_dp)
            ],
            axis=1,
        )
        for row in (2 * norm * layers + layer, (2 * norm + 1) * layers + layer)
    )
    unit = token_rows(r, layer, 0).astype(jnp.float32)
    return (unit * gain + bias).astype(jnp.bfloat16)


class Products:
    def __init__(self, r, links):
        self.r, self.links, self.stores = r, links, []

    def columns(self, ref, layer):
        block = ref[layer]
        return block.reshape(-1, block.shape[-1])

    def outputs(self, layer):
        r = self.r
        d_t = token_rows(r, layer, 1)
        return [
            Product(
                self.links, product_turn(self.links, layer, 1), own.at[layer], away.at[layer], land.at[layer], d_t,
                self.columns(columns, layer),
            )
            for own, away, land, columns in (
                (r.go_own, r.go_away, r.go_land, r.ctx_all),
                (r.gp_own, r.gp_away, r.gp_land, r.act_all),
            )
        ]

    def hidden(self, layer):
        r = self.r
        return Product(
            self.links, product_turn(self.links, layer, 0), r.gf_own.at[layer], r.gf_away.at[layer], r.gf_land.at[layer],
            normed_rows(r, self.links, layer, 1), self.columns(r.du_all, layer),
        )

    def heads(self, layer):
        r = self.r
        return Product(
            self.links, product_turn(self.links, layer, 0), r.gq_own.at[layer], r.gq_away.at[layer], r.gq_land.at[layer],
            normed_rows(r, self.links, layer, 0), self.columns(r.dqkv_all, layer),
        )

    def store_outputs(self, layer, products):
        r = self.r
        for product, turned, out in zip(products, (r.go_v, r.gp_v), (r.w_out_g, r.w_proj_g)):
            turned[layer] = jnp.transpose(product.total())
            self.stores.append(self.links.local(turned.at[layer], out.at[layer]))

    def store(self, layer, product, out):
        product.own[...] = product.total()
        self.stores.append(self.links.local(product.own, out.at[layer]))


def make_cross(r, links, layer, which, value):
    turn = product_turn(links, layer, which)
    return Cross(links, turn, r.stage.at[layer, which], r.cross.at[layer, which], value)


def layers_kernel(n_dp, n_tensor, names, *refs):
    r = types.SimpleNamespace(**dict(zip(names, refs)))
    links = Links(n_dp, n_tensor, r.send_sems, r.recv_sems, r.local_sems)
    bf16 = jnp.bfloat16
    layers = r.w_out.shape[0]
    last = layers - 1
    columns_ok = not hasattr(r, "wo_blocks")
    links.enter()
    x_load = links.local(r.x_in, r.resid.at[0])
    d_load = links.local(r.grad_out, r.dres.at[last])
    loads = [links.local(r.lens, r.lens_v)]
    for k, ref in enumerate((r.ln1_gain, r.ln1_bias, r.ln2_gain, r.ln2_bias, r.res_bias)):
        loads.append(links.local(ref, r.sv.at[k]))
    loads.append(links.local(r.b_qkv, r.sq))
    loads.append(links.local(r.b_fc, r.sf))

    qkv_g, fc_g, proj_g, fwd_g, du_g, dqkv_g = [], [], [], [], [], []
    for layer in range(layers):
        dp_width = r.w_qkv.shape[2]
        qkv_g.append(
            Group(DpGather(links, r.w_qkv.at[layer], middle_slot(r.wq.at[layer], dp_width), 1))
        )
        if columns_ok:
            slots = [column_slot(ref.at[layer], dp_width) for ref in (r.wo, r.wp)]
        else:
            slots = [lead_slot(ref.at[layer]) for ref in (r.wo_blocks, r.wp_blocks)]
        out_j = DpGather(links, r.w_out.at[layer], slots[0])
        fc_j = DpGather(links, r.w_fc.at[layer], row_slot(r.wf.at[layer], dp_width))
        fc_g.append(Group(out_j, fc_j))
        proj_g.append(Group(DpGather(links, r.w_proj.at[layer], slots[1])))
        rows = r.ctx.shape[1]
        ctx_j, act_j, dqkv_j, du_j = (
            PairGather(
                links, product_turn(links, layer, which), own.at[layer], lead_slot(whole.at[layer])
            )
            if links.paired
            else DpGather(links, own.at[layer], row_slot(whole.at[layer], rows))
            for own, whole, which in (
                (r.ctx, r.ctx_all, 1),
                (r.act, r.act_all, 1),
                (r.dqkv, r.dqkv_all, 0),
                (r.du, r.du_all, 0),
            )
        )
        fwd_g.append(Group(ctx_j, act_j))
        du_g.append(Group(du_j))
        dqkv_g.append(Group(dqkv_j))

    x_load.wait()
    unit = unit_rows(r.resid[0])[0].astype(bf16)
    unit_s = Spread(links, r.unit.at[0], unit)
    for load in loads:
        load.wait()
    pack_small(r, links)
    d_load.wait()
    d_bf = r.dres[last].astype(bf16)
    rows_s = Spread(links, r.drows.at[last], d_bf)
    crosses = [
        make_cross(r, links, 0, 0, unit),
        make_cross(r, links, last, 1, d_bf),
    ]
    r.sums[...] = jnp.zeros_like(r.sums)
    layout_tables(r)
    links.barrier()

    vec_sent = [
        links.send(r.pack_v, r.land_v.at[step - 1], tensor=links.tensor_peer(step))
        for step in range(1, n_tensor)
    ]
    b_here = r.small_b.at[links.dp]
    small_sent = [
        links.send(r.pack_b, b_here, dp=links.dp_peer(step)) for step in range(1, n_dp)
    ]
    small_kept = links.local(r.pack_b, b_here)
    pump = Pump()
    for layer in range(layers):
        for group in (qkv_g[layer], fc_g[layer], proj_g[layer]):
            pump.add(group)
    unit_s.send()
    crosses[0].send()
    total = r.pack_v[...]
    for step, copy in enumerate(vec_sent):
        copy.wait_recv()
        total = total + r.land_v[step]
    r.vec_all[links.dp] = total
    vec_here = r.vec_all.at[links.dp]
    vec_wide = [
        links.send(vec_here, vec_here, dp=links.dp_peer(step)) for step in range(1, n_dp)
    ]
    rows_s.send()
    pump.relay()
    crosses[1].send()
    small_kept.wait()
    for copy in small_sent + vec_wide:
        copy.wait_recv()
    unpack_small(r, links)

    for layer in range(layers):
        pump.rest()
        qkv_g[layer].finish()
        if layer == 0:
            crosses[0].forward()
        else:
            pump.relay()
        unit_s.finish()
        forward_attention(r, layer)
        if layer == 0:
            pump.relay()
            crosses[1].forward()
        pump.rest()
        fc_g[layer].finish()
        forward_hidden(r, layer)
        if layer > 0:
            crosses[-1].forward()
        if not links.paired:
            pump.add(fwd_g[layer])
        pump.relay()
        pump.rest()
        if links.paired and layer == last:
            fwd_g[last].start()
            fwd_g[0].start()
        proj_g[layer].finish()
        if not columns_ok:
            in_columns(r, links, layer)
        forward_part(r, layer)
        if layer < last:
            scatter = Scatter(links, r.part_f.at[layer], r.land_f.at[layer])
            pump.relay()
            values = r.resid[layer] + scatter.total() + gain_rows(r, layer)[4]
            r.resid[layer + 1] = values
            unit = unit_rows(values)[0].astype(bf16)
            unit_s = Spread(links, r.unit.at[layer + 1], unit)
            unit_s.send()
            crosses.append(make_cross(r, links, layer + 1, 0, unit))
            crosses[-1].send()

    if links.paired:
        finish = backward_paired
    else:
        finish = backward_gathered
    stores = finish(r, links, pump, fwd_g, du_g, dqkv_g, crosses, rows_s)
    for store in stores:
        store.wait()
    links.finish()
    assert (links.used, links.used_local) == copy_counts(n_dp, n_tensor, layers)


def start_back(r, links, layer):
    backward_part(r, layer)
    scatter = Scatter(links, r.part_e.at[layer], r.land_e.at[layer])
    r.sums[5 * layer + 4 : 5 * layer + 5, :] = jnp.sum(r.dres[layer], axis=0, keepdims=True)
    return scatter


def step_back(r, links, layer, scatter, crosses):
    new_d = r.dres[layer] + back_unit(r.resid[layer], scatter.total())
    r.dres[layer - 1] = new_d
    d_bf = new_d.astype(jnp.bfloat16)
    rows_s = Spread(links, r.drows.at[layer - 1], d_bf)
    rows_s.send()
    crosses.append(make_cross(r, links, layer - 1, 1, d_bf))
    crosses[-1].send()
    return rows_s


def store_y(r, links, scatter):
    last = r.resid.shape[0] - 1
    r.y_v[...] = r.resid[last] + scatter.total() + gain_rows(r, last)[4]
    return links.local(r.y_v, r.y_out)


def store_grad_x(r, links, scatter):
    r.gx_v[...] = r.dres[0] + back_unit(r.resid[0], scatter.total())
    return links.local(r.gx_v, r.grad_x)


def backward_paired(r, links, pump, fwd_g, du_g, dqkv_g, crosses, rows_s):
    layers = r.resid.shape[0]
    last = layers - 1
    products = Products(r, links)
    done = []
    for layer in reversed(range(1, layers)):
        rows_s.finish()
        backward_hidden(r, layer)
        backward_attention(r, layer)
        scatter = start_back(r, links, layer)
        du_g[layer].start()
        if layer == last:
            for cross in crosses:
                cross.finish()
        rows_s = step_back(r, links, layer, scatter, crosses)
        fwd_g[layer].rest()
        dqkv_g[layer].start()
        if layer > 1:
            fwd_g[layer - 1].start()
        fwd_g[layer].finish()
        outputs = products.outputs(layer)
        du_g[layer].rest()
        du_g[layer].finish()
        hidden = products.hidden(layer)
        done.append((layer, outputs, hidden))
        if layer > 1:
            crosses[-1].forward()
    rows_s.finish()
    crosses[-1].forward()
    backward_hidden(r, 0)
    du_g[0].start()
    for layer in reversed(range(1, layers)):
        dqkv_g[layer].rest()
        dqkv_g[layer].finish()
    late = [(layer, products.heads(layer)) for layer in reversed(range(1, layers))]
    backward_attention(r, 0)
    dqkv_g[0].start()
    scatter = start_back(r, links, 0)
    sums_sent = start_sums(r, links)
    fwd_g[0].rest()
    for layer, outputs, _ in done:
        products.store_outputs(layer, outputs)
    for cross in crosses[layers + 1 :]:
        cross.finish()
    fwd_g[0].finish()
    outputs = products.outputs(0)
    du_g[0].rest()
    du_g[0].finish()
    hidden = products.hidden(0)
    sent_y = Scatter(links, r.part_f.at[last], r.land_f.at[last])
    dqkv_g[0].rest()
    for layer, _, product in done:
        products.store(layer, product, r.w_fc_g)
    dqkv_g[0].finish()
    heads = products.heads(0)
    sums_wide = middle_sums(r, links, sums_sent)
    stores = [store_grad_x(r, links, scatter)]
    for layer, product in late:
        products.store(layer, product, r.w_qkv_g)
    products.store_outputs(0, outputs)
    stores.append(end_sums(r, links, sums_wide))
    stores.append(store_y(r, links, sent_y))
    products.store(0, hidden, r.w_fc_g)
    products.store(0, heads, r.w_qkv_g)
    return stores + products.stores


def backward_gathered(r, links, pump, fwd_g, du_g, dqkv_g, crosses, rows_s):
    layers = r.resid.shape[0]
    last = layers - 1
    sent_y = Scatter(links, r.part_f.at[last], r.land_f.at[last])
    for layer in reversed(range(layers)):
        rows_s.finish()
        backward_hidden(r, layer)
        pump.add(du_g[layer])
        if layer == last:
            pump.relay()
        else:
            crosses[-1].forward()
        backward_attention(r, layer)
        pump.add(dqkv_g[layer])
        scatter = start_back(r, links, layer)
        if layer == 0:
            sums_sent = start_sums(r, links)
        pump.rest()
        pump.relay()
        if layer > 0:
            rows_s = step_back(r, links, layer, scatter, crosses)
            pump.rest()
            pump.relay()

    stores = [store_grad_x(r, links, scatter), store_y(r, links, sent_y)]
    stores.append(links.local(r.vecs, r.vecs_out))
    sums_wide = middle_sums(r, links, sums_sent)
    while pump.relayed or pump.started:
        if pump.relayed:
            pump.rest()
        if pump.started:
            pump.relay()
    stores.append(end_sums(r, links, sums_wide))
    for group in fwd_g + du_g + dqkv_g:
        group.finish()
    for cross in crosses:
        cross.finish()
    return stores


def places_kernel(names, *refs):
    r = types.SimpleNamespace(**dict(zip(names, refs)))
    tensor = lax.axis_index("tensor")
    count = [0]

    def local(src, dst):
        copy = pltpu.make_async_copy(src, dst, r.sems.at[count[0]])
        count[0] += 1
        copy.start()
        return copy

    load = local(r.total, r.total_v)
    moves = [
        (local(source, held), held, out)
        for source, held, out in (
            (r.qkv_in, r.qkv_v, r.w_qkv_g),
            (r.fc_in, r.fc_v, r.w_fc_g),
            (r.proj_in, r.proj_v, r.w_proj_g),
            (r.out_in, r.out_v, r.w_out_g),
            (r.y_in, r.y_v, r.y_out),
            (r.gx_in, r.gx_v, r.grad_x),
        )
    ]
    stores = []
    load.wait()
    layers, vec = r.g0.shape
    width = r.total.shape[1]
    rolled = pltpu.roll(r.total_v[...], lax.rem(width - tensor * vec, width), 1)
    for k, out in enumerate((r.g0, r.g1, r.g2, r.g3, r.g4)):
        for layer in range(layers):
            r.g_v[k, layer : layer + 1, :] = rolled[5 * layer + k : 5 * layer + k + 1, 0:vec]
        stores.append(local(r.g_v.at[k], out))
    rows = -(-5 * layers // 8) * 8
    for which in range(3):
        at = rows + which * layers
        r.bq_v[which] = r.total_v[at : at + layers, 0 : r.bq_v.shape[2]]
    at = rows + 3 * layers
    r.bf_v[...] = r.total_v[at : at + layers, 0 : r.bf_v.shape[1]]
    stores.append(local(r.bq_v, r.b_qkv_g))
    stores.append(local(r.bf_v, r.b_fc_g))
    for move, held, out in moves:
        move.wait()
        stores.append(local(held, out))
    for store in stores:
        store.wait()


def shaped(shape, dtype):
    return jax.ShapeDtypeStruct(tuple(shape), dtype)


def kernel_call(kernel, name, ins, outs, scratch, params):
    names = list(ins) + list(outs) + list(scratch)
    results = pl.pallas_call(
        functools.partial(kernel, names),
        out_shape=tuple(outs.values()),
        in_specs=[ANY] * len(ins),
        out_specs=(ANY,) * len(outs),
        scratch_shapes=list(scratch.values()),
        name=name,
        compiler_params=pltpu.CompilerParams(**params),
    )(*ins.values())
    return dict(zip(outs, results))


def per_device(
    x_in,
    seq_lengths,
    ln1_gain,
    ln1_bias,
    ln2_gain,
    ln2_bias,
    res_bias,
    w_qkv,
    b_qkv,
    w_out,
    w_fc,
    b_fc,
    w_proj,
    grad_out,
):
    n_tensor, n_dp = lax.axis_size("tensor"), lax.axis_size("dp")
    my_tensor, my_dp = lax.axis_index("tensor"), lax.axis_index("dp")
    bf16, f32 = jnp.bfloat16, jnp.float32
    my_rows, width = x_in.shape
    group_rows = my_rows * n_tensor
    total_rows = group_rows * n_dp
    layers = w_qkv.shape[0]
    part = w_qkv.shape[3]
    hidden = w_fc.shape[2]
    dp_width = width // n_dp
    vec = ln1_gain.shape[1]
    columns_ok = dp_width % 128 == 0
    vm = pltpu.VMEM
    pad8 = lambda n: -(-n // 8) * 8
    small_rows = pad8(4 * layers)
    vec_rows = pad8(5 * layers)
    n_remote, n_local = copy_counts(n_dp, n_tensor, layers)
    paired = n_dp == 8

    ins = dict(
        x_in=x_in,
        lens=seq_lengths,
        ln1_gain=ln1_gain,
        ln1_bias=ln1_bias,
        ln2_gain=ln2_gain,
        ln2_bias=ln2_bias,
        res_bias=res_bias,
        w_qkv=jnp.transpose(w_qkv, (0, 2, 1, 3)),
        b_qkv=jnp.transpose(b_qkv, (1, 0, 2)),
        w_out=w_out,
        w_fc=w_fc,
        b_fc=b_fc,
        w_proj=w_proj,
        grad_out=grad_out,
    )
    outs = dict(
        y_out=shaped(x_in.shape, f32),
        grad_x=shaped(x_in.shape, f32),
        total_out=shaped((vec_rows + small_rows, dp_width), f32),
    )
    gathered = dict(ctx_all=part, act_all=hidden, dqkv_all=3 * part, du_all=hidden)
    if paired:
        cross = (layers, 2, 4, n_tensor, my_rows, 2 * dp_width)
        outs |= dict(
            w_qkv_g=shaped(ins["w_qkv"].shape, f32),
            w_out_g=shaped(w_out.shape, f32),
            w_fc_g=shaped(w_fc.shape, f32),
            w_proj_g=shaped(w_proj.shape, f32),
        )
    else:
        cross = (layers, 2, n_dp, n_tensor, my_rows, dp_width)
        outs |= dict(vecs_out=shaped((vec_rows, width), f32), cross=shaped(cross, bf16))
        for name, size in gathered.items():
            outs[name] = shaped((layers, total_rows, size), bf16)
    rows_block = (layers, my_rows, width)
    group_block = (layers, group_rows, width)
    land = (layers, n_tensor - 1, my_rows, width)
    scratch = dict(
        resid=vm(rows_block, f32),
        dres=vm(rows_block, f32),
        lens_v=vm(seq_lengths.shape, jnp.int32),
        sv=vm((5,) + ln1_gain.shape, f32),
        sq=vm(ins["b_qkv"].shape, f32),
        sf=vm(b_fc.shape, f32),
        pack_v=vm((vec_rows, dp_width), f32),
        pack_b=vm((small_rows, 128), f32),
        land_v=vm((n_tensor - 1, vec_rows, dp_width), f32),
        vec_all=vm((n_dp, vec_rows, dp_width), f32),
        small_b=vm((n_dp, small_rows, 128), f32),
        vecs=vm((vec_rows, width), f32),
        bq=vm((pad8(3 * layers), part), f32),
        bf=vm((pad8(layers), hidden), f32),
        same=vm((group_rows, part), f32),
        up=vm((group_rows, part), f32),
        down=vm((group_rows, part), f32),
        mask=vm((group_rows, group_rows), f32),
        wq=vm((layers, 3, width, part), bf16),
        wf=vm((layers, width, hidden), bf16),
        wo=vm((layers, part, width), bf16),
        wp=vm((layers, hidden, width), bf16),
        unit=vm(group_block, bf16),
        drows=vm(group_block, bf16),
        qkv=vm((layers, group_rows, 3 * part), bf16),
        ctx=vm((layers, group_rows, part), bf16),
        pre=vm((layers, group_rows, hidden), f32),
        act=vm((layers, group_rows, hidden), bf16),
        dctx=vm((group_rows, part), bf16),
        du=vm((layers, group_rows, hidden), bf16),
        dqkv=vm((layers, group_rows, 3 * part), bf16),
        part_f=vm(group_block, bf16),
        part_e=vm(group_block, bf16),
        land_f=vm(land, bf16),
        land_e=vm(land, bf16),
        stage=vm(cross[:3] + cross[4:], bf16),
        sums=vm((vec_rows, width), f32),
        sums_q=vm((pad8(3 * layers), part), f32),
        sums_f=vm((pad8(layers), hidden), f32),
        sums_stage=vm((n_dp, vec_rows + small_rows, dp_width), f32),
        land_s=vm((n_dp - 1, vec_rows + small_rows, dp_width), f32),
        half=vm((vec_rows, dp_width), f32),
        land_t=vm((n_tensor - 1, vec_rows, dp_width), f32),
        total_v=vm((vec_rows + small_rows, dp_width), f32),
        y_v=vm((my_rows, width), f32),
        gx_v=vm((my_rows, width), f32),
        send_sems=pltpu.SemaphoreType.DMA((n_remote,)),
        recv_sems=pltpu.SemaphoreType.DMA((n_remote,)),
        local_sems=pltpu.SemaphoreType.DMA((n_local,)),
    )
    if not columns_ok:
        scratch["wo_blocks"] = vm((layers, n_dp, part, dp_width), bf16)
        scratch["wp_blocks"] = vm((layers, n_dp, hidden, dp_width), bf16)
    if paired:
        scratch["cross"] = vm(cross, bf16)
        for name, size in gathered.items():
            scratch[name] = vm((layers, 4, group_rows, size), bf16)
        halves = dict(
            gq=ins["w_qkv"].shape,
            go=(layers, dp_width, part),
            gf=(layers, dp_width, hidden),
            gp=(layers, dp_width, hidden),
        )
        for name, shape in halves.items():
            scratch[name + "_own"] = vm(shape, f32)
            scratch[name + "_away"] = vm(shape, bf16)
            scratch[name + "_land"] = vm(shape, bf16)
        scratch |= dict(go_v=vm(w_out.shape, f32), gp_v=vm(w_proj.shape, f32))
    step = kernel_call(
        functools.partial(layers_kernel, n_dp, n_tensor),
        "layers",
        ins,
        outs,
        scratch,
        {"collective_id": 0, "has_side_effects": True, "vmem_limit_bytes": 58 << 20},
    )

    if paired:
        vectors = {f"g{k}": shaped(ln1_gain.shape, f32) for k in range(5)}
        done = kernel_call(
            places_kernel,
            "places",
            dict(
                y_in=step["y_out"],
                gx_in=step["grad_x"],
                total=step["total_out"],
                qkv_in=step["w_qkv_g"],
                out_in=step["w_out_g"],
                fc_in=step["w_fc_g"],
                proj_in=step["w_proj_g"],
            ),
            dict(
                y_out=shaped(x_in.shape, f32),
                grad_x=shaped(x_in.shape, f32),
                w_qkv_g=shaped(ins["w_qkv"].shape, f32),
                b_qkv_g=shaped(ins["b_qkv"].shape, f32),
                w_out_g=shaped(w_out.shape, f32),
                w_fc_g=shaped(w_fc.shape, f32),
                b_fc_g=shaped(b_fc.shape, f32),
                w_proj_g=shaped(w_proj.shape, f32),
                **vectors,
            ),
            dict(
                total_v=vm(step["total_out"].shape, f32),
                g_v=vm((5, layers, vec), f32),
                bq_v=vm(ins["b_qkv"].shape, f32),
                bf_v=vm(b_fc.shape, f32),
                qkv_v=vm(ins["w_qkv"].shape, f32),
                fc_v=vm(w_fc.shape, f32),
                proj_v=vm(w_proj.shape, f32),
                out_v=vm(w_out.shape, f32),
                y_v=vm(x_in.shape, f32),
                gx_v=vm(x_in.shape, f32),
                sems=pltpu.SemaphoreType.DMA((20,)),
            ),
            {"vmem_limit_bytes": 58 << 20},
        )
        return (
            (done["y_out"], done["grad_x"])
            + tuple(done[name] for name in vectors)
            + (
                jnp.transpose(done["w_qkv_g"], (0, 2, 1, 3)),
                jnp.transpose(done["b_qkv_g"], (1, 0, 2)),
            )
            + tuple(done[name] for name in ("w_out_g", "w_fc_g", "b_fc_g", "w_proj_g"))
        )

    over_tokens = (((0,), (0,)), ((), ()))
    grads = [[] for _ in range(6)]
    small = step["total_out"][vec_rows:]
    vectors = step["vecs_out"][: 5 * layers].reshape(5, layers, width)
    vectors = lax.dynamic_slice_in_dim(vectors, my_dp * dp_width, dp_width, axis=2)
    for layer in range(layers):
        context_t, act_t, dqkv_t, d_pre_t = (
            step[name][layer] for name in ("ctx_all", "act_all", "dqkv_all", "du_all")
        )
        unit_t = step["cross"][layer, 0].reshape(total_rows, dp_width).astype(f32)
        d_t = step["cross"][layer, 1].reshape(total_rows, dp_width)
        a_t = (unit_t * vectors[0, layer] + vectors[1, layer]).astype(bf16)
        m_t = (unit_t * vectors[2, layer] + vectors[3, layer]).astype(bf16)

        def contract(left, right):
            return lax.dot_general(left, right, over_tokens, preferred_element_type=f32)

        grads[0].append(contract(a_t, dqkv_t).reshape(w_qkv.shape[1:]))
        grads[1].append(small[layer : 3 * layers : layers, : b_qkv.shape[2]])
        grads[2].append(contract(context_t, d_t))
        grads[3].append(contract(m_t, d_pre_t))
        grads[4].append(small[3 * layers + layer, : b_fc.shape[1]])
        grads[5].append(contract(act_t, d_t))
    vector_grads = lax.dynamic_slice_in_dim(
        step["total_out"][: 5 * layers].reshape(layers, 5, dp_width), my_tensor * vec, vec, axis=2
    )
    return (
        (step["y_out"], step["grad_x"])
        + tuple(vector_grads[:, k] for k in range(5))
        + tuple(jnp.stack(group) for group in grads)
    )


def solution(mesh):
    in_specs = (
        P(("dp", "tensor"), None),
        P("dp", None),
        P(None, ("dp", "tensor")),
        P(None, ("dp", "tensor")),
        P(None, ("dp", "tensor")),
        P(None, ("dp", "tensor")),
        P(None, ("dp", "tensor")),
        P(None, "dp", None, "tensor"),
        P(None, None, ("tensor", "dp")),
        P(None, "tensor", "dp"),
        P(None, "dp", "tensor"),
        P(None, ("tensor", "dp")),
        P(None, "tensor", "dp"),
        P(("dp", "tensor"), None),
    )
    out_specs = (
        P(("dp", "tensor"), None),
        P(("dp", "tensor"), None),
        P(None, ("dp", "tensor")),
        P(None, ("dp", "tensor")),
        P(None, ("dp", "tensor")),
        P(None, ("dp", "tensor")),
        P(None, ("dp", "tensor")),
        P(None, "dp", None, "tensor"),
        P(None, None, ("tensor", "dp")),
        P(None, "tensor", "dp"),
        P(None, "dp", "tensor"),
        P(None, ("tensor", "dp")),
        P(None, "tensor", "dp"),
    )
    return jax.shard_map(
        per_device, mesh=mesh, in_specs=in_specs, out_specs=out_specs, check_vma=False
    )
```

```python
import functools
import types

import jax
import jax.numpy as jnp
from jax import lax
from jax.experimental import pallas as pl
from jax.experimental.pallas import tpu as pltpu
from jax.sharding import PartitionSpec as P

HD = 64
ROT = 16


EPS = 1e-05
NEG_FILL = -1e30


def gelu_exact(values):
    return 0.5 * values * (1.0 + jax.scipy.special.erf(values * 0.7071067811865476))


def gelu_slope(values):
    normal_cdf = 0.5 * (1.0 + jax.scipy.special.erf(values * 0.7071067811865476))
    return normal_cdf + values * jnp.exp(-0.5 * values * values) * 0.3989422804014327


MESH = pl.DeviceIdType.MESH
ANY = pl.BlockSpec(memory_space=pl.ANY)
VMEM = pl.BlockSpec(memory_space=pltpu.VMEM)


def copy_counts(n_dp, n_tensor, layers):
    chips = n_dp // 2
    remote = (n_tensor - 1) * (6 * layers + 2) + (n_dp - 1) * 3
    if chips == 4:
        remote = remote + layers * (4 * 13 + 4 * 3 + 2 * 3 + 4)
        again = (n_tensor - 1) * (3 * layers) + 15 * layers + n_dp - 4
        return remote, remote - again, 14 * layers + 14
    remote = remote + layers * (8 * (4 * chips - 3) + 2 * (n_dp - 1))
    return remote, remote, 10 * layers + 15


class Links:
    def __init__(self, n_dp, n_tensor, send_sems, recv_sems, local_sems):
        self.n_dp, self.n_tensor = n_dp, n_tensor
        self.dp, self.tensor = lax.axis_index("dp"), lax.axis_index("tensor")
        self.core, self.chip = lax.rem(self.dp, 2), self.dp // 2
        self.partner = self.dp + 1 - 2 * self.core
        self.paired = n_dp == 8
        if self.paired:
            self.gather_y, self.gather_x = Turn(self, False), Turn(self, True)
        self.send_sems, self.recv_sems, self.local_sems = send_sems, recv_sems, local_sems
        self.used, self.used_local, self.used_send = 0, 0, 0
        self.sent, self.free = [], []

    def send(self, src, dst, **where):
        if self.free:
            place = self.free.pop(0)
        else:
            place = self.used_send
            self.used_send += 1
        copy = pltpu.make_async_remote_copy(
            src_ref=src,
            dst_ref=dst,
            send_sem=self.send_sems.at[place],
            recv_sem=self.recv_sems.at[self.used],
            device_id=where,
            device_id_type=MESH,
        )
        self.used += 1
        copy.start()
        self.sent.append((copy, place))
        return copy

    def local(self, src, dst):
        copy = pltpu.make_async_copy(src, dst, self.local_sems.at[self.used_local])
        self.used_local += 1
        copy.start()
        return copy

    def dp_peer(self, step):
        return lax.rem(self.dp + step, self.n_dp)

    def tensor_peer(self, step):
        return lax.rem(self.tensor + step, self.n_tensor)

    def enter(self):
        sem = pltpu.get_barrier_semaphore()
        for step in range(1, self.n_tensor):
            pl.semaphore_signal(
                sem, inc=1, device_id={"tensor": self.tensor_peer(step)}, device_id_type=MESH
            )
        for step in range(1, self.n_dp):
            pl.semaphore_signal(
                sem, inc=1, device_id={"dp": self.dp_peer(step)}, device_id_type=MESH
            )

    def barrier(self):
        pl.semaphore_wait(pltpu.get_barrier_semaphore(), self.n_tensor + self.n_dp - 2)

    def settle(self, count):
        for copy, place in self.sent[:count]:
            copy.wait_send()
            self.free.append(place)
        self.sent = self.sent[count:]

    def finish(self):
        for copy, _ in self.sent:
            copy.wait_send()


class Turn:
    def __init__(self, links, gather_x):
        x, y = lax.rem(links.chip, 2), links.chip // 2
        over = (links.dp + 2 - 4 * x, lax.rem(links.dp + 4, 8))
        self.gather_x = gather_x
        self.gather_dp, self.sum_dp = over if gather_x else over[::-1]
        self.along, self.apart = (x, y) if gather_x else (y, x)
        self.place = self.along * 2 + links.core
        self.far_place = lax.rem(self.place + 2, 4)

    def block(self, place, apart):
        if self.gather_x:
            return apart * 4 + place
        return place // 2 * 4 + 2 * apart + lax.rem(place, 2)


class DpGather:
    def __init__(self, links, own, slot, axis=0):
        self.links, self.own, self.slot = links, own, slot
        self.chips = links.n_dp // 2
        self.core, self.chip, self.partner = links.core, links.chip, links.partner
        self.relays = self.chips == 4
        rows = own.shape[axis] // 2
        self.halves = [
            (slice(None),) * axis + (pl.ds(half * rows, rows),) for half in range(2)
        ]
        self.passed = []
        if self.relays:
            near = self.chip + 1 - 2 * lax.rem(self.chip, 2)
            far = lax.rem(self.chip + 2, 4)
            self.across = lax.rem(near + 2, 4)
            self.order = ((near, far), (far, near))

    def device(self, chip):
        return chip * 2 + self.core

    def out(self, rows, chip):
        return self.links.send(
            self.own.at[rows], self.slot(self.links.dp).at[rows], dp=self.device(chip)
        )

    def pass_on(self, rows, chip, target):
        block = self.slot(self.device(chip)).at[rows]
        return self.links.send(block, block, dp=target)

    def start(self):
        if self.relays:
            self.first = [self.out(rows, order[0]) for rows, order in zip(self.halves, self.order)]
            self.second = [self.out(rows, order[1]) for rows, order in zip(self.halves, self.order)]
        else:
            self.direct = [
                [self.out(rows, lax.rem(self.chip + step, self.chips)) for rows in self.halves]
                for step in range(1, self.chips)
            ]
        own_slot = self.slot(self.links.dp)
        self.passed.append(self.links.send(self.own, own_slot, dp=self.partner))
        self.kept = self.links.local(self.own, own_slot)

    def relay(self):
        if not self.relays:
            return
        self.relayed = []
        for copy, rows, order in zip(self.first, self.halves, self.order):
            copy.wait_recv()
            self.relayed.append(self.pass_on(rows, order[0], self.device(order[1])))
            self.passed.append(self.pass_on(rows, order[0], self.partner))

    def rest(self):
        if not self.relays:
            for step, copies in enumerate(self.direct):
                origin = lax.rem(self.chip + self.chips - step - 1, self.chips)
                for copy, rows in zip(copies, self.halves):
                    copy.wait_recv()
                    self.passed.append(self.pass_on(rows, origin, self.partner))
            return
        for copy, rows, order in zip(self.second, self.halves, self.order):
            copy.wait_recv()
            self.passed.append(self.pass_on(rows, order[1], self.partner))
        for copy, rows in zip(self.relayed, self.halves):
            copy.wait_recv()
            self.passed.append(self.pass_on(rows, self.across, self.partner))

    def finish(self):
        for copy in self.passed:
            copy.wait_recv()
        self.kept.wait()


class PairGather:
    def __init__(self, links, turn, own, slot):
        self.links, self.turn, self.own, self.slot = links, turn, own, slot

    def start(self):
        links, here = self.links, self.slot(self.turn.place)
        self.out = links.send(self.own, here, dp=self.turn.gather_dp)
        self.passed = [links.send(self.own, here, dp=links.partner)]
        self.kept = links.local(self.own, here)

    def rest(self):
        self.out.wait_recv()
        block = self.slot(self.turn.far_place)
        self.passed.append(self.links.send(block, block, dp=self.links.partner))

    def finish(self):
        for copy in self.passed:
            copy.wait_recv()
        self.kept.wait()


class Group:
    def __init__(self, *gathers):
        self.gathers = gathers

    def start(self):
        for gather in self.gathers:
            gather.start()

    def relay(self):
        for gather in self.gathers:
            gather.relay()

    def rest(self):
        for gather in self.gathers:
            gather.rest()

    def finish(self):
        for gather in self.gathers:
            gather.finish()


class Pump:
    def __init__(self):
        self.todo, self.started, self.relayed, self.every = [], [], [], []

    def add(self, group):
        self.todo.append(group)
        self.every.append(group)
        if not self.started:
            self.start()

    def start(self):
        if self.todo:
            group = self.todo.pop(0)
            group.start()
            self.started.append(group)

    def relay(self):
        group = self.started.pop(0)
        group.relay()
        self.relayed.append(group)
        if not self.started:
            self.start()

    def rest(self):
        self.relayed.pop(0).rest()


def row_slot(ref, rows):
    return lambda d: ref.at[pl.ds(pl.multiple_of(d * rows, rows), rows)]


def middle_slot(ref, rows):
    return lambda d: ref.at[:, pl.ds(pl.multiple_of(d * rows, rows), rows)]


def column_slot(ref, size):
    return lambda d: ref.at[:, pl.ds(pl.multiple_of(d * size, size), size)]


def lead_slot(ref):
    return lambda d: ref.at[d]


class Scatter:
    def __init__(self, links, part, landing):
        self.links, self.part, self.landing = links, part, landing
        self.rows = landing.shape[1]
        slot = row_slot(part, self.rows)
        self.copies = [
            links.send(
                slot(links.tensor_peer(step)),
                landing.at[step - 1],
                tensor=links.tensor_peer(step),
            )
            for step in range(1, links.n_tensor)
        ]

    def total(self):
        own = pl.ds(pl.multiple_of(self.links.tensor * self.rows, self.rows), self.rows)
        total = self.part[own, :].astype(jnp.float32)
        for step, copy in enumerate(self.copies):
            copy.wait_recv()
            total = total + self.landing[step].astype(jnp.float32)
        return total


class Spread:
    def __init__(self, links, ref, value):
        rows = value.shape[0]
        self.links, self.here = links, row_slot(ref, rows)(links.tensor)
        ref[pl.ds(pl.multiple_of(links.tensor * rows, rows), rows), :] = value

    def send(self):
        links = self.links
        self.copies = [
            links.send(self.here, self.here, tensor=links.tensor_peer(step))
            for step in range(1, links.n_tensor)
        ]

    def finish(self):
        for copy in self.copies:
            copy.wait_recv()


class Cross:
    def __init__(self, links, turn, stage, out, value):
        self.links, self.turn, self.stage, self.out = links, turn, stage, out
        self.count, _, width = stage.shape
        self.me = turn.place if links.paired else links.dp
        if not links.paired:
            for d in range(self.count):
                stage[d] = value[:, d * width : (d + 1) * width]
            return
        half = width // 2
        wide = value.astype(jnp.float32)
        for s in range(self.count):
            at = [
                (apart * 4 + s if turn.gather_x else s // 2 * 4 + 2 * apart + s % 2) * half
                for apart in range(2)
            ]
            one, two = (wide[:, place : place + half] for place in at)
            stage[s, :, 0:half] = jnp.where(turn.apart == 0, one, two).astype(value.dtype)
            stage[s, :, half:width] = jnp.where(turn.apart == 0, two, one).astype(value.dtype)

    def send(self):
        links, stage = self.links, self.stage
        here = self.out.at[self.me, links.tensor]
        self.copies = []
        for step in range(1, self.count):
            peer = lax.rem(self.me + step, self.count)
            device = self.turn.block(peer, self.turn.apart) if links.paired else peer
            self.copies.append(links.send(stage.at[peer], here, dp=device))
        self.kept = links.local(stage.at[self.me], here)

    def forward(self):
        links = self.links
        for copy in self.copies:
            copy.wait_recv()
        self.kept.wait()
        mine = self.out.at[:, links.tensor]
        self.wide = [
            links.send(mine, mine, tensor=links.tensor_peer(step))
            for step in range(1, links.n_tensor)
        ]

    def finish(self):
        for copy in self.wide:
            copy.wait_recv()


class Product:
    def __init__(self, links, turn, own, away, landing, rows, columns):
        self.own, self.landing = own, landing
        parts = own.shape[0] if len(own.shape) == 3 else 1
        half, width = own.shape[-2:]
        for k in range(parts):
            total = dot_tn(rows, columns[:, k * width : (k + 1) * width])
            if len(own.shape) == 3:
                own[k] = total[:half]
                away[k] = total[half:].astype(away.dtype)
            else:
                own[...] = total[:half]
                away[...] = total[half:].astype(away.dtype)
        self.copy = links.send(away, landing, dp=turn.sum_dp)

    def total(self):
        self.copy.wait_recv()
        return self.own[...] + self.landing[...].astype(jnp.float32)


def unit_rows(values):
    average = jnp.mean(values, axis=-1, keepdims=True)
    centred = values - average
    variance = jnp.mean(centred * centred, axis=-1, keepdims=True)
    scale = lax.rsqrt(variance + EPS)
    return centred * scale, scale


def back_unit(values, grad):
    unit, scale = unit_rows(values)
    return scale * (
        grad
        - jnp.mean(grad, axis=-1, keepdims=True)
        - unit * jnp.mean(grad * unit, axis=-1, keepdims=True)
    )


def dot_nn(left, right):
    return jnp.dot(left, right, preferred_element_type=jnp.float32)


def dot_nt(left, right):
    return lax.dot_general(left, right, (((1,), (1,)), ((), ())), preferred_element_type=jnp.float32)


def dot_tn(left, right):
    return lax.dot_general(left, right, (((0,), (0,)), ((), ())), preferred_element_type=jnp.float32)


def turn(vectors, same, up, down, sign):
    width = vectors.shape[1]
    above = pltpu.roll(vectors, width - ROT // 2, 1)
    below = pltpu.roll(vectors, ROT // 2, 1)
    return vectors * same + sign * (above * up + below * down)


def head_scores(query, key, mask):
    scores = dot_nt(query, key) * HD ** (-0.5)
    scores = jnp.where(mask, scores, NEG_FILL)
    terms = jnp.exp(scores - jnp.max(scores, axis=-1, keepdims=True))
    return terms / jnp.sum(terms, axis=-1, keepdims=True)


def layout_tables(r):
    f32 = jnp.float32
    rows, width = r.same.shape
    lengths = r.lens_v[...]
    row_of = lax.broadcasted_iota(jnp.int32, (rows, rows), 0)
    col_of = lax.broadcasted_iota(jnp.int32, (rows, rows), 1)
    row_lane = lax.broadcasted_iota(jnp.int32, (rows, 128), 0)
    start = jnp.zeros((rows, rows), jnp.int32)
    start_lane = jnp.zeros((rows, 128), jnp.int32)
    end = jnp.zeros((1, 1), jnp.int32)
    for k in range(lengths.shape[1]):
        end = end + lengths[:, k : k + 1]
        start = jnp.where(row_of >= end, end, start)
        start_lane = jnp.where(row_lane >= end, end, start_lane)
    r.mask[...] = jnp.where((col_of >= start) & (col_of <= row_of), 1.0, 0.0)
    positions = (row_lane - start_lane).astype(f32)
    lane = lax.rem(lax.broadcasted_iota(jnp.int32, (1, 128), 1), HD)
    half = ROT // 2
    inverse = jnp.power(10000.0, -2.0 * lax.rem(lane, half).astype(f32) / ROT)
    angles = positions * inverse
    cos_tab, sin_tab = jnp.cos(angles), jnp.sin(angles)
    same = jnp.where(lane < ROT, cos_tab, 1.0)
    up = jnp.where(lane < half, -sin_tab, 0.0)
    down = jnp.where((lane >= half) & (lane < ROT), sin_tab, 0.0)
    for ref, table in ((r.same, same), (r.up, up), (r.down, down)):
        for place in range(width // 128):
            ref[:, place * 128 : (place + 1) * 128] = table


def gain_rows(r, layer):
    layers = r.resid.shape[0]
    return tuple(r.vecs[k * layers + layer : k * layers + layer + 1, :] for k in range(5))


def forward_attention(r, layer):
    bf16 = jnp.bfloat16
    g1, b1, _, _, _ = gain_rows(r, layer)
    layers, _, part = r.ctx.shape
    normed_a = (r.unit[layer].astype(jnp.float32) * g1 + b1).astype(bf16)
    tables = (r.same[...], r.up[...], r.down[...])
    for which in range(3):
        row = which * layers + layer
        block = dot_nn(normed_a, r.wq[layer, which]) + r.bq[row : row + 1, :]
        if which < 2:
            block = turn(block, *tables, 1.0)
        r.qkv[layer, :, which * part : (which + 1) * part] = block.astype(bf16)
    allowed = r.mask[...] > 0.0
    for head in range(part // HD):
        q, k, v = (
            r.qkv[layer, :, which * part + head * HD : which * part + (head + 1) * HD]
            for which in range(3)
        )
        probs = head_scores(q, k, allowed).astype(bf16)
        r.ctx[layer, :, head * HD : (head + 1) * HD] = dot_nn(probs, v).astype(bf16)


def forward_hidden(r, layer):
    bf16 = jnp.bfloat16
    _, _, g2, b2, _ = gain_rows(r, layer)
    normed_m = (r.unit[layer].astype(jnp.float32) * g2 + b2).astype(bf16)
    hidden = dot_nn(normed_m, r.wf[layer]) + r.bf[layer : layer + 1, :]
    r.pre[layer] = hidden
    r.act[layer] = gelu_exact(hidden).astype(bf16)


def forward_part(r, layer):
    r.part_f[layer] = (
        dot_nn(r.ctx[layer], r.wo[layer]) + dot_nn(r.act[layer], r.wp[layer])
    ).astype(jnp.bfloat16)


def backward_hidden(r, layer):
    bf16 = jnp.bfloat16
    r.dctx[...] = dot_nt(r.drows[layer], r.wo[layer]).astype(bf16)
    d_pre = dot_nt(r.drows[layer], r.wp[layer]) * gelu_slope(r.pre[layer])
    r.sums_f[layer : layer + 1, :] = jnp.sum(d_pre, axis=0, keepdims=True)
    r.du[layer] = d_pre.astype(bf16)


def backward_attention(r, layer):
    bf16, f32 = jnp.bfloat16, jnp.float32
    part = r.ctx.shape[2]
    allowed = r.mask[...] > 0.0
    pieces = [[], [], []]
    for head in range(part // HD):
        here = slice(head * HD, (head + 1) * HD)
        q, k, v = (
            r.qkv[layer, :, which * part + head * HD : which * part + (head + 1) * HD]
            for which in range(3)
        )
        dc = r.dctx[:, here]
        probs = head_scores(q, k, allowed)
        delta = jnp.sum(
            dc.astype(f32) * r.ctx[layer, :, here].astype(f32), axis=-1, keepdims=True
        )
        d_scaled = (probs * (dot_nt(dc, v) - delta) * HD ** (-0.5)).astype(bf16)
        pieces[0].append(dot_nn(d_scaled, k))
        pieces[1].append(dot_tn(d_scaled, q))
        pieces[2].append(dot_tn(probs.astype(bf16), dc))
    tables = (r.same[...], r.up[...], r.down[...])
    for which in range(3):
        block = jnp.concatenate(pieces[which], axis=1)
        if which < 2:
            block = turn(block, *tables, -1.0)
        row = which * r.ctx.shape[0] + layer
        r.sums_q[row : row + 1, :] = jnp.sum(block, axis=0, keepdims=True)
        r.dqkv[layer, :, which * part : (which + 1) * part] = block.astype(bf16)


def backward_part(r, layer):
    g1, _, g2, _, _ = gain_rows(r, layer)
    part = r.ctx.shape[2]
    d_a = sum(
        dot_nt(r.dqkv[layer, :, which * part : (which + 1) * part], r.wq[layer, which])
        for which in range(3)
    )
    d_m = dot_nt(r.du[layer], r.wf[layer])
    r.part_e[layer] = (d_a * g1 + d_m * g2).astype(jnp.bfloat16)
    wide = r.unit[layer].astype(jnp.float32)
    for row, term in enumerate((d_a * wide, d_a, d_m * wide, d_m)):
        r.sums[5 * layer + row : 5 * layer + row + 1, :] = jnp.sum(term, axis=0, keepdims=True)


def pack_small(r, links):
    count, layers, vec = r.sv.shape
    r.pack_v[...] = jnp.zeros_like(r.pack_v)
    owner = lax.broadcasted_iota(jnp.int32, (layers, vec * links.n_tensor), 1) // vec
    for k in range(count):
        value = jnp.concatenate([r.sv[k]] * links.n_tensor, axis=1)
        r.pack_v[k * layers : (k + 1) * layers, :] = jnp.where(owner == links.tensor, value, 0.0)
    r.pack_b[...] = jnp.zeros_like(r.pack_b)
    for which in range(3):
        r.pack_b[which * layers : (which + 1) * layers, 0 : r.sq.shape[2]] = r.sq[which]
    r.pack_b[3 * layers : 4 * layers, 0 : r.sf.shape[1]] = r.sf[...]


def unpack_small(r, links):
    layers = r.sf.shape[0]
    width = r.vec_all.shape[2]
    rows = 0
    for d in range(links.n_dp):
        r.vecs[:, d * width : (d + 1) * width] = r.vec_all[d]
    for ref, height, lanes in ((r.bq, 3 * layers, r.sq.shape[2]), (r.bf, layers, r.sf.shape[1])):
        ref[0:height, :] = jnp.concatenate(
            [r.small_b[d, rows : rows + height, 0:lanes] for d in range(links.n_dp)], axis=1
        )
        rows = rows + height


def in_columns(r, links, layer):
    for blocks, whole in ((r.wo_blocks, r.wo), (r.wp_blocks, r.wp)):
        width = blocks.shape[3]
        for d in range(links.n_dp):
            whole[layer, :, d * width : (d + 1) * width] = blocks[layer, d]


def start_sums(r, links):
    layers = r.resid.shape[0]
    width = r.sums_stage.shape[2]
    rows = r.sums.shape[0]
    lanes_q, lanes_f = r.sq.shape[2], r.sf.shape[1]
    r.sums_stage[...] = jnp.zeros_like(r.sums_stage)
    for d in range(links.n_dp):
        r.sums_stage[d, 0:rows, :] = r.sums[:, d * width : (d + 1) * width]
        r.sums_stage[d, rows : rows + 3 * layers, 0:lanes_q] = r.sums_q[
            0 : 3 * layers, d * lanes_q : (d + 1) * lanes_q
        ]
        r.sums_stage[d, rows + 3 * layers : rows + 4 * layers, 0:lanes_f] = r.sums_f[
            0:layers, d * lanes_f : (d + 1) * lanes_f
        ]
    return [
        links.send(
            r.sums_stage.at[links.dp_peer(step)], r.land_s.at[step - 1], dp=links.dp_peer(step)
        )
        for step in range(1, links.n_dp)
    ]


def middle_sums(r, links, sent):
    rows = r.sums.shape[0]
    total = r.sums_stage[links.dp]
    for step, copy in enumerate(sent):
        copy.wait_recv()
        total = total + r.land_s[step]
    r.total_v[...] = total
    r.half[...] = total[0:rows]
    return [
        links.send(r.half, r.land_t.at[step - 1], tensor=links.tensor_peer(step))
        for step in range(1, links.n_tensor)
    ]


def end_sums(r, links, sent):
    rows = r.sums.shape[0]
    total = r.half[...]
    for step, copy in enumerate(sent):
        copy.wait_recv()
        total = total + r.land_t[step]
    r.total_v[0:rows, :] = total
    return links.local(r.total_v, r.total_out)


def token_rows(r, layer, which):
    block = r.cross[layer, which]
    return block.reshape(-1, block.shape[-1])


def product_turn(links, layer, which):
    if not links.paired:
        return None
    return links.gather_y if (layer, which) == (0, 1) else links.gather_x


def normed_rows(r, links, layer, norm):
    layers = r.resid.shape[0]
    half = r.cross.shape[-1] // 2
    gain, bias = (
        jnp.concatenate(
            [
                r.vecs[row : row + 1, pl.ds(pl.multiple_of(d * half, half), half)]
                for d in (links.dp, product_turn(links, layer, 0).sum_dp)
            ],
            axis=1,
        )
        for row in (2 * norm * layers + layer, (2 * norm + 1) * layers + layer)
    )
    unit = token_rows(r, layer, 0).astype(jnp.float32)
    return (unit * gain + bias).astype(jnp.bfloat16)


class Products:
    def __init__(self, r, links):
        self.r, self.links, self.stores = r, links, []

    def columns(self, ref, layer):
        block = ref[layer]
        return block.reshape(-1, block.shape[-1])

    def outputs(self, layer):
        r = self.r
        d_t = token_rows(r, layer, 1)
        return [
            Product(
                self.links, product_turn(self.links, layer, 1), own.at[layer], away.at[layer], land.at[layer], d_t,
                self.columns(columns, layer),
            )
            for own, away, land, columns in (
                (r.go_own, r.go_away, r.go_land, r.ctx_all),
                (r.gp_own, r.gp_away, r.gp_land, r.act_all),
            )
        ]

    def hidden(self, layer):
        r = self.r
        return Product(
            self.links, product_turn(self.links, layer, 0), r.gf_own.at[layer], r.gf_away.at[layer], r.gf_land.at[layer],
            normed_rows(r, self.links, layer, 1), self.columns(r.du_all, layer),
        )

    def heads(self, layer):
        r = self.r
        return Product(
            self.links, product_turn(self.links, layer, 0), r.gq_own.at[layer], r.gq_away.at[layer], r.gq_land.at[layer],
            normed_rows(r, self.links, layer, 0), self.columns(r.dqkv_all, layer),
        )

    def store_outputs(self, layer, products):
        r = self.r
        for product, turned, out in zip(products, (r.go_v, r.gp_v), (r.w_out_g, r.w_proj_g)):
            turned[layer] = jnp.transpose(product.total())
            self.stores.append(self.links.local(turned.at[layer], out.at[layer]))

    def store(self, layer, product, out):
        product.own[...] = product.total()
        self.stores.append(self.links.local(product.own, out.at[layer]))


def make_cross(r, links, layer, which, value):
    turn = product_turn(links, layer, which)
    return Cross(links, turn, r.stage.at[layer, which], r.cross.at[layer, which], value)


def layers_kernel(n_dp, n_tensor, names, *refs):
    r = types.SimpleNamespace(**dict(zip(names, refs)))
    links = Links(n_dp, n_tensor, r.send_sems, r.recv_sems, r.local_sems)
    bf16 = jnp.bfloat16
    layers = r.w_out.shape[0]
    last = layers - 1
    columns_ok = not hasattr(r, "wo_blocks")
    links.enter()
    x_load = links.local(r.x_in, r.resid.at[0])
    d_load = links.local(r.grad_out, r.dres.at[last])
    loads = [links.local(r.lens, r.lens_v)]
    for k, ref in enumerate((r.ln1_gain, r.ln1_bias, r.ln2_gain, r.ln2_bias, r.res_bias)):
        loads.append(links.local(ref, r.sv.at[k]))
    loads.append(links.local(r.b_qkv, r.sq))
    loads.append(links.local(r.b_fc, r.sf))

    qkv_g, fc_g, proj_g, fwd_g, du_g, dqkv_g = [], [], [], [], [], []
    for layer in range(layers):
        dp_width = r.w_qkv.shape[2]
        qkv_g.append(
            Group(DpGather(links, r.w_qkv.at[layer], middle_slot(r.wq.at[layer], dp_width), 1))
        )
        if columns_ok:
            slots = [column_slot(ref.at[layer], dp_width) for ref in (r.wo, r.wp)]
        else:
            slots = [lead_slot(ref.at[layer]) for ref in (r.wo_blocks, r.wp_blocks)]
        out_j = DpGather(links, r.w_out.at[layer], slots[0])
        fc_j = DpGather(links, r.w_fc.at[layer], row_slot(r.wf.at[layer], dp_width))
        fc_g.append(Group(out_j, fc_j))
        proj_g.append(Group(DpGather(links, r.w_proj.at[layer], slots[1])))
        rows = r.ctx.shape[1]
        ctx_j, act_j, dqkv_j, du_j = (
            PairGather(
                links, product_turn(links, layer, which), own.at[layer], lead_slot(whole.at[layer])
            )
            if links.paired
            else DpGather(links, own.at[layer], row_slot(whole.at[layer], rows))
            for own, whole, which in (
                (r.ctx, r.ctx_all, 1),
                (r.act, r.act_all, 1),
                (r.dqkv, r.dqkv_all, 0),
                (r.du, r.du_all, 0),
            )
        )
        fwd_g.append(Group(ctx_j, act_j))
        du_g.append(Group(du_j))
        dqkv_g.append(Group(dqkv_j))

    x_load.wait()
    unit = unit_rows(r.resid[0])[0].astype(bf16)
    unit_s = Spread(links, r.unit.at[0], unit)
    for load in loads:
        load.wait()
    pack_small(r, links)
    d_load.wait()
    d_bf = r.dres[last].astype(bf16)
    rows_s = Spread(links, r.drows.at[last], d_bf)
    crosses = [
        make_cross(r, links, 0, 0, unit),
        make_cross(r, links, last, 1, d_bf),
    ]
    r.sums[...] = jnp.zeros_like(r.sums)
    layout_tables(r)
    links.barrier()

    vec_sent = [
        links.send(r.pack_v, r.land_v.at[step - 1], tensor=links.tensor_peer(step))
        for step in range(1, n_tensor)
    ]
    b_here = r.small_b.at[links.dp]
    small_sent = [
        links.send(r.pack_b, b_here, dp=links.dp_peer(step)) for step in range(1, n_dp)
    ]
    small_kept = links.local(r.pack_b, b_here)
    pump = Pump()
    for layer in range(layers):
        for group in (qkv_g[layer], fc_g[layer], proj_g[layer]):
            pump.add(group)
    unit_s.send()
    crosses[0].send()
    total = r.pack_v[...]
    for step, copy in enumerate(vec_sent):
        copy.wait_recv()
        total = total + r.land_v[step]
    r.vec_all[links.dp] = total
    vec_here = r.vec_all.at[links.dp]
    vec_wide = [
        links.send(vec_here, vec_here, dp=links.dp_peer(step)) for step in range(1, n_dp)
    ]
    rows_s.send()
    pump.relay()
    crosses[1].send()
    small_kept.wait()
    for copy in small_sent + vec_wide:
        copy.wait_recv()
    unpack_small(r, links)

    for layer in range(layers):
        pump.rest()
        qkv_g[layer].finish()
        if layer == 0:
            crosses[0].forward()
        else:
            pump.relay()
        unit_s.finish()
        forward_attention(r, layer)
        if layer == 0:
            pump.relay()
            crosses[1].forward()
        pump.rest()
        fc_g[layer].finish()
        forward_hidden(r, layer)
        if layer > 0:
            crosses[-1].forward()
        if not links.paired:
            pump.add(fwd_g[layer])
        pump.relay()
        pump.rest()
        if links.paired and layer == last:
            fwd_g[last].start()
            fwd_g[0].start()
        proj_g[layer].finish()
        if not columns_ok:
            in_columns(r, links, layer)
        forward_part(r, layer)
        if layer < last:
            scatter = Scatter(links, r.part_f.at[layer], r.land_f.at[layer])
            pump.relay()
            values = r.resid[layer] + scatter.total() + gain_rows(r, layer)[4]
            r.resid[layer + 1] = values
            unit = unit_rows(values)[0].astype(bf16)
            unit_s = Spread(links, r.unit.at[layer + 1], unit)
            settled = len(links.sent)
            unit_s.send()
            crosses.append(make_cross(r, links, layer + 1, 0, unit))
            crosses[-1].send()

    if links.paired:
        links.settle(settled)
        finish = backward_paired
    else:
        finish = backward_gathered
    stores = finish(r, links, pump, fwd_g, du_g, dqkv_g, crosses, rows_s)
    for store in stores:
        store.wait()
    links.finish()
    counts = (links.used, links.used_send, links.used_local)
    assert counts == copy_counts(n_dp, n_tensor, layers), counts


def start_back(r, links, layer):
    backward_part(r, layer)
    scatter = Scatter(links, r.part_e.at[layer], r.land_e.at[layer])
    r.sums[5 * layer + 4 : 5 * layer + 5, :] = jnp.sum(r.dres[layer], axis=0, keepdims=True)
    return scatter


def step_back(r, links, layer, scatter, crosses):
    new_d = r.dres[layer] + back_unit(r.resid[layer], scatter.total())
    r.dres[layer - 1] = new_d
    d_bf = new_d.astype(jnp.bfloat16)
    rows_s = Spread(links, r.drows.at[layer - 1], d_bf)
    rows_s.send()
    crosses.append(make_cross(r, links, layer - 1, 1, d_bf))
    crosses[-1].send()
    return rows_s


def store_y(r, links, scatter):
    last = r.resid.shape[0] - 1
    r.y_v[...] = r.resid[last] + scatter.total() + gain_rows(r, last)[4]
    return links.local(r.y_v, r.y_out)


def store_grad_x(r, links, scatter):
    r.gx_v[...] = r.dres[0] + back_unit(r.resid[0], scatter.total())
    return links.local(r.gx_v, r.grad_x)


def backward_paired(r, links, pump, fwd_g, du_g, dqkv_g, crosses, rows_s):
    layers = r.resid.shape[0]
    last = layers - 1
    products = Products(r, links)
    done = []
    for layer in reversed(range(1, layers)):
        rows_s.finish()
        backward_hidden(r, layer)
        backward_attention(r, layer)
        scatter = start_back(r, links, layer)
        du_g[layer].start()
        if layer == last:
            for cross in crosses:
                cross.finish()
        rows_s = step_back(r, links, layer, scatter, crosses)
        fwd_g[layer].rest()
        dqkv_g[layer].start()
        if layer > 1:
            fwd_g[layer - 1].start()
        fwd_g[layer].finish()
        outputs = products.outputs(layer)
        du_g[layer].rest()
        du_g[layer].finish()
        hidden = products.hidden(layer)
        done.append((layer, outputs, hidden))
        if layer > 1:
            crosses[-1].forward()
    fwd_g[0].rest()
    rows_s.finish()
    crosses[-1].forward()
    backward_hidden(r, 0)
    du_g[0].start()
    for layer in reversed(range(1, layers)):
        dqkv_g[layer].rest()
        dqkv_g[layer].finish()
    late = [(layer, products.heads(layer)) for layer in reversed(range(1, layers))]
    backward_attention(r, 0)
    dqkv_g[0].start()
    scatter = start_back(r, links, 0)
    sums_sent = start_sums(r, links)
    for layer, outputs, _ in done:
        products.store_outputs(layer, outputs)
    for cross in crosses[layers + 1 :]:
        cross.finish()
    fwd_g[0].finish()
    outputs = products.outputs(0)
    du_g[0].rest()
    du_g[0].finish()
    hidden = products.hidden(0)
    sent_y = Scatter(links, r.part_f.at[last], r.land_f.at[last])
    dqkv_g[0].rest()
    for layer, _, product in done:
        products.store(layer, product, r.w_fc_g)
    dqkv_g[0].finish()
    heads = products.heads(0)
    sums_wide = middle_sums(r, links, sums_sent)
    stores = [store_grad_x(r, links, scatter)]
    for layer, product in late:
        products.store(layer, product, r.w_qkv_g)
    products.store_outputs(0, outputs)
    stores.append(end_sums(r, links, sums_wide))
    stores.append(store_y(r, links, sent_y))
    products.store(0, hidden, r.w_fc_g)
    products.store(0, heads, r.w_qkv_g)
    return stores + products.stores


def backward_gathered(r, links, pump, fwd_g, du_g, dqkv_g, crosses, rows_s):
    layers = r.resid.shape[0]
    last = layers - 1
    sent_y = Scatter(links, r.part_f.at[last], r.land_f.at[last])
    for layer in reversed(range(layers)):
        rows_s.finish()
        backward_hidden(r, layer)
        pump.add(du_g[layer])
        if layer == last:
            pump.relay()
        else:
            crosses[-1].forward()
        backward_attention(r, layer)
        pump.add(dqkv_g[layer])
        scatter = start_back(r, links, layer)
        if layer == 0:
            sums_sent = start_sums(r, links)
        pump.rest()
        pump.relay()
        if layer > 0:
            rows_s = step_back(r, links, layer, scatter, crosses)
            pump.rest()
            pump.relay()

    stores = [store_grad_x(r, links, scatter), store_y(r, links, sent_y)]
    stores.append(links.local(r.vecs, r.vecs_out))
    sums_wide = middle_sums(r, links, sums_sent)
    while pump.relayed or pump.started:
        if pump.relayed:
            pump.rest()
        if pump.started:
            pump.relay()
    stores.append(end_sums(r, links, sums_wide))
    for group in fwd_g + du_g + dqkv_g:
        group.finish()
    for cross in crosses:
        cross.finish()
    return stores


def places_kernel(names, *refs):
    r = types.SimpleNamespace(**dict(zip(names, refs)))
    tensor = lax.axis_index("tensor")
    count = [0]

    def local(src, dst):
        copy = pltpu.make_async_copy(src, dst, r.sems.at[count[0]])
        count[0] += 1
        copy.start()
        return copy

    load = local(r.total, r.total_v)
    moves = [
        (local(source, held), held, out)
        for source, held, out in (
            (r.qkv_in, r.qkv_v, r.w_qkv_g),
            (r.fc_in, r.fc_v, r.w_fc_g),
            (r.proj_in, r.proj_v, r.w_proj_g),
            (r.out_in, r.out_v, r.w_out_g),
            (r.y_in, r.y_v, r.y_out),
            (r.gx_in, r.gx_v, r.grad_x),
        )
    ]
    stores = []
    load.wait()
    layers, vec = r.g0.shape
    width = r.total.shape[1]
    rolled = pltpu.roll(r.total_v[...], lax.rem(width - tensor * vec, width), 1)
    for k, out in enumerate((r.g0, r.g1, r.g2, r.g3, r.g4)):
        for layer in range(layers):
            r.g_v[k, layer : layer + 1, :] = rolled[5 * layer + k : 5 * layer + k + 1, 0:vec]
        stores.append(local(r.g_v.at[k], out))
    rows = -(-5 * layers // 8) * 8
    for which in range(3):
        at = rows + which * layers
        r.bq_v[which] = r.total_v[at : at + layers, 0 : r.bq_v.shape[2]]
    at = rows + 3 * layers
    r.bf_v[...] = r.total_v[at : at + layers, 0 : r.bf_v.shape[1]]
    stores.append(local(r.bq_v, r.b_qkv_g))
    stores.append(local(r.bf_v, r.b_fc_g))
    for move, held, out in moves:
        move.wait()
        stores.append(local(held, out))
    for store in stores:
        store.wait()


def shaped(shape, dtype):
    return jax.ShapeDtypeStruct(tuple(shape), dtype)


def kernel_call(kernel, name, ins, outs, scratch, params):
    names = list(ins) + list(outs) + list(scratch)
    results = pl.pallas_call(
        functools.partial(kernel, names),
        out_shape=tuple(outs.values()),
        in_specs=[ANY] * len(ins),
        out_specs=(ANY,) * len(outs),
        scratch_shapes=list(scratch.values()),
        name=name,
        compiler_params=pltpu.CompilerParams(**params),
    )(*ins.values())
    return dict(zip(outs, results))


def per_device(
    x_in,
    seq_lengths,
    ln1_gain,
    ln1_bias,
    ln2_gain,
    ln2_bias,
    res_bias,
    w_qkv,
    b_qkv,
    w_out,
    w_fc,
    b_fc,
    w_proj,
    grad_out,
):
    n_tensor, n_dp = lax.axis_size("tensor"), lax.axis_size("dp")
    my_tensor, my_dp = lax.axis_index("tensor"), lax.axis_index("dp")
    bf16, f32 = jnp.bfloat16, jnp.float32
    my_rows, width = x_in.shape
    group_rows = my_rows * n_tensor
    total_rows = group_rows * n_dp
    layers = w_qkv.shape[0]
    part = w_qkv.shape[3]
    hidden = w_fc.shape[2]
    dp_width = width // n_dp
    vec = ln1_gain.shape[1]
    columns_ok = dp_width % 128 == 0
    vm = pltpu.VMEM
    pad8 = lambda n: -(-n // 8) * 8
    small_rows = pad8(4 * layers)
    vec_rows = pad8(5 * layers)
    n_remote, n_send, n_local = copy_counts(n_dp, n_tensor, layers)
    paired = n_dp == 8

    ins = dict(
        x_in=x_in,
        lens=seq_lengths,
        ln1_gain=ln1_gain,
        ln1_bias=ln1_bias,
        ln2_gain=ln2_gain,
        ln2_bias=ln2_bias,
        res_bias=res_bias,
        w_qkv=jnp.transpose(w_qkv, (0, 2, 1, 3)),
        b_qkv=jnp.transpose(b_qkv, (1, 0, 2)),
        w_out=w_out,
        w_fc=w_fc,
        b_fc=b_fc,
        w_proj=w_proj,
        grad_out=grad_out,
    )
    outs = dict(
        y_out=shaped(x_in.shape, f32),
        grad_x=shaped(x_in.shape, f32),
        total_out=shaped((vec_rows + small_rows, dp_width), f32),
    )
    gathered = dict(ctx_all=part, act_all=hidden, dqkv_all=3 * part, du_all=hidden)
    if paired:
        cross = (layers, 2, 4, n_tensor, my_rows, 2 * dp_width)
        outs |= dict(
            w_qkv_g=shaped(ins["w_qkv"].shape, f32),
            w_out_g=shaped(w_out.shape, f32),
            w_fc_g=shaped(w_fc.shape, f32),
            w_proj_g=shaped(w_proj.shape, f32),
        )
    else:
        cross = (layers, 2, n_dp, n_tensor, my_rows, dp_width)
        outs |= dict(vecs_out=shaped((vec_rows, width), f32), cross=shaped(cross, bf16))
        for name, size in gathered.items():
            outs[name] = shaped((layers, total_rows, size), bf16)
    rows_block = (layers, my_rows, width)
    group_block = (layers, group_rows, width)
    land = (layers, n_tensor - 1, my_rows, width)
    scratch = dict(
        resid=vm(rows_block, f32),
        dres=vm(rows_block, f32),
        lens_v=vm(seq_lengths.shape, jnp.int32),
        sv=vm((5,) + ln1_gain.shape, f32),
        sq=vm(ins["b_qkv"].shape, f32),
        sf=vm(b_fc.shape, f32),
        pack_v=vm((vec_rows, dp_width), f32),
        pack_b=vm((small_rows, 128), f32),
        land_v=vm((n_tensor - 1, vec_rows, dp_width), f32),
        vec_all=vm((n_dp, vec_rows, dp_width), f32),
        small_b=vm((n_dp, small_rows, 128), f32),
        vecs=vm((vec_rows, width), f32),
        bq=vm((pad8(3 * layers), part), f32),
        bf=vm((pad8(layers), hidden), f32),
        same=vm((group_rows, part), f32),
        up=vm((group_rows, part), f32),
        down=vm((group_rows, part), f32),
        mask=vm((group_rows, group_rows), f32),
        wq=vm((layers, 3, width, part), bf16),
        wf=vm((layers, width, hidden), bf16),
        wo=vm((layers, part, width), bf16),
        wp=vm((layers, hidden, width), bf16),
        unit=vm(group_block, bf16),
        drows=vm(group_block, bf16),
        qkv=vm((layers, group_rows, 3 * part), bf16),
        ctx=vm((layers, group_rows, part), bf16),
        pre=vm((layers, group_rows, hidden), f32),
        act=vm((layers, group_rows, hidden), bf16),
        dctx=vm((group_rows, part), bf16),
        du=vm((layers, group_rows, hidden), bf16),
        dqkv=vm((layers, group_rows, 3 * part), bf16),
        part_f=vm(group_block, bf16),
        part_e=vm(group_block, bf16),
        land_f=vm(land, bf16),
        land_e=vm(land, bf16),
        stage=vm(cross[:3] + cross[4:], bf16),
        sums=vm((vec_rows, width), f32),
        sums_q=vm((pad8(3 * layers), part), f32),
        sums_f=vm((pad8(layers), hidden), f32),
        sums_stage=vm((n_dp, vec_rows + small_rows, dp_width), f32),
        land_s=vm((n_dp - 1, vec_rows + small_rows, dp_width), f32),
        half=vm((vec_rows, dp_width), f32),
        land_t=vm((n_tensor - 1, vec_rows, dp_width), f32),
        total_v=vm((vec_rows + small_rows, dp_width), f32),
        y_v=vm((my_rows, width), f32),
        gx_v=vm((my_rows, width), f32),
        send_sems=pltpu.SemaphoreType.DMA((n_send,)),
        recv_sems=pltpu.SemaphoreType.DMA((n_remote,)),
        local_sems=pltpu.SemaphoreType.DMA((n_local,)),
    )
    if not columns_ok:
        scratch["wo_blocks"] = vm((layers, n_dp, part, dp_width), bf16)
        scratch["wp_blocks"] = vm((layers, n_dp, hidden, dp_width), bf16)
    if paired:
        scratch["cross"] = vm(cross, bf16)
        for name, size in gathered.items():
            scratch[name] = vm((layers, 4, group_rows, size), bf16)
        halves = dict(
            gq=ins["w_qkv"].shape,
            go=(layers, dp_width, part),
            gf=(layers, dp_width, hidden),
            gp=(layers, dp_width, hidden),
        )
        for name, shape in halves.items():
            scratch[name + "_own"] = vm(shape, f32)
            scratch[name + "_away"] = vm(shape, bf16)
            scratch[name + "_land"] = vm(shape, bf16)
        scratch |= dict(go_v=vm(w_out.shape, f32), gp_v=vm(w_proj.shape, f32))
    step = kernel_call(
        functools.partial(layers_kernel, n_dp, n_tensor),
        "layers",
        ins,
        outs,
        scratch,
        {"collective_id": 0, "has_side_effects": True, "vmem_limit_bytes": 58 << 20},
    )

    if paired:
        vectors = {f"g{k}": shaped(ln1_gain.shape, f32) for k in range(5)}
        done = kernel_call(
            places_kernel,
            "places",
            dict(
                y_in=step["y_out"],
                gx_in=step["grad_x"],
                total=step["total_out"],
                qkv_in=step["w_qkv_g"],
                out_in=step["w_out_g"],
                fc_in=step["w_fc_g"],
                proj_in=step["w_proj_g"],
            ),
            dict(
                y_out=shaped(x_in.shape, f32),
                grad_x=shaped(x_in.shape, f32),
                w_qkv_g=shaped(ins["w_qkv"].shape, f32),
                b_qkv_g=shaped(ins["b_qkv"].shape, f32),
                w_out_g=shaped(w_out.shape, f32),
                w_fc_g=shaped(w_fc.shape, f32),
                b_fc_g=shaped(b_fc.shape, f32),
                w_proj_g=shaped(w_proj.shape, f32),
                **vectors,
            ),
            dict(
                total_v=vm(step["total_out"].shape, f32),
                g_v=vm((5, layers, vec), f32),
                bq_v=vm(ins["b_qkv"].shape, f32),
                bf_v=vm(b_fc.shape, f32),
                qkv_v=vm(ins["w_qkv"].shape, f32),
                fc_v=vm(w_fc.shape, f32),
                proj_v=vm(w_proj.shape, f32),
                out_v=vm(w_out.shape, f32),
                y_v=vm(x_in.shape, f32),
                gx_v=vm(x_in.shape, f32),
                sems=pltpu.SemaphoreType.DMA((20,)),
            ),
            {"vmem_limit_bytes": 58 << 20},
        )
        return (
            (done["y_out"], done["grad_x"])
            + tuple(done[name] for name in vectors)
            + (
                jnp.transpose(done["w_qkv_g"], (0, 2, 1, 3)),
                jnp.transpose(done["b_qkv_g"], (1, 0, 2)),
            )
            + tuple(done[name] for name in ("w_out_g", "w_fc_g", "b_fc_g", "w_proj_g"))
        )

    over_tokens = (((0,), (0,)), ((), ()))
    grads = [[] for _ in range(6)]
    small = step["total_out"][vec_rows:]
    vectors = step["vecs_out"][: 5 * layers].reshape(5, layers, width)
    vectors = lax.dynamic_slice_in_dim(vectors, my_dp * dp_width, dp_width, axis=2)
    for layer in range(layers):
        context_t, act_t, dqkv_t, d_pre_t = (
            step[name][layer] for name in ("ctx_all", "act_all", "dqkv_all", "du_all")
        )
        unit_t = step["cross"][layer, 0].reshape(total_rows, dp_width).astype(f32)
        d_t = step["cross"][layer, 1].reshape(total_rows, dp_width)
        a_t = (unit_t * vectors[0, layer] + vectors[1, layer]).astype(bf16)
        m_t = (unit_t * vectors[2, layer] + vectors[3, layer]).astype(bf16)

        def contract(left, right):
            return lax.dot_general(left, right, over_tokens, preferred_element_type=f32)

        grads[0].append(contract(a_t, dqkv_t).reshape(w_qkv.shape[1:]))
        grads[1].append(small[layer : 3 * layers : layers, : b_qkv.shape[2]])
        grads[2].append(contract(context_t, d_t))
        grads[3].append(contract(m_t, d_pre_t))
        grads[4].append(small[3 * layers + layer, : b_fc.shape[1]])
        grads[5].append(contract(act_t, d_t))
    vector_grads = lax.dynamic_slice_in_dim(
        step["total_out"][: 5 * layers].reshape(layers, 5, dp_width), my_tensor * vec, vec, axis=2
    )
    return (
        (step["y_out"], step["grad_x"])
        + tuple(vector_grads[:, k] for k in range(5))
        + tuple(jnp.stack(group) for group in grads)
    )


def solution(mesh):
    in_specs = (
        P(("dp", "tensor"), None),
        P("dp", None),
        P(None, ("dp", "tensor")),
        P(None, ("dp", "tensor")),
        P(None, ("dp", "tensor")),
        P(None, ("dp", "tensor")),
        P(None, ("dp", "tensor")),
        P(None, "dp", None, "tensor"),
        P(None, None, ("tensor", "dp")),
        P(None, "tensor", "dp"),
        P(None, "dp", "tensor"),
        P(None, ("tensor", "dp")),
        P(None, "tensor", "dp"),
        P(("dp", "tensor"), None),
    )
    out_specs = (
        P(("dp", "tensor"), None),
        P(("dp", "tensor"), None),
        P(None, ("dp", "tensor")),
        P(None, ("dp", "tensor")),
        P(None, ("dp", "tensor")),
        P(None, ("dp", "tensor")),
        P(None, ("dp", "tensor")),
        P(None, "dp", None, "tensor"),
        P(None, None, ("tensor", "dp")),
        P(None, "tensor", "dp"),
        P(None, "dp", "tensor"),
        P(None, ("tensor", "dp")),
        P(None, "tensor", "dp"),
    )
    return jax.shard_map(
        per_device, mesh=mesh, in_specs=in_specs, out_specs=out_specs, check_vma=False
    )
```

```python
import functools
import types

import jax
import jax.numpy as jnp
from jax import lax
from jax.experimental import pallas as pl
from jax.experimental.pallas import tpu as pltpu
from jax.sharding import PartitionSpec as P

HD = 64
ROT = 16


EPS = 1e-05
NEG_FILL = -1e30


def gelu_exact(values):
    return 0.5 * values * (1.0 + jax.scipy.special.erf(values * 0.7071067811865476))


def gelu_slope(values):
    normal_cdf = 0.5 * (1.0 + jax.scipy.special.erf(values * 0.7071067811865476))
    return normal_cdf + values * jnp.exp(-0.5 * values * values) * 0.3989422804014327


MESH = pl.DeviceIdType.MESH
ANY = pl.BlockSpec(memory_space=pl.ANY)
VMEM = pl.BlockSpec(memory_space=pltpu.VMEM)


def copy_counts(n_dp, n_tensor, layers):
    chips = n_dp // 2
    remote = (n_tensor - 1) * (6 * layers + 2) + (n_dp - 1) * 3
    if chips == 4:
        remote = remote + layers * (4 * 13 + 4 * 3 + 2 * 3 + 4)
        again = (n_tensor - 1) * (3 * layers) + 15 * layers + n_dp - 4
        return remote, remote - again, 14 * layers + 14
    remote = remote + layers * (8 * (4 * chips - 3) + 2 * (n_dp - 1))
    return remote, remote, 10 * layers + 15


class Links:
    def __init__(self, n_dp, n_tensor, send_sems, recv_sems, local_sems):
        self.n_dp, self.n_tensor = n_dp, n_tensor
        self.dp, self.tensor = lax.axis_index("dp"), lax.axis_index("tensor")
        self.core, self.chip = lax.rem(self.dp, 2), self.dp // 2
        self.partner = self.dp + 1 - 2 * self.core
        self.paired = n_dp == 8
        if self.paired:
            self.gather_y, self.gather_x = Turn(self, False), Turn(self, True)
        self.send_sems, self.recv_sems, self.local_sems = send_sems, recv_sems, local_sems
        self.used, self.used_local, self.used_send = 0, 0, 0
        self.sent, self.free = [], []

    def send(self, src, dst, **where):
        if self.free:
            place = self.free.pop(0)
        else:
            place = self.used_send
            self.used_send += 1
        copy = pltpu.make_async_remote_copy(
            src_ref=src,
            dst_ref=dst,
            send_sem=self.send_sems.at[place],
            recv_sem=self.recv_sems.at[self.used],
            device_id=where,
            device_id_type=MESH,
        )
        self.used += 1
        copy.start()
        self.sent.append((copy, place))
        return copy

    def local(self, src, dst):
        copy = pltpu.make_async_copy(src, dst, self.local_sems.at[self.used_local])
        self.used_local += 1
        copy.start()
        return copy

    def dp_peer(self, step):
        return lax.rem(self.dp + step, self.n_dp)

    def tensor_peer(self, step):
        return lax.rem(self.tensor + step, self.n_tensor)

    def enter(self):
        sem = pltpu.get_barrier_semaphore()
        for step in range(1, self.n_tensor):
            pl.semaphore_signal(
                sem, inc=1, device_id={"tensor": self.tensor_peer(step)}, device_id_type=MESH
            )
        for step in range(1, self.n_dp):
            pl.semaphore_signal(
                sem, inc=1, device_id={"dp": self.dp_peer(step)}, device_id_type=MESH
            )

    def barrier(self):
        pl.semaphore_wait(pltpu.get_barrier_semaphore(), self.n_tensor + self.n_dp - 2)

    def settle(self, count):
        for copy, place in self.sent[:count]:
            copy.wait_send()
            self.free.append(place)
        self.sent = self.sent[count:]

    def finish(self):
        for copy, _ in self.sent:
            copy.wait_send()


class Turn:
    def __init__(self, links, gather_x):
        x, y = lax.rem(links.chip, 2), links.chip // 2
        over = (links.dp + 2 - 4 * x, lax.rem(links.dp + 4, 8))
        self.gather_x = gather_x
        self.gather_dp, self.sum_dp = over if gather_x else over[::-1]
        self.along, self.apart = (x, y) if gather_x else (y, x)
        self.place = self.along * 2 + links.core
        self.far_place = lax.rem(self.place + 2, 4)

    def block(self, place, apart):
        if self.gather_x:
            return apart * 4 + place
        return place // 2 * 4 + 2 * apart + lax.rem(place, 2)


class DpGather:
    def __init__(self, links, own, slot, axis=0):
        self.links, self.own, self.slot = links, own, slot
        self.chips = links.n_dp // 2
        self.core, self.chip, self.partner = links.core, links.chip, links.partner
        self.relays = self.chips == 4
        rows = own.shape[axis] // 2
        self.halves = [
            (slice(None),) * axis + (pl.ds(half * rows, rows),) for half in range(2)
        ]
        self.passed = []
        if self.relays:
            near = self.chip + 1 - 2 * lax.rem(self.chip, 2)
            far = lax.rem(self.chip + 2, 4)
            self.across = lax.rem(near + 2, 4)
            self.order = ((near, far), (far, near))

    def device(self, chip):
        return chip * 2 + self.core

    def out(self, rows, chip):
        return self.links.send(
            self.own.at[rows], self.slot(self.links.dp).at[rows], dp=self.device(chip)
        )

    def pass_on(self, rows, chip, target):
        block = self.slot(self.device(chip)).at[rows]
        return self.links.send(block, block, dp=target)

    def start(self):
        if self.relays:
            self.first = [self.out(rows, order[0]) for rows, order in zip(self.halves, self.order)]
            self.second = [self.out(rows, order[1]) for rows, order in zip(self.halves, self.order)]
        else:
            self.direct = [
                [self.out(rows, lax.rem(self.chip + step, self.chips)) for rows in self.halves]
                for step in range(1, self.chips)
            ]
        own_slot = self.slot(self.links.dp)
        self.passed.append(self.links.send(self.own, own_slot, dp=self.partner))
        self.kept = self.links.local(self.own, own_slot)

    def relay(self):
        if not self.relays:
            return
        self.relayed = []
        for copy, rows, order in zip(self.first, self.halves, self.order):
            copy.wait_recv()
            self.relayed.append(self.pass_on(rows, order[0], self.device(order[1])))
            self.passed.append(self.pass_on(rows, order[0], self.partner))

    def rest(self):
        if not self.relays:
            for step, copies in enumerate(self.direct):
                origin = lax.rem(self.chip + self.chips - step - 1, self.chips)
                for copy, rows in zip(copies, self.halves):
                    copy.wait_recv()
                    self.passed.append(self.pass_on(rows, origin, self.partner))
            return
        for copy, rows, order in zip(self.second, self.halves, self.order):
            copy.wait_recv()
            self.passed.append(self.pass_on(rows, order[1], self.partner))
        for copy, rows in zip(self.relayed, self.halves):
            copy.wait_recv()
            self.passed.append(self.pass_on(rows, self.across, self.partner))

    def finish(self):
        for copy in self.passed:
            copy.wait_recv()
        self.kept.wait()


class PairGather:
    def __init__(self, links, turn, own, slot):
        self.links, self.turn, self.own, self.slot = links, turn, own, slot

    def start(self):
        links, here = self.links, self.slot(self.turn.place)
        self.out = links.send(self.own, here, dp=self.turn.gather_dp)
        self.passed = [links.send(self.own, here, dp=links.partner)]
        self.kept = links.local(self.own, here)

    def rest(self):
        self.out.wait_recv()
        block = self.slot(self.turn.far_place)
        self.passed.append(self.links.send(block, block, dp=self.links.partner))

    def finish(self):
        for copy in self.passed:
            copy.wait_recv()
        self.kept.wait()


class Group:
    def __init__(self, *gathers):
        self.gathers = gathers

    def start(self):
        for gather in self.gathers:
            gather.start()

    def relay(self):
        for gather in self.gathers:
            gather.relay()

    def rest(self):
        for gather in self.gathers:
            gather.rest()

    def finish(self):
        for gather in self.gathers:
            gather.finish()


class Pump:
    def __init__(self):
        self.todo, self.started, self.relayed, self.every = [], [], [], []

    def add(self, group):
        self.todo.append(group)
        self.every.append(group)
        if not self.started:
            self.start()

    def start(self):
        if self.todo:
            group = self.todo.pop(0)
            group.start()
            self.started.append(group)

    def relay(self):
        group = self.started.pop(0)
        group.relay()
        self.relayed.append(group)
        if not self.started:
            self.start()

    def rest(self):
        self.relayed.pop(0).rest()


def row_slot(ref, rows):
    return lambda d: ref.at[pl.ds(pl.multiple_of(d * rows, rows), rows)]


def middle_slot(ref, rows):
    return lambda d: ref.at[:, pl.ds(pl.multiple_of(d * rows, rows), rows)]


def column_slot(ref, size):
    return lambda d: ref.at[:, pl.ds(pl.multiple_of(d * size, size), size)]


def lead_slot(ref):
    return lambda d: ref.at[d]


class Scatter:
    def __init__(self, links, part, landing):
        self.links, self.part, self.landing = links, part, landing
        self.rows = landing.shape[1]
        slot = row_slot(part, self.rows)
        self.copies = [
            links.send(
                slot(links.tensor_peer(step)),
                landing.at[step - 1],
                tensor=links.tensor_peer(step),
            )
            for step in range(1, links.n_tensor)
        ]

    def total(self):
        own = pl.ds(pl.multiple_of(self.links.tensor * self.rows, self.rows), self.rows)
        total = self.part[own, :].astype(jnp.float32)
        for step, copy in enumerate(self.copies):
            copy.wait_recv()
            total = total + self.landing[step].astype(jnp.float32)
        return total


class Spread:
    def __init__(self, links, ref, value):
        rows = value.shape[0]
        self.links, self.here = links, row_slot(ref, rows)(links.tensor)
        ref[pl.ds(pl.multiple_of(links.tensor * rows, rows), rows), :] = value

    def send(self):
        links = self.links
        self.copies = [
            links.send(self.here, self.here, tensor=links.tensor_peer(step))
            for step in range(1, links.n_tensor)
        ]

    def finish(self):
        for copy in self.copies:
            copy.wait_recv()


class Cross:
    def __init__(self, links, turn, stage, out, value):
        self.links, self.turn, self.stage, self.out = links, turn, stage, out
        self.count, _, width = stage.shape
        self.me = turn.place if links.paired else links.dp
        if not links.paired:
            for d in range(self.count):
                stage[d] = value[:, d * width : (d + 1) * width]
            return
        half = width // 2
        wide = value.astype(jnp.float32)
        for s in range(self.count):
            at = [
                (apart * 4 + s if turn.gather_x else s // 2 * 4 + 2 * apart + s % 2) * half
                for apart in range(2)
            ]
            one, two = (wide[:, place : place + half] for place in at)
            stage[s, :, 0:half] = jnp.where(turn.apart == 0, one, two).astype(value.dtype)
            stage[s, :, half:width] = jnp.where(turn.apart == 0, two, one).astype(value.dtype)

    def send(self):
        links, stage = self.links, self.stage
        here = self.out.at[self.me, links.tensor]
        self.copies = []
        for step in range(1, self.count):
            peer = lax.rem(self.me + step, self.count)
            device = self.turn.block(peer, self.turn.apart) if links.paired else peer
            self.copies.append(links.send(stage.at[peer], here, dp=device))
        self.kept = links.local(stage.at[self.me], here)

    def forward(self):
        links = self.links
        for copy in self.copies:
            copy.wait_recv()
        self.kept.wait()
        mine = self.out.at[:, links.tensor]
        self.wide = [
            links.send(mine, mine, tensor=links.tensor_peer(step))
            for step in range(1, links.n_tensor)
        ]

    def finish(self):
        for copy in self.wide:
            copy.wait_recv()


class Product:
    def __init__(self, links, turn, own, away, landing, rows, columns):
        self.own, self.landing = own, landing
        parts = own.shape[0] if len(own.shape) == 3 else 1
        half, width = own.shape[-2:]
        for k in range(parts):
            total = dot_tn(rows, columns[:, k * width : (k + 1) * width])
            if len(own.shape) == 3:
                own[k] = total[:half]
                away[k] = total[half:].astype(away.dtype)
            else:
                own[...] = total[:half]
                away[...] = total[half:].astype(away.dtype)
        self.copy = links.send(away, landing, dp=turn.sum_dp)

    def total(self):
        self.copy.wait_recv()
        return self.own[...] + self.landing[...].astype(jnp.float32)


def unit_rows(values):
    average = jnp.mean(values, axis=-1, keepdims=True)
    centred = values - average
    variance = jnp.mean(centred * centred, axis=-1, keepdims=True)
    scale = lax.rsqrt(variance + EPS)
    return centred * scale, scale


def back_unit(values, grad):
    unit, scale = unit_rows(values)
    return scale * (
        grad
        - jnp.mean(grad, axis=-1, keepdims=True)
        - unit * jnp.mean(grad * unit, axis=-1, keepdims=True)
    )


def dot_nn(left, right):
    return jnp.dot(left, right, preferred_element_type=jnp.float32)


def dot_nt(left, right):
    return lax.dot_general(left, right, (((1,), (1,)), ((), ())), preferred_element_type=jnp.float32)


def dot_tn(left, right):
    return lax.dot_general(left, right, (((0,), (0,)), ((), ())), preferred_element_type=jnp.float32)


def turn(vectors, same, up, down, sign):
    width = vectors.shape[1]
    above = pltpu.roll(vectors, width - ROT // 2, 1)
    below = pltpu.roll(vectors, ROT // 2, 1)
    return vectors * same + sign * (above * up + below * down)


def head_scores(query, key, mask):
    scores = dot_nt(query, key) * HD ** (-0.5)
    scores = jnp.where(mask, scores, NEG_FILL)
    terms = jnp.exp(scores - jnp.max(scores, axis=-1, keepdims=True))
    return terms / jnp.sum(terms, axis=-1, keepdims=True)


def layout_tables(r):
    f32 = jnp.float32
    rows, width = r.same.shape
    lengths = r.lens_v[...]
    row_of = lax.broadcasted_iota(jnp.int32, (rows, rows), 0)
    col_of = lax.broadcasted_iota(jnp.int32, (rows, rows), 1)
    row_lane = lax.broadcasted_iota(jnp.int32, (rows, 128), 0)
    start = jnp.zeros((rows, rows), jnp.int32)
    start_lane = jnp.zeros((rows, 128), jnp.int32)
    end = jnp.zeros((1, 1), jnp.int32)
    for k in range(lengths.shape[1]):
        end = end + lengths[:, k : k + 1]
        start = jnp.where(row_of >= end, end, start)
        start_lane = jnp.where(row_lane >= end, end, start_lane)
    r.mask[...] = jnp.where((col_of >= start) & (col_of <= row_of), 1.0, 0.0)
    positions = (row_lane - start_lane).astype(f32)
    lane = lax.rem(lax.broadcasted_iota(jnp.int32, (1, 128), 1), HD)
    half = ROT // 2
    inverse = jnp.power(10000.0, -2.0 * lax.rem(lane, half).astype(f32) / ROT)
    angles = positions * inverse
    cos_tab, sin_tab = jnp.cos(angles), jnp.sin(angles)
    same = jnp.where(lane < ROT, cos_tab, 1.0)
    up = jnp.where(lane < half, -sin_tab, 0.0)
    down = jnp.where((lane >= half) & (lane < ROT), sin_tab, 0.0)
    for ref, table in ((r.same, same), (r.up, up), (r.down, down)):
        for place in range(width // 128):
            ref[:, place * 128 : (place + 1) * 128] = table


def gain_rows(r, layer):
    layers = r.resid.shape[0]
    return tuple(r.vecs[k * layers + layer : k * layers + layer + 1, :] for k in range(5))


def forward_attention(r, layer):
    bf16 = jnp.bfloat16
    g1, b1, _, _, _ = gain_rows(r, layer)
    layers, _, part = r.ctx.shape
    normed_a = (r.unit[layer].astype(jnp.float32) * g1 + b1).astype(bf16)
    tables = (r.same[...], r.up[...], r.down[...])
    for which in range(3):
        row = which * layers + layer
        block = dot_nn(normed_a, r.wq[layer, which]) + r.bq[row : row + 1, :]
        if which < 2:
            block = turn(block, *tables, 1.0)
        r.qkv[layer, :, which * part : (which + 1) * part] = block.astype(bf16)
    allowed = r.mask[...] > 0.0
    for head in range(part // HD):
        q, k, v = (
            r.qkv[layer, :, which * part + head * HD : which * part + (head + 1) * HD]
            for which in range(3)
        )
        probs = head_scores(q, k, allowed).astype(bf16)
        r.ctx[layer, :, head * HD : (head + 1) * HD] = dot_nn(probs, v).astype(bf16)


def forward_hidden(r, layer):
    bf16 = jnp.bfloat16
    _, _, g2, b2, _ = gain_rows(r, layer)
    normed_m = (r.unit[layer].astype(jnp.float32) * g2 + b2).astype(bf16)
    hidden = dot_nn(normed_m, r.wf[layer]) + r.bf[layer : layer + 1, :]
    r.pre[layer] = hidden
    r.act[layer] = gelu_exact(hidden).astype(bf16)


def forward_part(r, layer):
    r.part_f[layer] = (
        dot_nn(r.ctx[layer], r.wo[layer]) + dot_nn(r.act[layer], r.wp[layer])
    ).astype(jnp.bfloat16)


def backward_hidden(r, layer):
    bf16 = jnp.bfloat16
    r.dctx[...] = dot_nt(r.drows[layer], r.wo[layer]).astype(bf16)
    d_pre = dot_nt(r.drows[layer], r.wp[layer]) * gelu_slope(r.pre[layer])
    r.sums_f[layer : layer + 1, :] = jnp.sum(d_pre, axis=0, keepdims=True)
    r.du[layer] = d_pre.astype(bf16)


def backward_attention(r, layer):
    bf16, f32 = jnp.bfloat16, jnp.float32
    part = r.ctx.shape[2]
    allowed = r.mask[...] > 0.0
    pieces = [[], [], []]
    for head in range(part // HD):
        here = slice(head * HD, (head + 1) * HD)
        q, k, v = (
            r.qkv[layer, :, which * part + head * HD : which * part + (head + 1) * HD]
            for which in range(3)
        )
        dc = r.dctx[:, here]
        probs = head_scores(q, k, allowed)
        delta = jnp.sum(
            dc.astype(f32) * r.ctx[layer, :, here].astype(f32), axis=-1, keepdims=True
        )
        d_scaled = (probs * (dot_nt(dc, v) - delta) * HD ** (-0.5)).astype(bf16)
        pieces[0].append(dot_nn(d_scaled, k))
        pieces[1].append(dot_tn(d_scaled, q))
        pieces[2].append(dot_tn(probs.astype(bf16), dc))
    tables = (r.same[...], r.up[...], r.down[...])
    for which in range(3):
        block = jnp.concatenate(pieces[which], axis=1)
        if which < 2:
            block = turn(block, *tables, -1.0)
        row = which * r.ctx.shape[0] + layer
        r.sums_q[row : row + 1, :] = jnp.sum(block, axis=0, keepdims=True)
        r.dqkv[layer, :, which * part : (which + 1) * part] = block.astype(bf16)


def backward_part(r, layer):
    g1, _, g2, _, _ = gain_rows(r, layer)
    part = r.ctx.shape[2]
    d_a = sum(
        dot_nt(r.dqkv[layer, :, which * part : (which + 1) * part], r.wq[layer, which])
        for which in range(3)
    )
    d_m = dot_nt(r.du[layer], r.wf[layer])
    r.part_e[layer] = (d_a * g1 + d_m * g2).astype(jnp.bfloat16)
    wide = r.unit[layer].astype(jnp.float32)
    for row, term in enumerate((d_a * wide, d_a, d_m * wide, d_m)):
        r.sums[5 * layer + row : 5 * layer + row + 1, :] = jnp.sum(term, axis=0, keepdims=True)


def pack_small(r, links):
    count, layers, vec = r.sv.shape
    r.pack_v[...] = jnp.zeros_like(r.pack_v)
    owner = lax.broadcasted_iota(jnp.int32, (layers, vec * links.n_tensor), 1) // vec
    for k in range(count):
        value = jnp.concatenate([r.sv[k]] * links.n_tensor, axis=1)
        r.pack_v[k * layers : (k + 1) * layers, :] = jnp.where(owner == links.tensor, value, 0.0)
    r.pack_b[...] = jnp.zeros_like(r.pack_b)
    for which in range(3):
        r.pack_b[which * layers : (which + 1) * layers, 0 : r.sq.shape[2]] = r.sq[which]
    r.pack_b[3 * layers : 4 * layers, 0 : r.sf.shape[1]] = r.sf[...]


def unpack_small(r, links):
    layers = r.sf.shape[0]
    width = r.vec_all.shape[2]
    rows = 0
    for d in range(links.n_dp):
        r.vecs[:, d * width : (d + 1) * width] = r.vec_all[d]
    for ref, height, lanes in ((r.bq, 3 * layers, r.sq.shape[2]), (r.bf, layers, r.sf.shape[1])):
        ref[0:height, :] = jnp.concatenate(
            [r.small_b[d, rows : rows + height, 0:lanes] for d in range(links.n_dp)], axis=1
        )
        rows = rows + height


def in_columns(r, links, layer):
    for blocks, whole in ((r.wo_blocks, r.wo), (r.wp_blocks, r.wp)):
        width = blocks.shape[3]
        for d in range(links.n_dp):
            whole[layer, :, d * width : (d + 1) * width] = blocks[layer, d]


def start_sums(r, links):
    layers = r.resid.shape[0]
    width = r.sums_stage.shape[2]
    rows = r.sums.shape[0]
    lanes_q, lanes_f = r.sq.shape[2], r.sf.shape[1]
    r.sums_stage[...] = jnp.zeros_like(r.sums_stage)
    for d in range(links.n_dp):
        r.sums_stage[d, 0:rows, :] = r.sums[:, d * width : (d + 1) * width]
        r.sums_stage[d, rows : rows + 3 * layers, 0:lanes_q] = r.sums_q[
            0 : 3 * layers, d * lanes_q : (d + 1) * lanes_q
        ]
        r.sums_stage[d, rows + 3 * layers : rows + 4 * layers, 0:lanes_f] = r.sums_f[
            0:layers, d * lanes_f : (d + 1) * lanes_f
        ]
    return [
        links.send(
            r.sums_stage.at[links.dp_peer(step)], r.land_s.at[step - 1], dp=links.dp_peer(step)
        )
        for step in range(1, links.n_dp)
    ]


def middle_sums(r, links, sent):
    rows = r.sums.shape[0]
    total = r.sums_stage[links.dp]
    for step, copy in enumerate(sent):
        copy.wait_recv()
        total = total + r.land_s[step]
    r.total_v[...] = total
    r.half[...] = total[0:rows]
    return [
        links.send(r.half, r.land_t.at[step - 1], tensor=links.tensor_peer(step))
        for step in range(1, links.n_tensor)
    ]


def end_sums(r, links, sent):
    rows = r.sums.shape[0]
    total = r.half[...]
    for step, copy in enumerate(sent):
        copy.wait_recv()
        total = total + r.land_t[step]
    r.total_v[0:rows, :] = total
    return links.local(r.total_v, r.total_out)


def token_rows(r, layer, which):
    block = r.cross[layer, which]
    return block.reshape(-1, block.shape[-1])


def product_turn(links, layer, which):
    if not links.paired:
        return None
    return links.gather_y if (layer, which) == (0, 1) else links.gather_x


def normed_rows(r, links, layer, norm):
    layers = r.resid.shape[0]
    half = r.cross.shape[-1] // 2
    gain, bias = (
        jnp.concatenate(
            [
                r.vecs[row : row + 1, pl.ds(pl.multiple_of(d * half, half), half)]
                for d in (links.dp, product_turn(links, layer, 0).sum_dp)
            ],
            axis=1,
        )
        for row in (2 * norm * layers + layer, (2 * norm + 1) * layers + layer)
    )
    unit = token_rows(r, layer, 0).astype(jnp.float32)
    return (unit * gain + bias).astype(jnp.bfloat16)


class Products:
    def __init__(self, r, links):
        self.r, self.links, self.stores = r, links, []

    def columns(self, ref, layer):
        block = ref[layer]
        return block.reshape(-1, block.shape[-1])

    def outputs(self, layer):
        r = self.r
        d_t = token_rows(r, layer, 1)
        return [
            Product(
                self.links, product_turn(self.links, layer, 1), own.at[layer], away.at[layer], land.at[layer], d_t,
                self.columns(columns, layer),
            )
            for own, away, land, columns in (
                (r.go_own, r.go_away, r.go_land, r.ctx_all),
                (r.gp_own, r.gp_away, r.gp_land, r.act_all),
            )
        ]

    def hidden(self, layer):
        r = self.r
        return Product(
            self.links, product_turn(self.links, layer, 0), r.gf_own.at[layer], r.gf_away.at[layer], r.gf_land.at[layer],
            normed_rows(r, self.links, layer, 1), self.columns(r.du_all, layer),
        )

    def heads(self, layer):
        r = self.r
        return Product(
            self.links, product_turn(self.links, layer, 0), r.gq_own.at[layer], r.gq_away.at[layer], r.gq_land.at[layer],
            normed_rows(r, self.links, layer, 0), self.columns(r.dqkv_all, layer),
        )

    def store_outputs(self, layer, products):
        r = self.r
        for product, turned, out in zip(products, (r.go_v, r.gp_v), (r.w_out_g, r.w_proj_g)):
            turned[layer] = jnp.transpose(product.total())
            self.stores.append(self.links.local(turned.at[layer], out.at[layer]))

    def store(self, layer, product, out):
        product.own[...] = product.total()
        self.stores.append(self.links.local(product.own, out.at[layer]))


def make_cross(r, links, layer, which, value):
    turn = product_turn(links, layer, which)
    return Cross(links, turn, r.stage.at[layer, which], r.cross.at[layer, which], value)


def layers_kernel(n_dp, n_tensor, names, *refs):
    r = types.SimpleNamespace(**dict(zip(names, refs)))
    links = Links(n_dp, n_tensor, r.send_sems, r.recv_sems, r.local_sems)
    bf16 = jnp.bfloat16
    layers = r.w_out.shape[0]
    last = layers - 1
    columns_ok = not hasattr(r, "wo_blocks")
    links.enter()
    x_load = links.local(r.x_in, r.resid.at[0])
    d_load = links.local(r.grad_out, r.dres.at[last])
    loads = [links.local(r.lens, r.lens_v)]
    for k, ref in enumerate((r.ln1_gain, r.ln1_bias, r.ln2_gain, r.ln2_bias, r.res_bias)):
        loads.append(links.local(ref, r.sv.at[k]))
    loads.append(links.local(r.b_qkv, r.sq))
    loads.append(links.local(r.b_fc, r.sf))

    qkv_g, fc_g, proj_g, fwd_g, du_g, dqkv_g = [], [], [], [], [], []
    for layer in range(layers):
        dp_width = r.w_qkv.shape[2]
        qkv_g.append(
            Group(DpGather(links, r.w_qkv.at[layer], middle_slot(r.wq.at[layer], dp_width), 1))
        )
        if columns_ok:
            slots = [column_slot(ref.at[layer], dp_width) for ref in (r.wo, r.wp)]
        else:
            slots = [lead_slot(ref.at[layer]) for ref in (r.wo_blocks, r.wp_blocks)]
        out_j = DpGather(links, r.w_out.at[layer], slots[0])
        fc_j = DpGather(links, r.w_fc.at[layer], row_slot(r.wf.at[layer], dp_width))
        fc_g.append(Group(out_j, fc_j))
        proj_g.append(Group(DpGather(links, r.w_proj.at[layer], slots[1])))
        rows = r.ctx.shape[1]
        ctx_j, act_j, dqkv_j, du_j = (
            PairGather(
                links, product_turn(links, layer, which), own.at[layer], lead_slot(whole.at[layer])
            )
            if links.paired
            else DpGather(links, own.at[layer], row_slot(whole.at[layer], rows))
            for own, whole, which in (
                (r.ctx, r.ctx_all, 1),
                (r.act, r.act_all, 1),
                (r.dqkv, r.dqkv_all, 0),
                (r.du, r.du_all, 0),
            )
        )
        fwd_g.append(Group(ctx_j, act_j))
        du_g.append(Group(du_j))
        dqkv_g.append(Group(dqkv_j))

    x_load.wait()
    unit = unit_rows(r.resid[0])[0].astype(bf16)
    unit_s = Spread(links, r.unit.at[0], unit)
    for load in loads:
        load.wait()
    pack_small(r, links)
    d_load.wait()
    d_bf = r.dres[last].astype(bf16)
    rows_s = Spread(links, r.drows.at[last], d_bf)
    crosses = [
        make_cross(r, links, 0, 0, unit),
        make_cross(r, links, last, 1, d_bf),
    ]
    r.sums[...] = jnp.zeros_like(r.sums)
    layout_tables(r)
    links.barrier()

    vec_sent = [
        links.send(r.pack_v, r.land_v.at[step - 1], tensor=links.tensor_peer(step))
        for step in range(1, n_tensor)
    ]
    b_here = r.small_b.at[links.dp]
    small_sent = [
        links.send(r.pack_b, b_here, dp=links.dp_peer(step)) for step in range(1, n_dp)
    ]
    small_kept = links.local(r.pack_b, b_here)
    pump = Pump()
    for layer in range(layers):
        for group in (qkv_g[layer], fc_g[layer], proj_g[layer]):
            pump.add(group)
    unit_s.send()
    crosses[0].send()
    total = r.pack_v[...]
    for step, copy in enumerate(vec_sent):
        copy.wait_recv()
        total = total + r.land_v[step]
    r.vec_all[links.dp] = total
    vec_here = r.vec_all.at[links.dp]
    vec_wide = [
        links.send(vec_here, vec_here, dp=links.dp_peer(step)) for step in range(1, n_dp)
    ]
    rows_s.send()
    pump.relay()
    crosses[1].send()
    small_kept.wait()
    for copy in small_sent + vec_wide:
        copy.wait_recv()
    unpack_small(r, links)

    for layer in range(layers):
        pump.rest()
        qkv_g[layer].finish()
        if layer == 0:
            crosses[0].forward()
        else:
            pump.relay()
        unit_s.finish()
        forward_attention(r, layer)
        if layer == 0:
            pump.relay()
            crosses[1].forward()
        pump.rest()
        fc_g[layer].finish()
        forward_hidden(r, layer)
        if layer > 0:
            crosses[-1].forward()
        if not links.paired:
            pump.add(fwd_g[layer])
        pump.relay()
        pump.rest()
        if links.paired and layer == last:
            fwd_g[last].start()
            fwd_g[0].start()
        proj_g[layer].finish()
        if not columns_ok:
            in_columns(r, links, layer)
        forward_part(r, layer)
        if layer < last:
            scatter = Scatter(links, r.part_f.at[layer], r.land_f.at[layer])
            pump.relay()
            values = r.resid[layer] + scatter.total() + gain_rows(r, layer)[4]
            r.resid[layer + 1] = values
            unit = unit_rows(values)[0].astype(bf16)
            unit_s = Spread(links, r.unit.at[layer + 1], unit)
            settled = len(links.sent)
            unit_s.send()
            crosses.append(make_cross(r, links, layer + 1, 0, unit))
            crosses[-1].send()

    if links.paired:
        links.settle(settled)
        finish = backward_paired
    else:
        finish = backward_gathered
    stores = finish(r, links, pump, fwd_g, du_g, dqkv_g, crosses, rows_s)
    for store in stores:
        store.wait()
    links.finish()
    counts = (links.used, links.used_send, links.used_local)
    assert counts == copy_counts(n_dp, n_tensor, layers), counts


def start_back(r, links, layer):
    backward_part(r, layer)
    scatter = Scatter(links, r.part_e.at[layer], r.land_e.at[layer])
    r.sums[5 * layer + 4 : 5 * layer + 5, :] = jnp.sum(r.dres[layer], axis=0, keepdims=True)
    return scatter


def step_back(r, links, layer, scatter, crosses):
    new_d = r.dres[layer] + back_unit(r.resid[layer], scatter.total())
    r.dres[layer - 1] = new_d
    d_bf = new_d.astype(jnp.bfloat16)
    rows_s = Spread(links, r.drows.at[layer - 1], d_bf)
    rows_s.send()
    crosses.append(make_cross(r, links, layer - 1, 1, d_bf))
    crosses[-1].send()
    return rows_s


def store_y(r, links, scatter):
    last = r.resid.shape[0] - 1
    r.y_v[...] = r.resid[last] + scatter.total() + gain_rows(r, last)[4]
    return links.local(r.y_v, r.y_out)


def store_grad_x(r, links, scatter):
    r.gx_v[...] = r.dres[0] + back_unit(r.resid[0], scatter.total())
    return links.local(r.gx_v, r.grad_x)


def backward_paired(r, links, pump, fwd_g, du_g, dqkv_g, crosses, rows_s):
    layers = r.resid.shape[0]
    last = layers - 1
    products = Products(r, links)
    done = []
    for layer in reversed(range(1, layers)):
        rows_s.finish()
        backward_hidden(r, layer)
        backward_attention(r, layer)
        scatter = start_back(r, links, layer)
        du_g[layer].start()
        if layer == last:
            for cross in crosses:
                cross.finish()
        rows_s = step_back(r, links, layer, scatter, crosses)
        fwd_g[layer].rest()
        dqkv_g[layer].start()
        if layer > 1:
            fwd_g[layer - 1].start()
        fwd_g[layer].finish()
        outputs = products.outputs(layer)
        du_g[layer].rest()
        du_g[layer].finish()
        hidden = products.hidden(layer)
        done.append((layer, outputs, hidden))
        if layer > 1:
            crosses[-1].forward()
    fwd_g[0].rest()
    rows_s.finish()
    crosses[-1].forward()
    backward_hidden(r, 0)
    du_g[0].start()
    for layer in reversed(range(1, layers)):
        dqkv_g[layer].rest()
        dqkv_g[layer].finish()
    late = [(layer, products.heads(layer)) for layer in reversed(range(1, layers))]
    backward_attention(r, 0)
    dqkv_g[0].start()
    scatter = start_back(r, links, 0)
    sums_sent = start_sums(r, links)
    for layer, outputs, _ in done:
        products.store_outputs(layer, outputs)
    for cross in crosses[layers + 1 :]:
        cross.finish()
    fwd_g[0].finish()
    outputs = products.outputs(0)
    du_g[0].rest()
    du_g[0].finish()
    hidden = products.hidden(0)
    sent_y = Scatter(links, r.part_f.at[last], r.land_f.at[last])
    dqkv_g[0].rest()
    for layer, _, product in done:
        products.store(layer, product, r.w_fc_g)
    dqkv_g[0].finish()
    heads = products.heads(0)
    sums_wide = middle_sums(r, links, sums_sent)
    stores = [store_grad_x(r, links, scatter)]
    for layer, product in late:
        products.store(layer, product, r.w_qkv_g)
    products.store_outputs(0, outputs)
    stores.append(end_sums(r, links, sums_wide))
    stores.append(store_y(r, links, sent_y))
    products.store(0, hidden, r.w_fc_g)
    products.store(0, heads, r.w_qkv_g)
    return stores + products.stores


def backward_gathered(r, links, pump, fwd_g, du_g, dqkv_g, crosses, rows_s):
    layers = r.resid.shape[0]
    last = layers - 1
    sent_y = Scatter(links, r.part_f.at[last], r.land_f.at[last])
    for layer in reversed(range(layers)):
        rows_s.finish()
        backward_hidden(r, layer)
        pump.add(du_g[layer])
        if layer == last:
            pump.relay()
        else:
            crosses[-1].forward()
        backward_attention(r, layer)
        pump.add(dqkv_g[layer])
        scatter = start_back(r, links, layer)
        if layer == 0:
            sums_sent = start_sums(r, links)
        pump.rest()
        pump.relay()
        if layer > 0:
            rows_s = step_back(r, links, layer, scatter, crosses)
            pump.rest()
            pump.relay()

    stores = [store_grad_x(r, links, scatter), store_y(r, links, sent_y)]
    stores.append(links.local(r.vecs, r.vecs_out))
    sums_wide = middle_sums(r, links, sums_sent)
    while pump.relayed or pump.started:
        if pump.relayed:
            pump.rest()
        if pump.started:
            pump.relay()
    stores.append(end_sums(r, links, sums_wide))
    for group in fwd_g + du_g + dqkv_g:
        group.finish()
    for cross in crosses:
        cross.finish()
    return stores


def places_kernel(names, *refs):
    r = types.SimpleNamespace(**dict(zip(names, refs)))
    tensor = lax.axis_index("tensor")
    count = [0]

    def local(src, dst):
        copy = pltpu.make_async_copy(src, dst, r.sems.at[count[0]])
        count[0] += 1
        copy.start()
        return copy

    load = local(r.total, r.total_v)
    layered = (
        (r.qkv_in, r.qkv_v, r.w_qkv_g),
        (r.fc_in, r.fc_v, r.w_fc_g),
        (r.proj_in, r.proj_v, r.w_proj_g),
        (r.out_in, r.out_v, r.w_out_g),
    )
    pieces = [
        tuple(ref.at[layer] for ref in refs)
        for layer in range(r.w_fc_g.shape[0])
        for refs in layered
    ]
    pieces += [(r.y_in, r.y_v, r.y_out), (r.gx_in, r.gx_v, r.grad_x)]
    moves = [(local(source, held), held, out) for source, held, out in pieces]
    stores = []
    load.wait()
    layers, vec = r.g0.shape
    width = r.total.shape[1]
    rolled = pltpu.roll(r.total_v[...], lax.rem(width - tensor * vec, width), 1)
    for k, out in enumerate((r.g0, r.g1, r.g2, r.g3, r.g4)):
        for layer in range(layers):
            r.g_v[k, layer : layer + 1, :] = rolled[5 * layer + k : 5 * layer + k + 1, 0:vec]
        stores.append(local(r.g_v.at[k], out))
    rows = -(-5 * layers // 8) * 8
    for which in range(3):
        at = rows + which * layers
        r.bq_v[which] = r.total_v[at : at + layers, 0 : r.bq_v.shape[2]]
    at = rows + 3 * layers
    r.bf_v[...] = r.total_v[at : at + layers, 0 : r.bf_v.shape[1]]
    stores.append(local(r.bq_v, r.b_qkv_g))
    stores.append(local(r.bf_v, r.b_fc_g))
    for move, held, out in moves:
        move.wait()
        stores.append(local(held, out))
    for store in stores:
        store.wait()


def shaped(shape, dtype):
    return jax.ShapeDtypeStruct(tuple(shape), dtype)


def kernel_call(kernel, name, ins, outs, scratch, params):
    names = list(ins) + list(outs) + list(scratch)
    results = pl.pallas_call(
        functools.partial(kernel, names),
        out_shape=tuple(outs.values()),
        in_specs=[ANY] * len(ins),
        out_specs=(ANY,) * len(outs),
        scratch_shapes=list(scratch.values()),
        name=name,
        compiler_params=pltpu.CompilerParams(**params),
    )(*ins.values())
    return dict(zip(outs, results))


def per_device(
    x_in,
    seq_lengths,
    ln1_gain,
    ln1_bias,
    ln2_gain,
    ln2_bias,
    res_bias,
    w_qkv,
    b_qkv,
    w_out,
    w_fc,
    b_fc,
    w_proj,
    grad_out,
):
    n_tensor, n_dp = lax.axis_size("tensor"), lax.axis_size("dp")
    my_tensor, my_dp = lax.axis_index("tensor"), lax.axis_index("dp")
    bf16, f32 = jnp.bfloat16, jnp.float32
    my_rows, width = x_in.shape
    group_rows = my_rows * n_tensor
    total_rows = group_rows * n_dp
    layers = w_qkv.shape[0]
    part = w_qkv.shape[3]
    hidden = w_fc.shape[2]
    dp_width = width // n_dp
    vec = ln1_gain.shape[1]
    columns_ok = dp_width % 128 == 0
    vm = pltpu.VMEM
    pad8 = lambda n: -(-n // 8) * 8
    small_rows = pad8(4 * layers)
    vec_rows = pad8(5 * layers)
    n_remote, n_send, n_local = copy_counts(n_dp, n_tensor, layers)
    paired = n_dp == 8

    ins = dict(
        x_in=x_in,
        lens=seq_lengths,
        ln1_gain=ln1_gain,
        ln1_bias=ln1_bias,
        ln2_gain=ln2_gain,
        ln2_bias=ln2_bias,
        res_bias=res_bias,
        w_qkv=jnp.transpose(w_qkv, (0, 2, 1, 3)),
        b_qkv=jnp.transpose(b_qkv, (1, 0, 2)),
        w_out=w_out,
        w_fc=w_fc,
        b_fc=b_fc,
        w_proj=w_proj,
        grad_out=grad_out,
    )
    outs = dict(
        y_out=shaped(x_in.shape, f32),
        grad_x=shaped(x_in.shape, f32),
        total_out=shaped((vec_rows + small_rows, dp_width), f32),
    )
    gathered = dict(ctx_all=part, act_all=hidden, dqkv_all=3 * part, du_all=hidden)
    if paired:
        cross = (layers, 2, 4, n_tensor, my_rows, 2 * dp_width)
        outs |= dict(
            w_qkv_g=shaped(ins["w_qkv"].shape, f32),
            w_out_g=shaped(w_out.shape, f32),
            w_fc_g=shaped(w_fc.shape, f32),
            w_proj_g=shaped(w_proj.shape, f32),
        )
    else:
        cross = (layers, 2, n_dp, n_tensor, my_rows, dp_width)
        outs |= dict(vecs_out=shaped((vec_rows, width), f32), cross=shaped(cross, bf16))
        for name, size in gathered.items():
            outs[name] = shaped((layers, total_rows, size), bf16)
    rows_block = (layers, my_rows, width)
    group_block = (layers, group_rows, width)
    land = (layers, n_tensor - 1, my_rows, width)
    scratch = dict(
        resid=vm(rows_block, f32),
        dres=vm(rows_block, f32),
        lens_v=vm(seq_lengths.shape, jnp.int32),
        sv=vm((5,) + ln1_gain.shape, f32),
        sq=vm(ins["b_qkv"].shape, f32),
        sf=vm(b_fc.shape, f32),
        pack_v=vm((vec_rows, dp_width), f32),
        pack_b=vm((small_rows, 128), f32),
        land_v=vm((n_tensor - 1, vec_rows, dp_width), f32),
        vec_all=vm((n_dp, vec_rows, dp_width), f32),
        small_b=vm((n_dp, small_rows, 128), f32),
        vecs=vm((vec_rows, width), f32),
        bq=vm((pad8(3 * layers), part), f32),
        bf=vm((pad8(layers), hidden), f32),
        same=vm((group_rows, part), f32),
        up=vm((group_rows, part), f32),
        down=vm((group_rows, part), f32),
        mask=vm((group_rows, group_rows), f32),
        wq=vm((layers, 3, width, part), bf16),
        wf=vm((layers, width, hidden), bf16),
        wo=vm((layers, part, width), bf16),
        wp=vm((layers, hidden, width), bf16),
        unit=vm(group_block, bf16),
        drows=vm(group_block, bf16),
        qkv=vm((layers, group_rows, 3 * part), bf16),
        ctx=vm((layers, group_rows, part), bf16),
        pre=vm((layers, group_rows, hidden), f32),
        act=vm((layers, group_rows, hidden), bf16),
        dctx=vm((group_rows, part), bf16),
        du=vm((layers, group_rows, hidden), bf16),
        dqkv=vm((layers, group_rows, 3 * part), bf16),
        part_f=vm(group_block, bf16),
        part_e=vm(group_block, bf16),
        land_f=vm(land, bf16),
        land_e=vm(land, bf16),
        stage=vm(cross[:3] + cross[4:], bf16),
        sums=vm((vec_rows, width), f32),
        sums_q=vm((pad8(3 * layers), part), f32),
        sums_f=vm((pad8(layers), hidden), f32),
        sums_stage=vm((n_dp, vec_rows + small_rows, dp_width), f32),
        land_s=vm((n_dp - 1, vec_rows + small_rows, dp_width), f32),
        half=vm((vec_rows, dp_width), f32),
        land_t=vm((n_tensor - 1, vec_rows, dp_width), f32),
        total_v=vm((vec_rows + small_rows, dp_width), f32),
        y_v=vm((my_rows, width), f32),
        gx_v=vm((my_rows, width), f32),
        send_sems=pltpu.SemaphoreType.DMA((n_send,)),
        recv_sems=pltpu.SemaphoreType.DMA((n_remote,)),
        local_sems=pltpu.SemaphoreType.DMA((n_local,)),
    )
    if not columns_ok:
        scratch["wo_blocks"] = vm((layers, n_dp, part, dp_width), bf16)
        scratch["wp_blocks"] = vm((layers, n_dp, hidden, dp_width), bf16)
    if paired:
        scratch["cross"] = vm(cross, bf16)
        for name, size in gathered.items():
            scratch[name] = vm((layers, 4, group_rows, size), bf16)
        halves = dict(
            gq=ins["w_qkv"].shape,
            go=(layers, dp_width, part),
            gf=(layers, dp_width, hidden),
            gp=(layers, dp_width, hidden),
        )
        for name, shape in halves.items():
            scratch[name + "_own"] = vm(shape, f32)
            scratch[name + "_away"] = vm(shape, bf16)
            scratch[name + "_land"] = vm(shape, bf16)
        scratch |= dict(go_v=vm(w_out.shape, f32), gp_v=vm(w_proj.shape, f32))
    step = kernel_call(
        functools.partial(layers_kernel, n_dp, n_tensor),
        "layers",
        ins,
        outs,
        scratch,
        {"collective_id": 0, "has_side_effects": True, "vmem_limit_bytes": 58 << 20},
    )

    if paired:
        vectors = {f"g{k}": shaped(ln1_gain.shape, f32) for k in range(5)}
        done = kernel_call(
            places_kernel,
            "places",
            dict(
                y_in=step["y_out"],
                gx_in=step["grad_x"],
                total=step["total_out"],
                qkv_in=step["w_qkv_g"],
                out_in=step["w_out_g"],
                fc_in=step["w_fc_g"],
                proj_in=step["w_proj_g"],
            ),
            dict(
                y_out=shaped(x_in.shape, f32),
                grad_x=shaped(x_in.shape, f32),
                w_qkv_g=shaped(ins["w_qkv"].shape, f32),
                b_qkv_g=shaped(ins["b_qkv"].shape, f32),
                w_out_g=shaped(w_out.shape, f32),
                w_fc_g=shaped(w_fc.shape, f32),
                b_fc_g=shaped(b_fc.shape, f32),
                w_proj_g=shaped(w_proj.shape, f32),
                **vectors,
            ),
            dict(
                total_v=vm(step["total_out"].shape, f32),
                g_v=vm((5, layers, vec), f32),
                bq_v=vm(ins["b_qkv"].shape, f32),
                bf_v=vm(b_fc.shape, f32),
                qkv_v=vm(ins["w_qkv"].shape, f32),
                fc_v=vm(w_fc.shape, f32),
                proj_v=vm(w_proj.shape, f32),
                out_v=vm(w_out.shape, f32),
                y_v=vm(x_in.shape, f32),
                gx_v=vm(x_in.shape, f32),
                sems=pltpu.SemaphoreType.DMA((12 + 8 * layers,)),
            ),
            {"vmem_limit_bytes": 58 << 20},
        )
        return (
            (done["y_out"], done["grad_x"])
            + tuple(done[name] for name in vectors)
            + (
                jnp.transpose(done["w_qkv_g"], (0, 2, 1, 3)),
                jnp.transpose(done["b_qkv_g"], (1, 0, 2)),
            )
            + tuple(done[name] for name in ("w_out_g", "w_fc_g", "b_fc_g", "w_proj_g"))
        )

    over_tokens = (((0,), (0,)), ((), ()))
    grads = [[] for _ in range(6)]
    small = step["total_out"][vec_rows:]
    vectors = step["vecs_out"][: 5 * layers].reshape(5, layers, width)
    vectors = lax.dynamic_slice_in_dim(vectors, my_dp * dp_width, dp_width, axis=2)
    for layer in range(layers):
        context_t, act_t, dqkv_t, d_pre_t = (
            step[name][layer] for name in ("ctx_all", "act_all", "dqkv_all", "du_all")
        )
        unit_t = step["cross"][layer, 0].reshape(total_rows, dp_width).astype(f32)
        d_t = step["cross"][layer, 1].reshape(total_rows, dp_width)
        a_t = (unit_t * vectors[0, layer] + vectors[1, layer]).astype(bf16)
        m_t = (unit_t * vectors[2, layer] + vectors[3, layer]).astype(bf16)

        def contract(left, right):
            return lax.dot_general(left, right, over_tokens, preferred_element_type=f32)

        grads[0].append(contract(a_t, dqkv_t).reshape(w_qkv.shape[1:]))
        grads[1].append(small[layer : 3 * layers : layers, : b_qkv.shape[2]])
        grads[2].append(contract(context_t, d_t))
        grads[3].append(contract(m_t, d_pre_t))
        grads[4].append(small[3 * layers + layer, : b_fc.shape[1]])
        grads[5].append(contract(act_t, d_t))
    vector_grads = lax.dynamic_slice_in_dim(
        step["total_out"][: 5 * layers].reshape(layers, 5, dp_width), my_tensor * vec, vec, axis=2
    )
    return (
        (step["y_out"], step["grad_x"])
        + tuple(vector_grads[:, k] for k in range(5))
        + tuple(jnp.stack(group) for group in grads)
    )


def solution(mesh):
    in_specs = (
        P(("dp", "tensor"), None),
        P("dp", None),
        P(None, ("dp", "tensor")),
        P(None, ("dp", "tensor")),
        P(None, ("dp", "tensor")),
        P(None, ("dp", "tensor")),
        P(None, ("dp", "tensor")),
        P(None, "dp", None, "tensor"),
        P(None, None, ("tensor", "dp")),
        P(None, "tensor", "dp"),
        P(None, "dp", "tensor"),
        P(None, ("tensor", "dp")),
        P(None, "tensor", "dp"),
        P(("dp", "tensor"), None),
    )
    out_specs = (
        P(("dp", "tensor"), None),
        P(("dp", "tensor"), None),
        P(None, ("dp", "tensor")),
        P(None, ("dp", "tensor")),
        P(None, ("dp", "tensor")),
        P(None, ("dp", "tensor")),
        P(None, ("dp", "tensor")),
        P(None, "dp", None, "tensor"),
        P(None, None, ("tensor", "dp")),
        P(None, "tensor", "dp"),
        P(None, "dp", "tensor"),
        P(None, ("tensor", "dp")),
        P(None, "tensor", "dp"),
    )
    return jax.shard_map(
        per_device, mesh=mesh, in_specs=in_specs, out_specs=out_specs, check_vma=False
    )
```

```python
import functools
import types

import jax
import jax.numpy as jnp
from jax import lax
from jax.experimental import pallas as pl
from jax.experimental.pallas import tpu as pltpu
from jax.sharding import PartitionSpec as P

HD = 64
ROT = 16


EPS = 1e-05
NEG_FILL = -1e30


def gelu_exact(values):
    return 0.5 * values * (1.0 + jax.scipy.special.erf(values * 0.7071067811865476))


def gelu_slope(values):
    normal_cdf = 0.5 * (1.0 + jax.scipy.special.erf(values * 0.7071067811865476))
    return normal_cdf + values * jnp.exp(-0.5 * values * values) * 0.3989422804014327


MESH = pl.DeviceIdType.MESH
ANY = pl.BlockSpec(memory_space=pl.ANY)
VMEM = pl.BlockSpec(memory_space=pltpu.VMEM)


def copy_counts(n_dp, n_tensor, layers):
    chips = n_dp // 2
    remote = (n_tensor - 1) * (6 * layers + 2) + (n_dp - 1) * 3
    if chips == 4:
        remote = remote + layers * (4 * 13 + 4 * 3 + 2 * 3 + 4)
        again = (n_tensor - 1) * (3 * layers) + 15 * layers + n_dp - 4
        return remote, remote - again, 14 * layers + 14
    remote = remote + layers * (8 * (4 * chips - 3) + 2 * (n_dp - 1))
    return remote, remote, 10 * layers + 15


class Links:
    def __init__(self, n_dp, n_tensor, send_sems, recv_sems, local_sems):
        self.n_dp, self.n_tensor = n_dp, n_tensor
        self.dp, self.tensor = lax.axis_index("dp"), lax.axis_index("tensor")
        self.core, self.chip = lax.rem(self.dp, 2), self.dp // 2
        self.partner = self.dp + 1 - 2 * self.core
        self.paired = n_dp == 8
        if self.paired:
            self.gather_y, self.gather_x = Turn(self, False), Turn(self, True)
        self.send_sems, self.recv_sems, self.local_sems = send_sems, recv_sems, local_sems
        self.used, self.used_local, self.used_send = 0, 0, 0
        self.sent, self.free = [], []

    def send(self, src, dst, **where):
        if self.free:
            place = self.free.pop(0)
        else:
            place = self.used_send
            self.used_send += 1
        copy = pltpu.make_async_remote_copy(
            src_ref=src,
            dst_ref=dst,
            send_sem=self.send_sems.at[place],
            recv_sem=self.recv_sems.at[self.used],
            device_id=where,
            device_id_type=MESH,
        )
        self.used += 1
        copy.start()
        self.sent.append((copy, place))
        return copy

    def local(self, src, dst):
        copy = pltpu.make_async_copy(src, dst, self.local_sems.at[self.used_local])
        self.used_local += 1
        copy.start()
        return copy

    def dp_peer(self, step):
        return lax.rem(self.dp + step, self.n_dp)

    def tensor_peer(self, step):
        return lax.rem(self.tensor + step, self.n_tensor)

    def enter(self):
        sem = pltpu.get_barrier_semaphore()
        for step in range(1, self.n_tensor):
            pl.semaphore_signal(
                sem, inc=1, device_id={"tensor": self.tensor_peer(step)}, device_id_type=MESH
            )
        for step in range(1, self.n_dp):
            pl.semaphore_signal(
                sem, inc=1, device_id={"dp": self.dp_peer(step)}, device_id_type=MESH
            )

    def barrier(self):
        pl.semaphore_wait(pltpu.get_barrier_semaphore(), self.n_tensor + self.n_dp - 2)

    def settle(self, count):
        for copy, place in self.sent[:count]:
            copy.wait_send()
            self.free.append(place)
        self.sent = self.sent[count:]

    def finish(self):
        for copy, _ in self.sent:
            copy.wait_send()


class Turn:
    def __init__(self, links, gather_x):
        x, y = lax.rem(links.chip, 2), links.chip // 2
        over = (links.dp + 2 - 4 * x, lax.rem(links.dp + 4, 8))
        self.gather_x = gather_x
        self.gather_dp, self.sum_dp = over if gather_x else over[::-1]
        self.along, self.apart = (x, y) if gather_x else (y, x)
        self.place = self.along * 2 + links.core
        self.far_place = lax.rem(self.place + 2, 4)

    def block(self, place, apart):
        if self.gather_x:
            return apart * 4 + place
        return place // 2 * 4 + 2 * apart + lax.rem(place, 2)


class DpGather:
    def __init__(self, links, own, slot, axis=0):
        self.links, self.own, self.slot = links, own, slot
        self.chips = links.n_dp // 2
        self.core, self.chip, self.partner = links.core, links.chip, links.partner
        self.relays = self.chips == 4
        rows = own.shape[axis] // 2
        self.halves = [
            (slice(None),) * axis + (pl.ds(half * rows, rows),) for half in range(2)
        ]
        self.passed = []
        if self.relays:
            near = self.chip + 1 - 2 * lax.rem(self.chip, 2)
            far = lax.rem(self.chip + 2, 4)
            self.across = lax.rem(near + 2, 4)
            self.order = ((near, far), (far, near))

    def device(self, chip):
        return chip * 2 + self.core

    def out(self, rows, chip):
        return self.links.send(
            self.own.at[rows], self.slot(self.links.dp).at[rows], dp=self.device(chip)
        )

    def pass_on(self, rows, chip, target):
        block = self.slot(self.device(chip)).at[rows]
        return self.links.send(block, block, dp=target)

    def start(self):
        if self.relays:
            self.first = [self.out(rows, order[0]) for rows, order in zip(self.halves, self.order)]
            self.second = [self.out(rows, order[1]) for rows, order in zip(self.halves, self.order)]
        else:
            self.direct = [
                [self.out(rows, lax.rem(self.chip + step, self.chips)) for rows in self.halves]
                for step in range(1, self.chips)
            ]
        own_slot = self.slot(self.links.dp)
        self.passed.append(self.links.send(self.own, own_slot, dp=self.partner))
        self.kept = self.links.local(self.own, own_slot)

    def relay(self):
        if not self.relays:
            return
        self.relayed = []
        for copy, rows, order in zip(self.first, self.halves, self.order):
            copy.wait_recv()
            self.relayed.append(self.pass_on(rows, order[0], self.device(order[1])))
            self.passed.append(self.pass_on(rows, order[0], self.partner))

    def rest(self):
        if not self.relays:
            for step, copies in enumerate(self.direct):
                origin = lax.rem(self.chip + self.chips - step - 1, self.chips)
                for copy, rows in zip(copies, self.halves):
                    copy.wait_recv()
                    self.passed.append(self.pass_on(rows, origin, self.partner))
            return
        for copy, rows, order in zip(self.second, self.halves, self.order):
            copy.wait_recv()
            self.passed.append(self.pass_on(rows, order[1], self.partner))
        for copy, rows in zip(self.relayed, self.halves):
            copy.wait_recv()
            self.passed.append(self.pass_on(rows, self.across, self.partner))

    def finish(self):
        for copy in self.passed:
            copy.wait_recv()
        self.kept.wait()


class PairGather:
    def __init__(self, links, turn, own, slot):
        self.links, self.turn, self.own, self.slot = links, turn, own, slot

    def start(self):
        links, here = self.links, self.slot(self.turn.place)
        self.out = links.send(self.own, here, dp=self.turn.gather_dp)
        self.passed = [links.send(self.own, here, dp=links.partner)]
        self.kept = links.local(self.own, here)

    def rest(self):
        self.out.wait_recv()
        block = self.slot(self.turn.far_place)
        self.passed.append(self.links.send(block, block, dp=self.links.partner))

    def finish(self):
        for copy in self.passed:
            copy.wait_recv()
        self.kept.wait()


class Group:
    def __init__(self, *gathers):
        self.gathers = gathers

    def start(self):
        for gather in self.gathers:
            gather.start()

    def relay(self):
        for gather in self.gathers:
            gather.relay()

    def rest(self):
        for gather in self.gathers:
            gather.rest()

    def finish(self):
        for gather in self.gathers:
            gather.finish()


class Pump:
    def __init__(self):
        self.todo, self.started, self.relayed, self.every = [], [], [], []

    def add(self, group):
        self.todo.append(group)
        self.every.append(group)
        if not self.started:
            self.start()

    def start(self):
        if self.todo:
            group = self.todo.pop(0)
            group.start()
            self.started.append(group)

    def relay(self):
        group = self.started.pop(0)
        group.relay()
        self.relayed.append(group)
        if not self.started:
            self.start()

    def rest(self):
        self.relayed.pop(0).rest()


def row_slot(ref, rows):
    return lambda d: ref.at[pl.ds(pl.multiple_of(d * rows, rows), rows)]


def middle_slot(ref, rows):
    return lambda d: ref.at[:, pl.ds(pl.multiple_of(d * rows, rows), rows)]


def column_slot(ref, size):
    return lambda d: ref.at[:, pl.ds(pl.multiple_of(d * size, size), size)]


def lead_slot(ref):
    return lambda d: ref.at[d]


class Scatter:
    def __init__(self, links, part, landing):
        self.links, self.part, self.landing = links, part, landing
        self.rows = landing.shape[1]
        slot = row_slot(part, self.rows)
        self.copies = [
            links.send(
                slot(links.tensor_peer(step)),
                landing.at[step - 1],
                tensor=links.tensor_peer(step),
            )
            for step in range(1, links.n_tensor)
        ]

    def total(self):
        own = pl.ds(pl.multiple_of(self.links.tensor * self.rows, self.rows), self.rows)
        total = self.part[own, :].astype(jnp.float32)
        for step, copy in enumerate(self.copies):
            copy.wait_recv()
            total = total + self.landing[step].astype(jnp.float32)
        return total


class Spread:
    def __init__(self, links, ref, value):
        rows = value.shape[0]
        self.links, self.here = links, row_slot(ref, rows)(links.tensor)
        ref[pl.ds(pl.multiple_of(links.tensor * rows, rows), rows), :] = value

    def send(self):
        links = self.links
        self.copies = [
            links.send(self.here, self.here, tensor=links.tensor_peer(step))
            for step in range(1, links.n_tensor)
        ]

    def finish(self):
        for copy in self.copies:
            copy.wait_recv()


class Cross:
    def __init__(self, links, turn, stage, out, value):
        self.links, self.turn, self.stage, self.out = links, turn, stage, out
        self.count, _, width = stage.shape
        self.me = turn.place if links.paired else links.dp
        if not links.paired:
            for d in range(self.count):
                stage[d] = value[:, d * width : (d + 1) * width]
            return
        half = width // 2
        wide = value.astype(jnp.float32)
        for s in range(self.count):
            at = [
                (apart * 4 + s if turn.gather_x else s // 2 * 4 + 2 * apart + s % 2) * half
                for apart in range(2)
            ]
            one, two = (wide[:, place : place + half] for place in at)
            stage[s, :, 0:half] = jnp.where(turn.apart == 0, one, two).astype(value.dtype)
            stage[s, :, half:width] = jnp.where(turn.apart == 0, two, one).astype(value.dtype)

    def send(self):
        links, stage = self.links, self.stage
        here = self.out.at[self.me, links.tensor]
        self.copies = []
        for step in range(1, self.count):
            peer = lax.rem(self.me + step, self.count)
            device = self.turn.block(peer, self.turn.apart) if links.paired else peer
            self.copies.append(links.send(stage.at[peer], here, dp=device))
        self.kept = links.local(stage.at[self.me], here)

    def forward(self):
        links = self.links
        for copy in self.copies:
            copy.wait_recv()
        self.kept.wait()
        mine = self.out.at[:, links.tensor]
        self.wide = [
            links.send(mine, mine, tensor=links.tensor_peer(step))
            for step in range(1, links.n_tensor)
        ]

    def finish(self):
        for copy in self.wide:
            copy.wait_recv()


class Product:
    def __init__(self, links, turn, own, away, landing, rows, columns):
        self.own, self.landing = own, landing
        parts = own.shape[0] if len(own.shape) == 3 else 1
        half, width = own.shape[-2:]
        for k in range(parts):
            total = dot_tn(rows, columns[:, k * width : (k + 1) * width])
            if len(own.shape) == 3:
                own[k] = total[:half]
                away[k] = total[half:].astype(away.dtype)
            else:
                own[...] = total[:half]
                away[...] = total[half:].astype(away.dtype)
        self.copy = links.send(away, landing, dp=turn.sum_dp)

    def total(self):
        self.copy.wait_recv()
        return self.own[...] + self.landing[...].astype(jnp.float32)


def unit_rows(values):
    average = jnp.mean(values, axis=-1, keepdims=True)
    centred = values - average
    variance = jnp.mean(centred * centred, axis=-1, keepdims=True)
    scale = lax.rsqrt(variance + EPS)
    return centred * scale, scale


def back_unit(values, grad):
    unit, scale = unit_rows(values)
    return scale * (
        grad
        - jnp.mean(grad, axis=-1, keepdims=True)
        - unit * jnp.mean(grad * unit, axis=-1, keepdims=True)
    )


def dot_nn(left, right):
    return jnp.dot(left, right, preferred_element_type=jnp.float32)


def dot_nt(left, right):
    return lax.dot_general(left, right, (((1,), (1,)), ((), ())), preferred_element_type=jnp.float32)


def dot_tn(left, right):
    return lax.dot_general(left, right, (((0,), (0,)), ((), ())), preferred_element_type=jnp.float32)


def turn(vectors, same, up, down, sign):
    width = vectors.shape[1]
    above = pltpu.roll(vectors, width - ROT // 2, 1)
    below = pltpu.roll(vectors, ROT // 2, 1)
    return vectors * same + sign * (above * up + below * down)


def head_scores(query, key, mask):
    scores = dot_nt(query, key) * HD ** (-0.5)
    scores = jnp.where(mask, scores, NEG_FILL)
    terms = jnp.exp(scores - jnp.max(scores, axis=-1, keepdims=True))
    return terms / jnp.sum(terms, axis=-1, keepdims=True)


def layout_tables(r):
    f32 = jnp.float32
    rows, width = r.same.shape
    lengths = r.lens_v[...]
    row_of = lax.broadcasted_iota(jnp.int32, (rows, rows), 0)
    col_of = lax.broadcasted_iota(jnp.int32, (rows, rows), 1)
    row_lane = lax.broadcasted_iota(jnp.int32, (rows, 128), 0)
    start = jnp.zeros((rows, rows), jnp.int32)
    start_lane = jnp.zeros((rows, 128), jnp.int32)
    end = jnp.zeros((1, 1), jnp.int32)
    for k in range(lengths.shape[1]):
        end = end + lengths[:, k : k + 1]
        start = jnp.where(row_of >= end, end, start)
        start_lane = jnp.where(row_lane >= end, end, start_lane)
    r.mask[...] = jnp.where((col_of >= start) & (col_of <= row_of), 1.0, 0.0)
    positions = (row_lane - start_lane).astype(f32)
    lane = lax.rem(lax.broadcasted_iota(jnp.int32, (1, 128), 1), HD)
    half = ROT // 2
    inverse = jnp.power(10000.0, -2.0 * lax.rem(lane, half).astype(f32) / ROT)
    angles = positions * inverse
    cos_tab, sin_tab = jnp.cos(angles), jnp.sin(angles)
    same = jnp.where(lane < ROT, cos_tab, 1.0)
    up = jnp.where(lane < half, -sin_tab, 0.0)
    down = jnp.where((lane >= half) & (lane < ROT), sin_tab, 0.0)
    for ref, table in ((r.same, same), (r.up, up), (r.down, down)):
        for place in range(width // 128):
            ref[:, place * 128 : (place + 1) * 128] = table


def gain_rows(r, layer):
    layers = r.resid.shape[0]
    return tuple(r.vecs[k * layers + layer : k * layers + layer + 1, :] for k in range(5))


def forward_attention(r, layer):
    bf16 = jnp.bfloat16
    g1, b1, _, _, _ = gain_rows(r, layer)
    layers, _, part = r.ctx.shape
    normed_a = (r.unit[layer].astype(jnp.float32) * g1 + b1).astype(bf16)
    tables = (r.same[...], r.up[...], r.down[...])
    for which in range(3):
        row = which * layers + layer
        block = dot_nn(normed_a, r.wq[layer, which]) + r.bq[row : row + 1, :]
        if which < 2:
            block = turn(block, *tables, 1.0)
        r.qkv[layer, :, which * part : (which + 1) * part] = block.astype(bf16)
    allowed = r.mask[...] > 0.0
    for head in range(part // HD):
        q, k, v = (
            r.qkv[layer, :, which * part + head * HD : which * part + (head + 1) * HD]
            for which in range(3)
        )
        probs = head_scores(q, k, allowed).astype(bf16)
        r.ctx[layer, :, head * HD : (head + 1) * HD] = dot_nn(probs, v).astype(bf16)


def forward_hidden(r, layer):
    bf16 = jnp.bfloat16
    _, _, g2, b2, _ = gain_rows(r, layer)
    normed_m = (r.unit[layer].astype(jnp.float32) * g2 + b2).astype(bf16)
    hidden = dot_nn(normed_m, r.wf[layer]) + r.bf[layer : layer + 1, :]
    r.pre[layer] = hidden
    r.act[layer] = gelu_exact(hidden).astype(bf16)


def forward_part(r, layer):
    r.part_f[layer] = (
        dot_nn(r.ctx[layer], r.wo[layer]) + dot_nn(r.act[layer], r.wp[layer])
    ).astype(jnp.bfloat16)


def backward_hidden(r, layer):
    bf16 = jnp.bfloat16
    r.dctx[...] = dot_nt(r.drows[layer], r.wo[layer]).astype(bf16)
    d_pre = dot_nt(r.drows[layer], r.wp[layer]) * gelu_slope(r.pre[layer])
    r.sums_f[layer : layer + 1, :] = jnp.sum(d_pre, axis=0, keepdims=True)
    r.du[layer] = d_pre.astype(bf16)


def backward_attention(r, layer):
    bf16, f32 = jnp.bfloat16, jnp.float32
    part = r.ctx.shape[2]
    allowed = r.mask[...] > 0.0
    pieces = [[], [], []]
    for head in range(part // HD):
        here = slice(head * HD, (head + 1) * HD)
        q, k, v = (
            r.qkv[layer, :, which * part + head * HD : which * part + (head + 1) * HD]
            for which in range(3)
        )
        dc = r.dctx[:, here]
        probs = head_scores(q, k, allowed)
        delta = jnp.sum(
            dc.astype(f32) * r.ctx[layer, :, here].astype(f32), axis=-1, keepdims=True
        )
        d_scaled = (probs * (dot_nt(dc, v) - delta) * HD ** (-0.5)).astype(bf16)
        pieces[0].append(dot_nn(d_scaled, k))
        pieces[1].append(dot_tn(d_scaled, q))
        pieces[2].append(dot_tn(probs.astype(bf16), dc))
    tables = (r.same[...], r.up[...], r.down[...])
    for which in range(3):
        block = jnp.concatenate(pieces[which], axis=1)
        if which < 2:
            block = turn(block, *tables, -1.0)
        row = which * r.ctx.shape[0] + layer
        r.sums_q[row : row + 1, :] = jnp.sum(block, axis=0, keepdims=True)
        r.dqkv[layer, :, which * part : (which + 1) * part] = block.astype(bf16)


def backward_part(r, layer):
    g1, _, g2, _, _ = gain_rows(r, layer)
    part = r.ctx.shape[2]
    d_a = sum(
        dot_nt(r.dqkv[layer, :, which * part : (which + 1) * part], r.wq[layer, which])
        for which in range(3)
    )
    d_m = dot_nt(r.du[layer], r.wf[layer])
    r.part_e[layer] = (d_a * g1 + d_m * g2).astype(jnp.bfloat16)
    wide = r.unit[layer].astype(jnp.float32)
    for row, term in enumerate((d_a * wide, d_a, d_m * wide, d_m)):
        r.sums[5 * layer + row : 5 * layer + row + 1, :] = jnp.sum(term, axis=0, keepdims=True)


def pack_small(r, links):
    count, layers, vec = r.sv.shape
    r.pack_v[...] = jnp.zeros_like(r.pack_v)
    owner = lax.broadcasted_iota(jnp.int32, (layers, vec * links.n_tensor), 1) // vec
    for k in range(count):
        value = jnp.concatenate([r.sv[k]] * links.n_tensor, axis=1)
        r.pack_v[k * layers : (k + 1) * layers, :] = jnp.where(owner == links.tensor, value, 0.0)
    r.pack_b[...] = jnp.zeros_like(r.pack_b)
    for which in range(3):
        r.pack_b[which * layers : (which + 1) * layers, 0 : r.sq.shape[2]] = r.sq[which]
    r.pack_b[3 * layers : 4 * layers, 0 : r.sf.shape[1]] = r.sf[...]


def unpack_small(r, links):
    layers = r.sf.shape[0]
    width = r.vec_all.shape[2]
    rows = 0
    for d in range(links.n_dp):
        r.vecs[:, d * width : (d + 1) * width] = r.vec_all[d]
    for ref, height, lanes in ((r.bq, 3 * layers, r.sq.shape[2]), (r.bf, layers, r.sf.shape[1])):
        ref[0:height, :] = jnp.concatenate(
            [r.small_b[d, rows : rows + height, 0:lanes] for d in range(links.n_dp)], axis=1
        )
        rows = rows + height


def in_columns(r, links, layer):
    for blocks, whole in ((r.wo_blocks, r.wo), (r.wp_blocks, r.wp)):
        width = blocks.shape[3]
        for d in range(links.n_dp):
            whole[layer, :, d * width : (d + 1) * width] = blocks[layer, d]


def start_sums(r, links):
    layers = r.resid.shape[0]
    width = r.sums_stage.shape[2]
    rows = r.sums.shape[0]
    lanes_q, lanes_f = r.sq.shape[2], r.sf.shape[1]
    r.sums_stage[...] = jnp.zeros_like(r.sums_stage)
    for d in range(links.n_dp):
        r.sums_stage[d, 0:rows, :] = r.sums[:, d * width : (d + 1) * width]
        r.sums_stage[d, rows : rows + 3 * layers, 0:lanes_q] = r.sums_q[
            0 : 3 * layers, d * lanes_q : (d + 1) * lanes_q
        ]
        r.sums_stage[d, rows + 3 * layers : rows + 4 * layers, 0:lanes_f] = r.sums_f[
            0:layers, d * lanes_f : (d + 1) * lanes_f
        ]
    return [
        links.send(
            r.sums_stage.at[links.dp_peer(step)], r.land_s.at[step - 1], dp=links.dp_peer(step)
        )
        for step in range(1, links.n_dp)
    ]


def middle_sums(r, links, sent):
    rows = r.sums.shape[0]
    total = r.sums_stage[links.dp]
    for step, copy in enumerate(sent):
        copy.wait_recv()
        total = total + r.land_s[step]
    r.total_v[...] = total
    r.half[...] = total[0:rows]
    return [
        links.send(r.half, r.land_t.at[step - 1], tensor=links.tensor_peer(step))
        for step in range(1, links.n_tensor)
    ]


def end_sums(r, links, sent):
    rows = r.sums.shape[0]
    total = r.half[...]
    for step, copy in enumerate(sent):
        copy.wait_recv()
        total = total + r.land_t[step]
    r.total_v[0:rows, :] = total
    return links.local(r.total_v, r.total_out)


def token_rows(r, layer, which):
    block = r.cross[layer, which]
    return block.reshape(-1, block.shape[-1])


def product_turn(links, layer, which):
    if not links.paired:
        return None
    return links.gather_y if (layer, which) == (0, 1) else links.gather_x


def normed_rows(r, links, layer, norm):
    layers = r.resid.shape[0]
    half = r.cross.shape[-1] // 2
    gain, bias = (
        jnp.concatenate(
            [
                r.vecs[row : row + 1, pl.ds(pl.multiple_of(d * half, half), half)]
                for d in (links.dp, product_turn(links, layer, 0).sum_dp)
            ],
            axis=1,
        )
        for row in (2 * norm * layers + layer, (2 * norm + 1) * layers + layer)
    )
    unit = token_rows(r, layer, 0).astype(jnp.float32)
    return (unit * gain + bias).astype(jnp.bfloat16)


class Products:
    def __init__(self, r, links):
        self.r, self.links, self.stores = r, links, []

    def columns(self, ref, layer):
        block = ref[layer]
        return block.reshape(-1, block.shape[-1])

    def outputs(self, layer):
        r = self.r
        d_t = token_rows(r, layer, 1)
        return [
            Product(
                self.links, product_turn(self.links, layer, 1), own.at[layer], away.at[layer], land.at[layer], d_t,
                self.columns(columns, layer),
            )
            for own, away, land, columns in (
                (r.go_own, r.go_away, r.go_land, r.ctx_all),
                (r.gp_own, r.gp_away, r.gp_land, r.act_all),
            )
        ]

    def hidden(self, layer):
        r = self.r
        return Product(
            self.links, product_turn(self.links, layer, 0), r.gf_own.at[layer], r.gf_away.at[layer], r.gf_land.at[layer],
            normed_rows(r, self.links, layer, 1), self.columns(r.du_all, layer),
        )

    def heads(self, layer):
        r = self.r
        return Product(
            self.links, product_turn(self.links, layer, 0), r.gq_own.at[layer], r.gq_away.at[layer], r.gq_land.at[layer],
            normed_rows(r, self.links, layer, 0), self.columns(r.dqkv_all, layer),
        )

    def store_outputs(self, layer, products):
        r = self.r
        for product, turned, out in zip(products, (r.go_v, r.gp_v), (r.w_out_g, r.w_proj_g)):
            turned[layer] = jnp.transpose(product.total())
            self.stores.append(self.links.local(turned.at[layer], out.at[layer]))

    def store(self, layer, product, out):
        product.own[...] = product.total()
        self.stores.append(self.links.local(product.own, out.at[layer]))


def make_cross(r, links, layer, which, value):
    turn = product_turn(links, layer, which)
    return Cross(links, turn, r.stage.at[layer, which], r.cross.at[layer, which], value)


def layers_kernel(n_dp, n_tensor, names, *refs):
    r = types.SimpleNamespace(**dict(zip(names, refs)))
    links = Links(n_dp, n_tensor, r.send_sems, r.recv_sems, r.local_sems)
    bf16 = jnp.bfloat16
    layers = r.w_out.shape[0]
    last = layers - 1
    columns_ok = not hasattr(r, "wo_blocks")
    links.enter()
    x_load = links.local(r.x_in, r.resid.at[0])
    d_load = links.local(r.grad_out, r.dres.at[last])
    loads = [links.local(r.lens, r.lens_v)]
    for k, ref in enumerate((r.ln1_gain, r.ln1_bias, r.ln2_gain, r.ln2_bias, r.res_bias)):
        loads.append(links.local(ref, r.sv.at[k]))
    loads.append(links.local(r.b_qkv, r.sq))
    loads.append(links.local(r.b_fc, r.sf))

    qkv_g, fc_g, proj_g, fwd_g, du_g, dqkv_g = [], [], [], [], [], []
    for layer in range(layers):
        dp_width = r.w_qkv.shape[2]
        qkv_g.append(
            Group(DpGather(links, r.w_qkv.at[layer], middle_slot(r.wq.at[layer], dp_width), 1))
        )
        if columns_ok:
            slots = [column_slot(ref.at[layer], dp_width) for ref in (r.wo, r.wp)]
        else:
            slots = [lead_slot(ref.at[layer]) for ref in (r.wo_blocks, r.wp_blocks)]
        out_j = DpGather(links, r.w_out.at[layer], slots[0])
        fc_j = DpGather(links, r.w_fc.at[layer], row_slot(r.wf.at[layer], dp_width))
        fc_g.append(Group(out_j, fc_j))
        proj_g.append(Group(DpGather(links, r.w_proj.at[layer], slots[1])))
        rows = r.ctx.shape[1]
        ctx_j, act_j, dqkv_j, du_j = (
            PairGather(
                links, product_turn(links, layer, which), own.at[layer], lead_slot(whole.at[layer])
            )
            if links.paired
            else DpGather(links, own.at[layer], row_slot(whole.at[layer], rows))
            for own, whole, which in (
                (r.ctx, r.ctx_all, 1),
                (r.act, r.act_all, 1),
                (r.dqkv, r.dqkv_all, 0),
                (r.du, r.du_all, 0),
            )
        )
        fwd_g.append(Group(ctx_j, act_j))
        du_g.append(Group(du_j))
        dqkv_g.append(Group(dqkv_j))

    x_load.wait()
    unit = unit_rows(r.resid[0])[0].astype(bf16)
    unit_s = Spread(links, r.unit.at[0], unit)
    for load in loads:
        load.wait()
    pack_small(r, links)
    d_load.wait()
    d_bf = r.dres[last].astype(bf16)
    rows_s = Spread(links, r.drows.at[last], d_bf)
    crosses = [
        make_cross(r, links, 0, 0, unit),
        make_cross(r, links, last, 1, d_bf),
    ]
    r.sums[...] = jnp.zeros_like(r.sums)
    layout_tables(r)
    links.barrier()

    vec_sent = [
        links.send(r.pack_v, r.land_v.at[step - 1], tensor=links.tensor_peer(step))
        for step in range(1, n_tensor)
    ]
    b_here = r.small_b.at[links.dp]
    small_sent = [
        links.send(r.pack_b, b_here, dp=links.dp_peer(step)) for step in range(1, n_dp)
    ]
    small_kept = links.local(r.pack_b, b_here)
    pump = Pump()
    for layer in range(layers):
        for group in (qkv_g[layer], fc_g[layer], proj_g[layer]):
            pump.add(group)
    unit_s.send()
    crosses[0].send()
    total = r.pack_v[...]
    for step, copy in enumerate(vec_sent):
        copy.wait_recv()
        total = total + r.land_v[step]
    r.vec_all[links.dp] = total
    vec_here = r.vec_all.at[links.dp]
    vec_wide = [
        links.send(vec_here, vec_here, dp=links.dp_peer(step)) for step in range(1, n_dp)
    ]
    rows_s.send()
    pump.relay()
    crosses[1].send()
    small_kept.wait()
    for copy in small_sent + vec_wide:
        copy.wait_recv()
    unpack_small(r, links)

    for layer in range(layers):
        pump.rest()
        qkv_g[layer].finish()
        if layer == 0:
            crosses[0].forward()
        else:
            pump.relay()
        unit_s.finish()
        forward_attention(r, layer)
        if layer == 0:
            pump.relay()
            crosses[1].forward()
        pump.rest()
        fc_g[layer].finish()
        forward_hidden(r, layer)
        if layer > 0:
            crosses[-1].forward()
        if not links.paired:
            pump.add(fwd_g[layer])
        pump.relay()
        pump.rest()
        if links.paired and layer == last:
            fwd_g[last].start()
            fwd_g[0].start()
        proj_g[layer].finish()
        if not columns_ok:
            in_columns(r, links, layer)
        forward_part(r, layer)
        if layer < last:
            scatter = Scatter(links, r.part_f.at[layer], r.land_f.at[layer])
            pump.relay()
            values = r.resid[layer] + scatter.total() + gain_rows(r, layer)[4]
            r.resid[layer + 1] = values
            unit = unit_rows(values)[0].astype(bf16)
            unit_s = Spread(links, r.unit.at[layer + 1], unit)
            settled = len(links.sent)
            unit_s.send()
            crosses.append(make_cross(r, links, layer + 1, 0, unit))
            crosses[-1].send()

    if links.paired:
        links.settle(settled)
        finish = backward_paired
    else:
        finish = backward_gathered
    stores = finish(r, links, pump, fwd_g, du_g, dqkv_g, crosses, rows_s)
    for store in stores:
        store.wait()
    links.finish()
    counts = (links.used, links.used_send, links.used_local)
    assert counts == copy_counts(n_dp, n_tensor, layers), counts


def start_back(r, links, layer):
    backward_part(r, layer)
    scatter = Scatter(links, r.part_e.at[layer], r.land_e.at[layer])
    r.sums[5 * layer + 4 : 5 * layer + 5, :] = jnp.sum(r.dres[layer], axis=0, keepdims=True)
    return scatter


def step_back(r, links, layer, scatter, crosses):
    new_d = r.dres[layer] + back_unit(r.resid[layer], scatter.total())
    r.dres[layer - 1] = new_d
    d_bf = new_d.astype(jnp.bfloat16)
    rows_s = Spread(links, r.drows.at[layer - 1], d_bf)
    rows_s.send()
    crosses.append(make_cross(r, links, layer - 1, 1, d_bf))
    crosses[-1].send()
    return rows_s


def store_y(r, links, scatter):
    last = r.resid.shape[0] - 1
    r.y_v[...] = r.resid[last] + scatter.total() + gain_rows(r, last)[4]
    return links.local(r.y_v, r.y_out)


def store_grad_x(r, links, scatter):
    r.gx_v[...] = r.dres[0] + back_unit(r.resid[0], scatter.total())
    return links.local(r.gx_v, r.grad_x)


def backward_paired(r, links, pump, fwd_g, du_g, dqkv_g, crosses, rows_s):
    layers = r.resid.shape[0]
    last = layers - 1
    products = Products(r, links)
    done = []
    for layer in reversed(range(1, layers)):
        rows_s.finish()
        backward_hidden(r, layer)
        backward_attention(r, layer)
        scatter = start_back(r, links, layer)
        du_g[layer].start()
        if layer == last:
            for cross in crosses:
                cross.finish()
        rows_s = step_back(r, links, layer, scatter, crosses)
        fwd_g[layer].rest()
        dqkv_g[layer].start()
        if layer > 1:
            fwd_g[layer - 1].start()
        fwd_g[layer].finish()
        outputs = products.outputs(layer)
        du_g[layer].rest()
        du_g[layer].finish()
        hidden = products.hidden(layer)
        done.append((layer, outputs, hidden))
        if layer > 1:
            crosses[-1].forward()
    fwd_g[0].rest()
    rows_s.finish()
    crosses[-1].forward()
    backward_hidden(r, 0)
    du_g[0].start()
    for layer in reversed(range(1, layers)):
        dqkv_g[layer].rest()
        dqkv_g[layer].finish()
    backward_attention(r, 0)
    dqkv_g[0].start()
    late = [(layer, products.heads(layer)) for layer in reversed(range(1, layers))]
    scatter = start_back(r, links, 0)
    sums_sent = start_sums(r, links)
    for layer, outputs, _ in done:
        products.store_outputs(layer, outputs)
    for cross in crosses[layers + 1 :]:
        cross.finish()
    fwd_g[0].finish()
    outputs = products.outputs(0)
    du_g[0].rest()
    du_g[0].finish()
    hidden = products.hidden(0)
    sent_y = Scatter(links, r.part_f.at[last], r.land_f.at[last])
    dqkv_g[0].rest()
    for layer, _, product in done:
        products.store(layer, product, r.w_fc_g)
    dqkv_g[0].finish()
    heads = products.heads(0)
    sums_wide = middle_sums(r, links, sums_sent)
    stores = [store_grad_x(r, links, scatter)]
    for layer, product in late:
        products.store(layer, product, r.w_qkv_g)
    products.store_outputs(0, outputs)
    stores.append(end_sums(r, links, sums_wide))
    stores.append(store_y(r, links, sent_y))
    products.store(0, hidden, r.w_fc_g)
    products.store(0, heads, r.w_qkv_g)
    return stores + products.stores


def backward_gathered(r, links, pump, fwd_g, du_g, dqkv_g, crosses, rows_s):
    layers = r.resid.shape[0]
    last = layers - 1
    sent_y = Scatter(links, r.part_f.at[last], r.land_f.at[last])
    for layer in reversed(range(layers)):
        rows_s.finish()
        backward_hidden(r, layer)
        pump.add(du_g[layer])
        if layer == last:
            pump.relay()
        else:
            crosses[-1].forward()
        backward_attention(r, layer)
        pump.add(dqkv_g[layer])
        scatter = start_back(r, links, layer)
        if layer == 0:
            sums_sent = start_sums(r, links)
        pump.rest()
        pump.relay()
        if layer > 0:
            rows_s = step_back(r, links, layer, scatter, crosses)
            pump.rest()
            pump.relay()

    stores = [store_grad_x(r, links, scatter), store_y(r, links, sent_y)]
    stores.append(links.local(r.vecs, r.vecs_out))
    sums_wide = middle_sums(r, links, sums_sent)
    while pump.relayed or pump.started:
        if pump.relayed:
            pump.rest()
        if pump.started:
            pump.relay()
    stores.append(end_sums(r, links, sums_wide))
    for group in fwd_g + du_g + dqkv_g:
        group.finish()
    for cross in crosses:
        cross.finish()
    return stores


def places_kernel(names, *refs):
    r = types.SimpleNamespace(**dict(zip(names, refs)))
    tensor = lax.axis_index("tensor")
    count = [0]

    def local(src, dst):
        copy = pltpu.make_async_copy(src, dst, r.sems.at[count[0]])
        count[0] += 1
        copy.start()
        return copy

    load = local(r.total, r.total_v)
    moves = [
        (local(source, held), held, out)
        for source, held, out in (
            (r.qkv_in, r.qkv_v, r.w_qkv_g),
            (r.fc_in, r.fc_v, r.w_fc_g),
            (r.proj_in, r.proj_v, r.w_proj_g),
            (r.out_in, r.out_v, r.w_out_g),
            (r.y_in, r.y_v, r.y_out),
            (r.gx_in, r.gx_v, r.grad_x),
        )
    ]
    stores = []
    load.wait()
    layers, vec = r.g0.shape
    width = r.total.shape[1]
    rolled = pltpu.roll(r.total_v[...], lax.rem(width - tensor * vec, width), 1)
    for k, out in enumerate((r.g0, r.g1, r.g2, r.g3, r.g4)):
        for layer in range(layers):
            r.g_v[k, layer : layer + 1, :] = rolled[5 * layer + k : 5 * layer + k + 1, 0:vec]
        stores.append(local(r.g_v.at[k], out))
    rows = -(-5 * layers // 8) * 8
    for which in range(3):
        at = rows + which * layers
        r.bq_v[which] = r.total_v[at : at + layers, 0 : r.bq_v.shape[2]]
    at = rows + 3 * layers
    r.bf_v[...] = r.total_v[at : at + layers, 0 : r.bf_v.shape[1]]
    stores.append(local(r.bq_v, r.b_qkv_g))
    stores.append(local(r.bf_v, r.b_fc_g))
    for move, held, out in moves:
        move.wait()
        stores.append(local(held, out))
    for store in stores:
        store.wait()


def shaped(shape, dtype):
    return jax.ShapeDtypeStruct(tuple(shape), dtype)


def kernel_call(kernel, name, ins, outs, scratch, params):
    names = list(ins) + list(outs) + list(scratch)
    results = pl.pallas_call(
        functools.partial(kernel, names),
        out_shape=tuple(outs.values()),
        in_specs=[ANY] * len(ins),
        out_specs=(ANY,) * len(outs),
        scratch_shapes=list(scratch.values()),
        name=name,
        compiler_params=pltpu.CompilerParams(**params),
    )(*ins.values())
    return dict(zip(outs, results))


def per_device(
    x_in,
    seq_lengths,
    ln1_gain,
    ln1_bias,
    ln2_gain,
    ln2_bias,
    res_bias,
    w_qkv,
    b_qkv,
    w_out,
    w_fc,
    b_fc,
    w_proj,
    grad_out,
):
    n_tensor, n_dp = lax.axis_size("tensor"), lax.axis_size("dp")
    my_tensor, my_dp = lax.axis_index("tensor"), lax.axis_index("dp")
    bf16, f32 = jnp.bfloat16, jnp.float32
    my_rows, width = x_in.shape
    group_rows = my_rows * n_tensor
    total_rows = group_rows * n_dp
    layers = w_qkv.shape[0]
    part = w_qkv.shape[3]
    hidden = w_fc.shape[2]
    dp_width = width // n_dp
    vec = ln1_gain.shape[1]
    columns_ok = dp_width % 128 == 0
    vm = pltpu.VMEM
    pad8 = lambda n: -(-n // 8) * 8
    small_rows = pad8(4 * layers)
    vec_rows = pad8(5 * layers)
    n_remote, n_send, n_local = copy_counts(n_dp, n_tensor, layers)
    paired = n_dp == 8

    ins = dict(
        x_in=x_in,
        lens=seq_lengths,
        ln1_gain=ln1_gain,
        ln1_bias=ln1_bias,
        ln2_gain=ln2_gain,
        ln2_bias=ln2_bias,
        res_bias=res_bias,
        w_qkv=jnp.transpose(w_qkv, (0, 2, 1, 3)),
        b_qkv=jnp.transpose(b_qkv, (1, 0, 2)),
        w_out=w_out,
        w_fc=w_fc,
        b_fc=b_fc,
        w_proj=w_proj,
        grad_out=grad_out,
    )
    outs = dict(
        y_out=shaped(x_in.shape, f32),
        grad_x=shaped(x_in.shape, f32),
        total_out=shaped((vec_rows + small_rows, dp_width), f32),
    )
    gathered = dict(ctx_all=part, act_all=hidden, dqkv_all=3 * part, du_all=hidden)
    if paired:
        cross = (layers, 2, 4, n_tensor, my_rows, 2 * dp_width)
        outs |= dict(
            w_qkv_g=shaped(ins["w_qkv"].shape, f32),
            w_out_g=shaped(w_out.shape, f32),
            w_fc_g=shaped(w_fc.shape, f32),
            w_proj_g=shaped(w_proj.shape, f32),
        )
    else:
        cross = (layers, 2, n_dp, n_tensor, my_rows, dp_width)
        outs |= dict(vecs_out=shaped((vec_rows, width), f32), cross=shaped(cross, bf16))
        for name, size in gathered.items():
            outs[name] = shaped((layers, total_rows, size), bf16)
    rows_block = (layers, my_rows, width)
    group_block = (layers, group_rows, width)
    land = (layers, n_tensor - 1, my_rows, width)
    scratch = dict(
        resid=vm(rows_block, f32),
        dres=vm(rows_block, f32),
        lens_v=vm(seq_lengths.shape, jnp.int32),
        sv=vm((5,) + ln1_gain.shape, f32),
        sq=vm(ins["b_qkv"].shape, f32),
        sf=vm(b_fc.shape, f32),
        pack_v=vm((vec_rows, dp_width), f32),
        pack_b=vm((small_rows, 128), f32),
        land_v=vm((n_tensor - 1, vec_rows, dp_width), f32),
        vec_all=vm((n_dp, vec_rows, dp_width), f32),
        small_b=vm((n_dp, small_rows, 128), f32),
        vecs=vm((vec_rows, width), f32),
        bq=vm((pad8(3 * layers), part), f32),
        bf=vm((pad8(layers), hidden), f32),
        same=vm((group_rows, part), f32),
        up=vm((group_rows, part), f32),
        down=vm((group_rows, part), f32),
        mask=vm((group_rows, group_rows), f32),
        wq=vm((layers, 3, width, part), bf16),
        wf=vm((layers, width, hidden), bf16),
        wo=vm((layers, part, width), bf16),
        wp=vm((layers, hidden, width), bf16),
        unit=vm(group_block, bf16),
        drows=vm(group_block, bf16),
        qkv=vm((layers, group_rows, 3 * part), bf16),
        ctx=vm((layers, group_rows, part), bf16),
        pre=vm((layers, group_rows, hidden), f32),
        act=vm((layers, group_rows, hidden), bf16),
        dctx=vm((group_rows, part), bf16),
        du=vm((layers, group_rows, hidden), bf16),
        dqkv=vm((layers, group_rows, 3 * part), bf16),
        part_f=vm(group_block, bf16),
        part_e=vm(group_block, bf16),
        land_f=vm(land, bf16),
        land_e=vm(land, bf16),
        stage=vm(cross[:3] + cross[4:], bf16),
        sums=vm((vec_rows, width), f32),
        sums_q=vm((pad8(3 * layers), part), f32),
        sums_f=vm((pad8(layers), hidden), f32),
        sums_stage=vm((n_dp, vec_rows + small_rows, dp_width), f32),
        land_s=vm((n_dp - 1, vec_rows + small_rows, dp_width), f32),
        half=vm((vec_rows, dp_width), f32),
        land_t=vm((n_tensor - 1, vec_rows, dp_width), f32),
        total_v=vm((vec_rows + small_rows, dp_width), f32),
        y_v=vm((my_rows, width), f32),
        gx_v=vm((my_rows, width), f32),
        send_sems=pltpu.SemaphoreType.DMA((n_send,)),
        recv_sems=pltpu.SemaphoreType.DMA((n_remote,)),
        local_sems=pltpu.SemaphoreType.DMA((n_local,)),
    )
    if not columns_ok:
        scratch["wo_blocks"] = vm((layers, n_dp, part, dp_width), bf16)
        scratch["wp_blocks"] = vm((layers, n_dp, hidden, dp_width), bf16)
    if paired:
        scratch["cross"] = vm(cross, bf16)
        for name, size in gathered.items():
            scratch[name] = vm((layers, 4, group_rows, size), bf16)
        halves = dict(
            gq=ins["w_qkv"].shape,
            go=(layers, dp_width, part),
            gf=(layers, dp_width, hidden),
            gp=(layers, dp_width, hidden),
        )
        for name, shape in halves.items():
            scratch[name + "_own"] = vm(shape, f32)
            scratch[name + "_away"] = vm(shape, bf16)
            scratch[name + "_land"] = vm(shape, bf16)
        scratch |= dict(go_v=vm(w_out.shape, f32), gp_v=vm(w_proj.shape, f32))
    step = kernel_call(
        functools.partial(layers_kernel, n_dp, n_tensor),
        "layers",
        ins,
        outs,
        scratch,
        {"collective_id": 0, "has_side_effects": True, "vmem_limit_bytes": 58 << 20},
    )

    if paired:
        vectors = {f"g{k}": shaped(ln1_gain.shape, f32) for k in range(5)}
        done = kernel_call(
            places_kernel,
            "places",
            dict(
                y_in=step["y_out"],
                gx_in=step["grad_x"],
                total=step["total_out"],
                qkv_in=step["w_qkv_g"],
                out_in=step["w_out_g"],
                fc_in=step["w_fc_g"],
                proj_in=step["w_proj_g"],
            ),
            dict(
                y_out=shaped(x_in.shape, f32),
                grad_x=shaped(x_in.shape, f32),
                w_qkv_g=shaped(ins["w_qkv"].shape, f32),
                b_qkv_g=shaped(ins["b_qkv"].shape, f32),
                w_out_g=shaped(w_out.shape, f32),
                w_fc_g=shaped(w_fc.shape, f32),
                b_fc_g=shaped(b_fc.shape, f32),
                w_proj_g=shaped(w_proj.shape, f32),
                **vectors,
            ),
            dict(
                total_v=vm(step["total_out"].shape, f32),
                g_v=vm((5, layers, vec), f32),
                bq_v=vm(ins["b_qkv"].shape, f32),
                bf_v=vm(b_fc.shape, f32),
                qkv_v=vm(ins["w_qkv"].shape, f32),
                fc_v=vm(w_fc.shape, f32),
                proj_v=vm(w_proj.shape, f32),
                out_v=vm(w_out.shape, f32),
                y_v=vm(x_in.shape, f32),
                gx_v=vm(x_in.shape, f32),
                sems=pltpu.SemaphoreType.DMA((20,)),
            ),
            {"vmem_limit_bytes": 58 << 20},
        )
        return (
            (done["y_out"], done["grad_x"])
            + tuple(done[name] for name in vectors)
            + (
                jnp.transpose(done["w_qkv_g"], (0, 2, 1, 3)),
                jnp.transpose(done["b_qkv_g"], (1, 0, 2)),
            )
            + tuple(done[name] for name in ("w_out_g", "w_fc_g", "b_fc_g", "w_proj_g"))
        )

    over_tokens = (((0,), (0,)), ((), ()))
    grads = [[] for _ in range(6)]
    small = step["total_out"][vec_rows:]
    vectors = step["vecs_out"][: 5 * layers].reshape(5, layers, width)
    vectors = lax.dynamic_slice_in_dim(vectors, my_dp * dp_width, dp_width, axis=2)
    for layer in range(layers):
        context_t, act_t, dqkv_t, d_pre_t = (
            step[name][layer] for name in ("ctx_all", "act_all", "dqkv_all", "du_all")
        )
        unit_t = step["cross"][layer, 0].reshape(total_rows, dp_width).astype(f32)
        d_t = step["cross"][layer, 1].reshape(total_rows, dp_width)
        a_t = (unit_t * vectors[0, layer] + vectors[1, layer]).astype(bf16)
        m_t = (unit_t * vectors[2, layer] + vectors[3, layer]).astype(bf16)

        def contract(left, right):
            return lax.dot_general(left, right, over_tokens, preferred_element_type=f32)

        grads[0].append(contract(a_t, dqkv_t).reshape(w_qkv.shape[1:]))
        grads[1].append(small[layer : 3 * layers : layers, : b_qkv.shape[2]])
        grads[2].append(contract(context_t, d_t))
        grads[3].append(contract(m_t, d_pre_t))
        grads[4].append(small[3 * layers + layer, : b_fc.shape[1]])
        grads[5].append(contract(act_t, d_t))
    vector_grads = lax.dynamic_slice_in_dim(
        step["total_out"][: 5 * layers].reshape(layers, 5, dp_width), my_tensor * vec, vec, axis=2
    )
    return (
        (step["y_out"], step["grad_x"])
        + tuple(vector_grads[:, k] for k in range(5))
        + tuple(jnp.stack(group) for group in grads)
    )


def solution(mesh):
    in_specs = (
        P(("dp", "tensor"), None),
        P("dp", None),
        P(None, ("dp", "tensor")),
        P(None, ("dp", "tensor")),
        P(None, ("dp", "tensor")),
        P(None, ("dp", "tensor")),
        P(None, ("dp", "tensor")),
        P(None, "dp", None, "tensor"),
        P(None, None, ("tensor", "dp")),
        P(None, "tensor", "dp"),
        P(None, "dp", "tensor"),
        P(None, ("tensor", "dp")),
        P(None, "tensor", "dp"),
        P(("dp", "tensor"), None),
    )
    out_specs = (
        P(("dp", "tensor"), None),
        P(("dp", "tensor"), None),
        P(None, ("dp", "tensor")),
        P(None, ("dp", "tensor")),
        P(None, ("dp", "tensor")),
        P(None, ("dp", "tensor")),
        P(None, ("dp", "tensor")),
        P(None, "dp", None, "tensor"),
        P(None, None, ("tensor", "dp")),
        P(None, "tensor", "dp"),
        P(None, "dp", "tensor"),
        P(None, ("tensor", "dp")),
        P(None, "tensor", "dp"),
    )
    return jax.shard_map(
        per_device, mesh=mesh, in_specs=in_specs, out_specs=out_specs, check_vma=False
    )
```
